128 devices in a mesh: dp: 4 (over x), ctx: 8 (over y, core), head: 4 (over z).
Axes of the slice: x: 4, y: 4, z: 4, core: 2. Of those that a mesh axis runs over, the one named last changes fastest.
Arguments:
- x_rows: bfloat16 [16384, 8192], P(('dp', 'ctx', 'head')), may hold values from -6 to 6
- b_rows: bfloat16 [16384, 1024], P(('dp', 'ctx', 'head')), may hold values from -3 to 3
- c_rows: bfloat16 [16384, 1024], P(('dp', 'ctx', 'head')), may hold values from -3 to 3
- dt_rows: bfloat16 [16384, 128], P(('dp', 'ctx', 'head')), may hold values from -5 to 5
- length_plan: int32 [8192], replicated, may hold values from 0 to 8191, as said below
- trace_lengths: int32 [4, 6], P('dp'), may hold values from 1 to 2048, 4096 in all within a row
- x_taps: float32 [4, 8192], P(None, 'head'), may hold values from -3 to 3
- bc_taps: float32 [2, 4, 1024], P(None, None, 'head'), may hold values from -3 to 3
- x_bias: float32 [8192], P('head'), may hold values from -3 to 3
- bc_bias: float32 [2, 1024], P(None, 'head'), may hold values from -1.5 to 1.5
- dt_bias: float32 [128], P('head'), may hold values from -1.5 to 0.5
- decay_rate: float32 [128], P('head'), may hold values from 0.00012207031 to 0.05
- skip_gain: float32 [128], P('head'), may hold values from 0.25 to 4
- out_grad: bfloat16 [16384, 8192], P(('dp', 'ctx'), 'head'), may hold values from -6 to 6
Outputs:
- mixer_out: bfloat16 [16384, 8192], P(('dp', 'ctx'), 'head')
- x_rows_grad: bfloat16 [16384, 8192], P(('dp', 'ctx', 'head'))
- b_rows_grad: bfloat16 [16384, 1024], P(('dp', 'ctx', 'head'))
- c_rows_grad: bfloat16 [16384, 1024], P(('dp', 'ctx', 'head'))
- dt_rows_grad: bfloat16 [16384, 128], P(('dp', 'ctx', 'head'))
- x_taps_grad: float32 [4, 8192], P(None, 'head')
- bc_taps_grad: float32 [2, 4, 1024], P(None, None, 'head')
- x_bias_grad: float32 [8192], P('head')
- bc_bias_grad: float32 [2, 1024], P(None, 'head')
- dt_bias_grad: float32 [128], P('head')
- decay_rate_grad: float32 [128], P('head')
- skip_gain_grad: float32 [128], P('head')
The draws below stay inside these ranges and needn't reach their ends.
Inputs may be any that keep to these rules, and one draw needn't show every extreme that they name: A permutation: each loader block fills exactly one packed block. Packed block g belongs to owner g // 256; loader block b sits on loader device b // 64 of owner b // 256 and head index b // 64 % 4. The head index of length_plan[g] is g % 256 // 64. One loader device sends at most 4 blocks to one owner, and some loader device sends exactly 4 blocks to some owner.
All inputs are finite; a program needn't handle non-finite values.
Results may differ from the reference program's by a relative error of at most 0.015.
Values may be sent and summed in bfloat16 or wider, within the bound.
A program may use at most 128 MiB of HBM per device.

```python
import math
from functools import partial
import jax
import jax.numpy as jnp
import numpy as np
from jax import lax

HEADS = 128
HEAD_DIM = 64
GROUPS = 8
STATE = 128
KERNEL = 4
STRETCH = 256
BLK = 2
TRACES = 6
TOK_DEV = 512
D_INNER = 8192
STREAMS = 4
STREAM = 4096
OWNERS = 32
TOKENS = 16384
OWNER_BLOCKS = 256
LBLOCKS = 64
BLOCKS = 8192
N_CTX = 8


def column_plan(key):
    parts = jax.random.split(key, 5)
    owners = OWNERS
    width = LBLOCKS
    base = width // owners
    order = jax.random.permutation(parts[0], owners).astype(jnp.int32)
    where_at = jnp.zeros((owners,), jnp.int32).at[order].set(jnp.arange(owners, dtype=jnp.int32))
    shuffled = jax.random.permutation(parts[1], owners).astype(jnp.int32)
    half = owners // 2
    moves = jax.random.randint(parts[2], (half,), 0, base + 1).astype(jnp.int32)
    moves = moves.at[0].set(base)
    counts = jnp.full((owners,), base, jnp.int32).at[shuffled[:half]].add(moves).at[shuffled[half:2 * half]].add(-moves)
    ends = jnp.cumsum(counts).astype(jnp.int32)
    ranks = jnp.arange(width, dtype=jnp.int32)
    offset = jnp.sum((ranks[:, None] >= ends[None, :]).astype(jnp.int32), axis=1)
    targets = jnp.arange(owners, dtype=jnp.int32)
    senders = order[(where_at[targets][:, None] - offset[None, :]) % owners]
    send_perm = jax.vmap(lambda inner_key: jax.random.permutation(inner_key, width))(jax.random.split(parts[3], owners)).astype(jnp.int32)
    land_perm = jax.vmap(lambda inner_key: jax.random.permutation(inner_key, width))(jax.random.split(parts[4], owners)).astype(jnp.int32)
    sender_slot = send_perm[senders, ranks[None, :]]
    return (senders, sender_slot, land_perm)


def draw_length_plan(key, part):
    width = LBLOCKS
    columns = OWNER_BLOCKS // LBLOCKS
    senders, sender_slot, land_perm = jax.vmap(column_plan)(jax.random.split(jax.random.fold_in(key, 7), columns))
    column = jnp.arange(columns, dtype=jnp.int32)[:, None, None]
    targets = jnp.arange(OWNERS, dtype=jnp.int32)[None, :, None]
    values = (senders * columns + column) * width + sender_slot
    places = targets * OWNER_BLOCKS + column * width + land_perm
    return jnp.zeros((BLOCKS,), jnp.int32).at[places.reshape(-1)].set(values.reshape(-1).astype(jnp.int32))


def draw_skip_gain(key, part):
    subkeys = jax.random.split(jax.random.fold_in(key, 13), 2)
    return jax.random.uniform(subkeys[1], (HEADS,), jnp.float32, 0.25, 4.0).astype(jnp.float32)


def block_scale(own_key, dims, cuts, low, high):
    loudness = 1.0
    for dim, blocks in cuts:
        heights = jax.random.uniform(jax.random.fold_in(jax.random.fold_in(own_key, 6), dim), (blocks,), jnp.float32, low / len(cuts), high / len(cuts))
        loudness = loudness * jnp.repeat(jnp.exp(heights), dims[dim] // blocks).reshape((-1,) + (1,) * (len(dims) - 1 - dim))
    return loudness


def length_profile(amount, total, bound, slope):
    loads = [(1 << 20) // math.isqrt(rank ** slope) + 1 for rank in range(2, amount + 1)]
    spare, given = total - bound - (amount - 1), [1] * (amount - 1)
    while spare > 0:
        movable = [i for i in range(amount - 1) if given[i] < bound]
        whole, remaining = sum([loads[i] for i in movable]), spare
        for i in movable:
            more = min(bound - given[i], max(1, remaining * loads[i] // whole), spare)
            given[i] = given[i] + more
            spare = spare - more
    return np.array([bound] + given)


def ragged(stream_key, count, total, reach, lean):
    if count == 2:
        one = jax.random.randint(stream_key, (), max(1, total - reach), min(reach, total - 1) + 1)
        return jnp.stack([one, total - one])
    tallies = jnp.asarray(length_profile(count, total, reach, lean), jnp.int32)
    couples = (count - 1) // 2
    source_of, sink = tallies[1:1 + 2 * couples:2], tallies[2:2 + 2 * couples:2]
    slack = jnp.minimum(source_of - 1, reach - sink)
    moved = jax.random.randint(jax.random.fold_in(stream_key, 1), (couples,), 0, 1 << 20) % (slack + 1)
    tallies = tallies.at[1:1 + 2 * couples:2].set(source_of - moved).at[2:2 + 2 * couples:2].set(sink + moved)
    return tallies[jax.random.permutation(jax.random.fold_in(stream_key, 2), count)]


def normal_values(stream_key, shape, spread, limit, cuts=(), kind=jnp.bfloat16):
    drawn = spread * jax.random.normal(stream_key, shape, jnp.float32)
    if cuts:
        drawn = drawn * block_scale(stream_key, shape, cuts, -0.22, 0.18)
    return jnp.clip(drawn, -limit, limit).astype(kind)


def setup_inputs(seed: int = 0) -> dict:
    key_list = jax.random.split(jax.random.key(seed), 15)
    return {
        "x_rows": normal_values(key_list[0], (TOKENS, D_INNER), 1.0, 6.0, ((0, 128),)),
        "b_rows": normal_values(key_list[1], (TOKENS, GROUPS * STATE), 0.5, 3.0, ((0, 128),)),
        "c_rows": normal_values(key_list[2], (TOKENS, GROUPS * STATE), 0.5, 3.0, ((0, 128),)),
        "dt_rows": normal_values(key_list[3], (TOKENS, HEADS), 1.0, 5.0, ((0, 128),)),
        "length_plan": draw_length_plan(jax.random.fold_in(key_list[14], 71), 0),
        "trace_lengths": jax.vmap(lambda own: ragged(own, TRACES, STREAM, STREAM // 2, 2))(jax.random.split(key_list[5], STREAMS)).reshape((STREAMS, TRACES)).astype(jnp.int32),
        "x_taps": normal_values(key_list[6], (KERNEL, D_INNER), KERNEL ** -0.5, 3.0, ((1, 4),), jnp.float32),
        "bc_taps": normal_values(key_list[7], (2, KERNEL, GROUPS * STATE), KERNEL ** -0.5, 3.0, ((2, 4),), jnp.float32),
        "x_bias": normal_values(key_list[8], (D_INNER,), 0.5, 3.0, ((0, 4),), jnp.float32),
        "bc_bias": normal_values(key_list[9], (2, GROUPS * STATE), 0.25, 1.5, ((1, 4),), jnp.float32),
        "dt_bias": jnp.clip(-1.5 + 2.0 * jax.random.uniform(key_list[10], (HEADS,), jnp.float32) ** block_scale(key_list[10], (HEADS,), ((0, 4),), -0.2, 0.2), -1.5, 0.5),
        "decay_rate": jnp.clip(jnp.exp(math.log(0.05) - 6.015181 * jax.random.uniform(key_list[11], (HEADS,), jnp.float32) ** block_scale(key_list[11], (HEADS,), ((0, 4),), -0.2, 0.2)), 0.00012207031, 0.05),
        "skip_gain": draw_skip_gain(jax.random.fold_in(key_list[14], 71), 0),
        "out_grad": normal_values(key_list[13], (TOKENS, D_INNER), 1.0, 6.0, ((0, 32), (1, 4))),
    }


head_batch = 4

def segment_of(ends, positions):
    return lax.optimization_barrier(jnp.sum((positions[:, None] >= ends[None, :]).astype(jnp.int32), axis=1)).astype(jnp.int32)

def mask_parts(lengths_row, start, count):
    ends = jnp.cumsum(lengths_row).astype(jnp.int32)
    positions = (start + jnp.arange(count, dtype=jnp.int32)).astype(jnp.int32)
    labels = segment_of(ends, positions)
    behind = positions[:, None] - (KERNEL - 1) + jnp.arange(KERNEL, dtype=jnp.int32)[None, :]
    behind_labels = segment_of(ends, behind.reshape(-1)).reshape(count, KERNEL)
    conv_keep = ((behind >= 0) & (behind_labels == labels[:, None])).astype(jnp.float32)
    earlier = segment_of(ends, jnp.reshape(start - 1, (1,)).astype(jnp.int32))[0]
    before = jnp.where(start > 0, earlier, -1).astype(jnp.int32)
    stretches = count // STRETCH
    grid = labels.reshape(stretches, STRETCH)
    prior = jnp.concatenate([jnp.reshape(before, (1,)), grid[:-1, -1]]).astype(jnp.int32)
    lower = jnp.arange(STRETCH, dtype=jnp.int32)[:, None] >= jnp.arange(STRETCH, dtype=jnp.int32)[None, :]
    same = (grid[:, :, None] == grid[:, None, :]) & lower[None]
    last_keep = (grid == grid[:, -1:]).astype(jnp.float32)
    first_keep = (grid == prior[:, None]).astype(jnp.float32)
    carry_keep = (grid[:, -1] == prior).astype(jnp.float32)
    return (conv_keep, same, last_keep, first_keep, carry_keep)

def convolve(padded, weight, bias, keep):
    count = keep.shape[0]
    total = jnp.broadcast_to(bias, (count, bias.shape[0]))
    for tap_at in range(KERNEL):
        total = total + weight[tap_at] * padded[tap_at:tap_at + count] * keep[:, tap_at:tap_at + 1]
    return jax.nn.silu(total).astype(jnp.bfloat16)

def contract(form, left, right):
    return jnp.einsum(form, left.astype(jnp.float32), right.astype(jnp.float32), precision=lax.Precision.HIGHEST)

def decay_parts(dt_raw, shift_part, rate_part):
    step_size = jax.nn.softplus(dt_raw.astype(jnp.float32) + shift_part)
    count = step_size.shape[0]
    folded = step_size.reshape(count // STRETCH, STRETCH, -1)
    log_decay = jnp.cumsum(-rate_part * folded, axis=1)
    return (folded, log_decay)

def stretch_states(inner_f, b_low, step_size, log_decay, last_keep, carry_keep):
    to_end = jnp.exp(log_decay[:, -1:, :] - log_decay) * last_keep[:, :, None]
    weighted = ((step_size * to_end)[:, :, :, None] * inner_f).astype(jnp.bfloat16)
    e_stretch = contract('kqhp,kqn->khpn', weighted, b_low)
    g_stretch = jnp.exp(log_decay[:, -1, :]) * carry_keep[:, None]
    return (e_stretch, g_stretch)

def ssd_local(x_part, b_full, c_full, dt_raw, shift_part, rate_part, skip_part, same, last_keep, first_keep, carry_keep, h_in):
    count = x_part.shape[0]
    stretches = count // STRETCH
    width = h_in.shape[0]
    step_size, log_decay = decay_parts(dt_raw, shift_part, rate_part)
    inner_f = x_part.astype(jnp.float32).reshape(stretches, STRETCH, width, HEAD_DIM)
    b_low = b_full.astype(jnp.bfloat16).reshape(stretches, STRETCH, STATE)
    c_low = c_full.astype(jnp.bfloat16).reshape(stretches, STRETCH, STATE)
    x_step = (step_size[:, :, :, None] * inner_f).astype(jnp.bfloat16)
    intersections = contract('kqn,ksn->kqs', c_low, b_low)
    decay_h = jnp.swapaxes(log_decay, 1, 2)
    gaps = jnp.where(same[:, None], decay_h[:, :, :, None] - decay_h[:, :, None, :], -jnp.inf)
    mixing = (intersections[:, None] * jnp.exp(gaps)).astype(jnp.bfloat16)
    inner = contract('khqs,kshp->kqhp', mixing, x_step)
    e_stretch, g_stretch = stretch_states(inner_f, b_low, step_size, log_decay, last_keep, carry_keep)
    state = h_in
    entering = []
    for stretch_at in range(stretches):
        entering.append(state)
        state = g_stretch[stretch_at][:, None, None] * state + e_stretch[stretch_at]
    entering = jnp.stack(entering)
    gains = jnp.exp(log_decay) * first_keep[:, :, None]
    carried = jnp.einsum('kqn,khpn->kqhp', c_full.reshape(stretches, STRETCH, STATE), entering, precision=lax.Precision.HIGHEST)
    total = inner + carried * gains[:, :, :, None] + skip_part[:, None] * inner_f
    return (total.astype(jnp.bfloat16).reshape(count, width * HEAD_DIM), state)

def reference(x_rows, b_rows, c_rows, dt_rows, length_plan, trace_lengths, x_taps, bc_taps, x_bias, bc_bias, dt_bias, decay_rate, skip_gain, out_grad):
    per_group = HEADS // GROUPS // head_batch
    batches = HEADS // head_batch

    def pack(rows):
        width = rows.shape[1]
        blocks = rows.reshape(BLOCKS, BLK, width)[length_plan]
        return blocks.reshape(STREAMS, N_CTX, TOK_DEV, width)

    def forward(x_rows, b_rows, c_rows, dt_rows, x_taps, bc_taps, x_bias, bc_bias, dt_bias, decay_rate, skip_gain):

        def stretch_step(lengths_row, carry, inputs):
            rim_x, rim_b, rim_c, state = carry
            x_blk, b_blk, c_blk, dt_blk, stretch_at = inputs
            count = x_blk.shape[0]
            conv_keep, same, last_keep, first_keep, carry_keep = mask_parts(lengths_row, stretch_at * count, count)
            x_wide = x_blk.astype(jnp.float32)
            b_wide = b_blk.astype(jnp.float32)
            c_wide = c_blk.astype(jnp.float32)
            x_conv = convolve(jnp.concatenate([rim_x, x_wide]), x_taps, x_bias, conv_keep)
            b_conv = convolve(jnp.concatenate([rim_b, b_wide]), bc_taps[0], bc_bias[0], conv_keep).astype(jnp.float32)
            c_conv = convolve(jnp.concatenate([rim_c, c_wide]), bc_taps[1], bc_bias[1], conv_keep).astype(jnp.float32)

            def one_batch(batch_at):
                group = batch_at // per_group
                x_part = lax.dynamic_slice_in_dim(x_conv, batch_at * head_batch * HEAD_DIM, head_batch * HEAD_DIM, 1)
                b_full = lax.dynamic_slice_in_dim(b_conv, group * STATE, STATE, 1)
                c_full = lax.dynamic_slice_in_dim(c_conv, group * STATE, STATE, 1)
                dt_raw = lax.dynamic_slice_in_dim(dt_blk, batch_at * head_batch, head_batch, 1)
                shift_part = lax.dynamic_slice_in_dim(dt_bias, batch_at * head_batch, head_batch)
                rate_part = lax.dynamic_slice_in_dim(decay_rate, batch_at * head_batch, head_batch)
                skip_part = lax.dynamic_slice_in_dim(skip_gain, batch_at * head_batch, head_batch)
                h_in = lax.dynamic_slice_in_dim(state, batch_at * head_batch, head_batch, 0)
                return ssd_local(x_part, b_full, c_full, dt_raw, shift_part, rate_part, skip_part, same, last_keep, first_keep, carry_keep, h_in)
            outs, states = lax.map(jax.checkpoint(one_batch), jnp.arange(batches, dtype=jnp.int32))
            mixed = jnp.swapaxes(outs, 0, 1).reshape(count, D_INNER)
            tail = KERNEL - 1
            return ((x_wide[-tail:], b_wide[-tail:], c_wide[-tail:], states.reshape(HEADS, HEAD_DIM, STATE)), mixed)

        def one_stream(items):
            x_s, b_s, c_s, dt_s, lengths_row = items
            tail = KERNEL - 1
            start = (jnp.zeros((tail, D_INNER), jnp.float32), jnp.zeros((tail, GROUPS * STATE), jnp.float32), jnp.zeros((tail, GROUPS * STATE), jnp.float32), jnp.zeros((HEADS, HEAD_DIM, STATE), jnp.float32))
            stepper = jax.checkpoint(partial(stretch_step, lengths_row))
            _, mixed = lax.scan(stepper, start, (x_s, b_s, c_s, dt_s, jnp.arange(N_CTX, dtype=jnp.int32)))
            return mixed
        outs = lax.map(one_stream, (pack(x_rows), pack(b_rows), pack(c_rows), pack(dt_rows), trace_lengths))
        return outs.reshape(TOKENS, D_INNER)
    mixer_out, pull = jax.vjp(forward, x_rows, b_rows, c_rows, dt_rows, x_taps, bc_taps, x_bias, bc_bias, dt_bias, decay_rate, skip_gain)
    grads = pull(out_grad)
    return (mixer_out, grads[0], grads[1], grads[2], grads[3], grads[4], grads[5], grads[6], grads[7], grads[8], grads[9], grads[10])
```

```python
import functools

import jax
import jax.numpy as jnp
from jax import lax
from jax.experimental import pallas as pl
from jax.experimental.pallas import tpu as pltpu
from jax.sharding import PartitionSpec as P

HEADS = 128
HEAD_DIM = 64
GROUPS = 8
STATE = 128
KERNEL = 4
STRETCH = 256
BLK = 2
LANES = 128
OWNERS = 32
WAYS = 4
LBLOCKS = 64
DEPTH = 4
ROWS = 512
XCOLS = 2048
BCOLS = 256
COLS = XCOLS + 2 * BCOLS + LANES
PAIRS = 16
GROUP_PAIRS = 8
EXTRA = 16
NEG = -1e30

F32 = jnp.float32
BF16 = jnp.bfloat16
ROUTE = ("head", "dp", "ctx")


def dot(left, right):
    return lax.dot_general(left, right, (((1,), (0,)), ((), ())), preferred_element_type=F32)


def dot_nt(left, right):
    return lax.dot_general(left, right, (((1,), (1,)), ((), ())), preferred_element_type=F32)


def iota(shape, dim):
    return lax.broadcasted_iota(jnp.int32, shape, dim)


def one_hot(condition):
    return jnp.where(condition, 1.0, 0.0).astype(BF16)


def eye(size):
    return one_hot(iota((size, size), 0) == iota((size, size), 1))


def send_kernel(d_ref, x_ref, b_ref, c_ref, dt_ref, out_ref):
    way = pl.program_id(0)
    rows = x_ref.shape[0]
    spread = one_hot(iota((OWNERS * DEPTH * BLK, rows), 0) == d_ref[...])
    out_ref[0, :, :XCOLS] = dot(spread, x_ref[...]).astype(BF16)
    out_ref[0, :, XCOLS : XCOLS + BCOLS] = dot(spread, b_ref[...]).astype(BF16)
    out_ref[0, :, XCOLS + BCOLS : XCOLS + 2 * BCOLS] = dot(spread, c_ref[...]).astype(BF16)
    width = HEADS // WAYS
    lane = iota((LANES, LANES), 1)
    pick = one_hot((iota((LANES, LANES), 0) == way * width + lane) & (lane < width))
    dt_part = dot(dt_ref[...], pick).astype(BF16)
    out_ref[0, :, XCOLS + 2 * BCOLS :] = dot(spread, dt_part).astype(BF16)


def send_rows(d_row, x_rows, b_rows, c_rows, dt_rows):
    rows = x_rows.shape[0]
    slots = OWNERS * DEPTH * BLK
    return pl.pallas_call(
        send_kernel,
        grid=(WAYS,),
        in_specs=[
            pl.BlockSpec((1, rows), lambda h: (0, 0)),
            pl.BlockSpec((rows, XCOLS), lambda h: (0, h)),
            pl.BlockSpec((rows, BCOLS), lambda h: (0, h)),
            pl.BlockSpec((rows, BCOLS), lambda h: (0, h)),
            pl.BlockSpec((rows, HEADS), lambda h: (0, 0)),
        ],
        out_specs=pl.BlockSpec((1, slots, COLS), lambda h: (h, 0, 0)),
        out_shape=jax.ShapeDtypeStruct((WAYS, slots, COLS), BF16),
        name="send_rows",
    )(d_row, x_rows, b_rows, c_rows, dt_rows)


def pack_kernel(q_ref, in_ref, out_ref):
    rows = out_ref.shape[0]
    slots = in_ref.shape[1]
    pick = one_hot(iota((rows, slots), 1) == q_ref[0])
    out_ref[...] = dot(pick, in_ref[0]).astype(BF16)


def pack_rows(q_col, landed):
    slots = landed.shape[1]
    rows = ROWS // WAYS
    return pl.pallas_call(
        pack_kernel,
        grid=(WAYS,),
        in_specs=[
            pl.BlockSpec((1, rows, 1), lambda j: (j, 0, 0)),
            pl.BlockSpec((1, slots, COLS), lambda j: (j, 0, 0)),
        ],
        out_specs=pl.BlockSpec((rows, COLS), lambda j: (j, 0)),
        out_shape=jax.ShapeDtypeStruct((ROWS, COLS), BF16),
        name="pack_rows",
    )(q_col, landed)


def unpack_kernel(q_ref, x_ref, b_ref, c_ref, dt_ref, tx_ref, tb_ref, tc_ref, back_ref, out_ref):
    j = pl.program_id(0)
    rows = x_ref.shape[0]
    slots = out_ref.shape[1]
    spread = one_hot(iota((slots, rows), 0) == q_ref[0])
    last = j == WAYS - 1

    def one(ref, tail_ref, low, high):
        whole = ref[...].astype(F32)
        tail = tail_ref[...] + back_ref[:, low:high]
        fixed = jnp.concatenate([whole[: rows - 8], jnp.where(last, tail, whole[rows - 8 :])])
        out_ref[0, :, low:high] = dot(spread, fixed.astype(BF16)).astype(BF16)

    one(x_ref, tx_ref, 0, XCOLS)
    one(b_ref, tb_ref, XCOLS, XCOLS + BCOLS)
    one(c_ref, tc_ref, XCOLS + BCOLS, XCOLS + 2 * BCOLS)
    out_ref[0, :, XCOLS + 2 * BCOLS :] = dot(spread, dt_ref[...]).astype(BF16)


def unpack_rows(q_row, dx, db, dc, ddt, tx, tb, tc, back):
    slots = OWNERS * DEPTH * BLK
    rows = ROWS // WAYS
    full = lambda j: (0, 0)
    return pl.pallas_call(
        unpack_kernel,
        grid=(WAYS,),
        in_specs=[
            pl.BlockSpec((1, 1, rows), lambda j: (j, 0, 0)),
            pl.BlockSpec((rows, XCOLS), lambda j: (j, 0)),
            pl.BlockSpec((rows, BCOLS), lambda j: (j, 0)),
            pl.BlockSpec((rows, BCOLS), lambda j: (j, 0)),
            pl.BlockSpec((rows, LANES), lambda j: (j, 0)),
            pl.BlockSpec((8, XCOLS), full),
            pl.BlockSpec((8, BCOLS), full),
            pl.BlockSpec((8, BCOLS), full),
            pl.BlockSpec((8, XCOLS + 2 * BCOLS), full),
        ],
        out_specs=pl.BlockSpec((1, slots, COLS), lambda j: (j, 0, 0)),
        out_shape=jax.ShapeDtypeStruct((WAYS, slots, COLS), BF16),
        name="unpack_rows",
    )(q_row, dx, db, dc, ddt, tx, tb, tc, back)


def home_kernel(d_ref, in_ref, x_ref, b_ref, c_ref, dt_ref, acc_ref):
    way = pl.program_id(0)
    rows = x_ref.shape[0]
    slots = in_ref.shape[1]
    pick = one_hot(iota((rows, slots), 1) == d_ref[...])
    x_ref[...] = dot(pick, in_ref[0, :, :XCOLS]).astype(BF16)
    b_ref[...] = dot(pick, in_ref[0, :, XCOLS : XCOLS + BCOLS]).astype(BF16)
    c_ref[...] = dot(pick, in_ref[0, :, XCOLS + BCOLS : XCOLS + 2 * BCOLS]).astype(BF16)
    width = HEADS // WAYS
    lane = iota((LANES, LANES), 0)
    put = one_hot((iota((LANES, LANES), 1) == way * width + lane) & (lane < width))
    dt_part = dot(pick, in_ref[0, :, XCOLS + 2 * BCOLS :]).astype(BF16)

    @pl.when(way == 0)
    def _():
        acc_ref[...] = jnp.zeros_like(acc_ref)

    acc_ref[...] += dot(dt_part, put)
    dt_ref[...] = acc_ref[...].astype(BF16)


def home_rows(d_col, landed):
    slots = landed.shape[1]
    rows = d_col.shape[0]
    return pl.pallas_call(
        home_kernel,
        grid=(WAYS,),
        in_specs=[
            pl.BlockSpec((rows, 1), lambda h: (0, 0)),
            pl.BlockSpec((1, slots, COLS), lambda h: (h, 0, 0)),
        ],
        out_specs=[
            pl.BlockSpec((rows, XCOLS), lambda h: (0, h)),
            pl.BlockSpec((rows, BCOLS), lambda h: (0, h)),
            pl.BlockSpec((rows, BCOLS), lambda h: (0, h)),
            pl.BlockSpec((rows, HEADS), lambda h: (0, 0)),
        ],
        out_shape=[
            jax.ShapeDtypeStruct((rows, WAYS * XCOLS), BF16),
            jax.ShapeDtypeStruct((rows, WAYS * BCOLS), BF16),
            jax.ShapeDtypeStruct((rows, WAYS * BCOLS), BF16),
            jax.ShapeDtypeStruct((rows, HEADS), BF16),
        ],
        scratch_shapes=[pltpu.VMEM((rows, HEADS), F32)],
        name="home_rows",
    )(d_col, landed)


def fill_pad(pad_ref, rows_ref, halo_ref):
    pad_ref[0:8, :] = halo_ref[...].astype(F32)
    pad_ref[8 : 8 + ROWS, :] = rows_ref[...].astype(F32)


def conv_sum(pad_ref, taps, bias, keep_ref):
    total = bias + taps[0:1] * pad_ref[5 : 5 + ROWS, :] * keep_ref[0]
    total = total + taps[1:2] * pad_ref[6 : 6 + ROWS, :] * keep_ref[1]
    total = total + taps[2:3] * pad_ref[7 : 7 + ROWS, :] * keep_ref[2]
    return total + taps[3:4] * pad_ref[8 : 8 + ROWS, :]


def conv_value(pad_ref, rows_ref, halo_ref, taps, bias, keep_ref):
    fill_pad(pad_ref, rows_ref, halo_ref)
    total = conv_sum(pad_ref, taps, bias, keep_ref)
    return (total * jax.nn.sigmoid(total)).astype(BF16)


def conv_back(pad_ref, dpad_ref, rows_ref, halo_ref, taps, bias, keep_ref, keeps_ref, grad):
    fill_pad(pad_ref, rows_ref, halo_ref)
    total = conv_sum(pad_ref, taps, bias, keep_ref)
    sig = jax.nn.sigmoid(total)
    dpre = grad * (sig * (1.0 + total * (1.0 - sig)))
    dpad_ref[8 : 8 + ROWS, :] = dpre
    sums = []
    for k in range(KERNEL):
        value = dpre * pad_ref[5 + k : 5 + k + ROWS, :]
        if k < KERNEL - 1:
            value = value * keep_ref[k]
        sums.append(jnp.sum(value, axis=0, keepdims=True))
    sums.append(jnp.sum(dpre, axis=0, keepdims=True))
    sums.append(jnp.zeros((3, LANES), F32))
    span = ROWS + 8
    moved = taps[3:4] * dpad_ref[0:span, :]
    for k in range(KERNEL - 1):
        moved = moved + taps[k : k + 1] * (keeps_ref[k] * dpad_ref[3 - k : 3 - k + span, :])
    return moved, jnp.concatenate(sums)


def pair_rows(first, second, count=HEAD_DIM):
    width = first.shape[1]
    return jnp.concatenate(
        [jnp.broadcast_to(first, (count, width)), jnp.broadcast_to(second, (count, width))]
    )


def pair_scale(first, second, shape):
    return jnp.where(iota(shape, 0) < HEAD_DIM, first, second)


def first_kernel(
    gs_ref,
    rows_ref,
    x_ref,
    b_ref,
    c_ref,
    hx_ref,
    hb_ref,
    hc_ref,
    xt_ref,
    xb_ref,
    bt_ref,
    bb_ref,
    ct_ref,
    cb_ref,
    keep_ref,
    og_ref,
    ep_ref,
    xT_ref,
    gT_ref,
    bn_ref,
    cn_ref,
    e0_ref,
    t1_ref,
    pad_ref,
):
    i = pl.program_id(0)

    @pl.when(i % GROUP_PAIRS == 0)
    def _():
        bn_ref[...] = conv_value(pad_ref, b_ref, hb_ref, bt_ref[0], bb_ref[0], keep_ref)
        cn_ref[...] = conv_value(pad_ref, c_ref, hc_ref, ct_ref[0], cb_ref[0], keep_ref)

    unit = eye(LANES)
    xc = conv_value(pad_ref, x_ref, hx_ref, xt_ref[...], xb_ref[...], keep_ref)
    x_all = dot_nt(unit, xc)
    g_all = dot_nt(unit, og_ref[...])
    xT_ref[...] = x_all.astype(BF16)
    gT_ref[...] = g_all.astype(BF16)
    rows = rows_ref[0]
    states = []
    touched = []
    for k in range(2):
        span = slice(k * STRETCH, (k + 1) * STRETCH)
        coef = pair_rows(rows[0:1, span] * rows[4:5, span], rows[1:2, span] * rows[5:6, span])
        gain = pair_rows(rows[6:7, span], rows[7:8, span])
        states.append(dot((coef * x_all[:, span]).astype(BF16), bn_ref[span, :]))
        touched.append(dot((gain * g_all[:, span]).astype(BF16), cn_ref[span, :]))
    shape = (LANES, STATE)
    ga0, ga1 = gs_ref[4 * i], gs_ref[4 * i + 1]
    gb0, gb1 = gs_ref[4 * i + 2], gs_ref[4 * i + 3]
    ep_ref[0, 0:LANES, :] = (pair_scale(ga1, gb1, shape) * states[0] + states[1]).astype(BF16)
    ep_ref[0, LANES : 2 * LANES, :] = (
        touched[0] + pair_scale(ga0, gb0, shape) * touched[1]
    ).astype(BF16)
    lane = iota((EXTRA, LANES), 1)
    whole = jnp.where(lane < HEAD_DIM, ga0 * ga1, gb0 * gb1)
    high = whole.astype(BF16).astype(F32)
    low = whole - high
    ep_ref[0, 2 * LANES :, :] = jnp.where(iota((EXTRA, LANES), 0) < 8, high, low).astype(BF16)
    e0_ref[...] = states[0]
    t1_ref[...] = touched[1]


def conv_specs():
    group = lambda i: i // GROUP_PAIRS
    base_b = XCOLS // LANES
    base_c = base_b + BCOLS // LANES
    return [
        pl.BlockSpec((ROWS, LANES), lambda i: (0, i)),
        pl.BlockSpec((ROWS, LANES), lambda i: (0, base_b + group(i))),
        pl.BlockSpec((ROWS, LANES), lambda i: (0, base_c + group(i))),
        pl.BlockSpec((8, LANES), lambda i: (0, i)),
        pl.BlockSpec((8, LANES), lambda i: (0, base_b + group(i))),
        pl.BlockSpec((8, LANES), lambda i: (0, base_c + group(i))),
        pl.BlockSpec((KERNEL, LANES), lambda i: (0, i)),
        pl.BlockSpec((1, LANES), lambda i: (0, i)),
        pl.BlockSpec((1, KERNEL, LANES), lambda i: (0, 0, group(i))),
        pl.BlockSpec((1, 1, LANES), lambda i: (0, 0, group(i))),
        pl.BlockSpec((1, KERNEL, LANES), lambda i: (1, 0, group(i))),
        pl.BlockSpec((1, 1, LANES), lambda i: (1, 0, group(i))),
        pl.BlockSpec((KERNEL - 1, ROWS, LANES), lambda i: (0, 0, 0)),
    ]


def first_pass(gs, rows, conv_args, out_grad):
    wide = lambda i: (i, 0)
    group = lambda i: (0, i // GROUP_PAIRS)
    return pl.pallas_call(
        first_kernel,
        grid=(PAIRS,),
        in_specs=[
            pl.BlockSpec(memory_space=pltpu.SMEM),
            pl.BlockSpec((1, 8, ROWS), lambda i: (i, 0, 0)),
        ]
        + conv_specs()
        + [pl.BlockSpec((ROWS, LANES), lambda i: (0, i))],
        out_specs=[
            pl.BlockSpec((1, 2 * LANES + EXTRA, STATE), lambda i: (i, 0, 0)),
            pl.BlockSpec((LANES, ROWS), wide),
            pl.BlockSpec((LANES, ROWS), wide),
            pl.BlockSpec((ROWS, LANES), group),
            pl.BlockSpec((ROWS, LANES), group),
            pl.BlockSpec((LANES, STATE), wide),
            pl.BlockSpec((LANES, STATE), wide),
        ],
        out_shape=[
            jax.ShapeDtypeStruct((PAIRS, 2 * LANES + EXTRA, STATE), BF16),
            jax.ShapeDtypeStruct((XCOLS, ROWS), BF16),
            jax.ShapeDtypeStruct((XCOLS, ROWS), BF16),
            jax.ShapeDtypeStruct((ROWS, BCOLS), BF16),
            jax.ShapeDtypeStruct((ROWS, BCOLS), BF16),
            jax.ShapeDtypeStruct((XCOLS, STATE), F32),
            jax.ShapeDtypeStruct((XCOLS, STATE), F32),
        ],
        scratch_shapes=[pltpu.VMEM((ROWS + 16, LANES), F32)],
        name="first_pass",
    )(gs, rows, *conv_args, out_grad)


def scan_kernel(in_ref, out_ref):
    count = in_ref.shape[0]
    shape = (LANES, STATE)
    gains = []
    for at in range(count):
        extra = in_ref[at, 0, 2 * LANES :, :].astype(F32)
        gain = extra[0:1] + extra[8:9]
        gains.append(pair_scale(gain[:, 0:1], gain[:, HEAD_DIM : HEAD_DIM + 1], shape))
    state = jnp.zeros(shape, F32)
    for at in range(count):
        out_ref[at, 0, 0:LANES, :] = state.astype(BF16)
        state = gains[at] * state + in_ref[at, 0, 0:LANES, :].astype(F32)
    state = jnp.zeros(shape, F32)
    for at in reversed(range(count)):
        out_ref[at, 0, LANES : 2 * LANES, :] = state.astype(BF16)
        state = in_ref[at, 0, LANES : 2 * LANES, :].astype(F32) + gains[at] * state


def scan_states(landed):
    count, pairs = landed.shape[:2]
    return pl.pallas_call(
        scan_kernel,
        grid=(pairs,),
        in_specs=[pl.BlockSpec((count, 1, 2 * LANES + EXTRA, STATE), lambda i: (0, i, 0, 0))],
        out_specs=pl.BlockSpec((count, 1, 2 * LANES, STATE), lambda i: (0, i, 0, 0)),
        out_shape=jax.ShapeDtypeStruct((count, pairs, 2 * LANES, STATE), BF16),
        name="scan_states",
    )(landed)


def main_kernel(
    gs_ref,
    skip_ref,
    rows_ref,
    x_ref,
    b_ref,
    c_ref,
    hx_ref,
    hb_ref,
    hc_ref,
    xt_ref,
    xb_ref,
    bt_ref,
    bb_ref,
    ct_ref,
    cb_ref,
    keep_ref,
    keeps_ref,
    og_ref,
    xT_ref,
    gT_ref,
    bn_ref,
    cn_ref,
    ent_ref,
    e0_ref,
    t1_ref,
    labr_ref,
    labc_ref,
    y_ref,
    dx_ref,
    db_ref,
    dc_ref,
    tx_ref,
    tb_ref,
    tc_ref,
    px_ref,
    pb_ref,
    pc_ref,
    rout_ref,
    sx_ref,
    sb_ref,
    sc_ref,
    mask_ref,
    score_ref,
    dscore_ref,
    bT_ref,
    cT_ref,
    dbT_ref,
    dcT_ref,
    pad_ref,
    dpad_ref,
    dxn_ref,
):
    i = pl.program_id(0)
    unit = eye(LANES)
    wide_unit = eye(STRETCH)
    spans = [slice(k * STRETCH, (k + 1) * STRETCH) for k in range(2)]

    @pl.when(i == 0)
    def _():
        dpad_ref[...] = jnp.zeros_like(dpad_ref)
        for k in range(2):
            for t in range(2):
                shape = (STRETCH, LANES)
                left = k * STRETCH + t * LANES
                same = labc_ref[spans[k], :] == labr_ref[0:1, left : left + LANES]
                lower = iota(shape, 0) >= iota(shape, 1) + t * LANES
                mask_ref[k, :, t * LANES : (t + 1) * LANES] = jnp.where(same & lower, 0.0, NEG)

    @pl.when(i % GROUP_PAIRS == 0)
    def _():
        bT_ref[...] = dot_nt(unit, bn_ref[...]).astype(BF16)
        cT_ref[...] = dot_nt(unit, cn_ref[...]).astype(BF16)
        dbT_ref[...] = jnp.zeros_like(dbT_ref)
        dcT_ref[...] = jnp.zeros_like(dcT_ref)
        dscore_ref[...] = jnp.zeros_like(dscore_ref)
        for k in range(2):
            score_ref[k] = dot_nt(cn_ref[spans[k], :], bn_ref[spans[k], :])

    rows = rows_ref[0]
    columns = jnp.transpose(rows)
    shape = (LANES, STATE)
    gains = [
        (gs_ref[4 * i + k], gs_ref[4 * i + 2 + k]) for k in range(2)
    ]
    skip = pair_scale(skip_ref[2 * i], skip_ref[2 * i + 1], (LANES, STRETCH))
    enter0 = ent_ref[0, 0:LANES, :].astype(F32)
    leave1 = ent_ref[0, LANES : 2 * LANES, :].astype(F32)
    enter1 = pair_scale(*gains[0], shape) * enter0 + e0_ref[...]
    leave0 = t1_ref[...] + pair_scale(*gains[1], shape) * leave1
    enters = (enter0, enter1)
    leaves = (leave0, leave1)
    for k in range(2):
        span = spans[k]
        x = xT_ref[:, span].astype(F32)
        g_low = gT_ref[:, span]
        g = g_low.astype(F32)
        og = og_ref[span, :]
        step = pair_rows(rows[0:1, span], rows[1:2, span])
        ends = (rows[4:5, span], rows[5:6, span])
        coefs = (rows[0:1, span] * ends[0], rows[1:2, span] * ends[1])
        coef = pair_rows(*coefs)
        gain = pair_rows(rows[6:7, span], rows[7:8, span])
        xs = (step * x).astype(BF16)
        weighted = (coef * x).astype(BF16)
        nothing = jnp.zeros((HEAD_DIM, STRETCH), BF16)
        inner = []
        dxs = []
        for h in range(2):
            part = slice(h * HEAD_DIM, (h + 1) * HEAD_DIM)
            gap = columns[span, 2 + h : 3 + h] - rows[2 + h : 3 + h, span]
            decay = jnp.exp(gap + mask_ref[k])
            mix = (score_ref[k] * decay).astype(BF16)
            own = (xs[part], nothing) if h == 0 else (nothing, xs[part])
            dmix = dot(og, jnp.concatenate(own))
            dscore_ref[k] += dmix * decay
            inner.append(dot_nt(xs[part], mix))
            dxs.append(dot(g_low[part], mix))
        inner = jnp.concatenate(inner)
        dxs = jnp.concatenate(dxs)
        enter = enters[k].astype(BF16)
        leave = leaves[k].astype(BF16)
        carried = gain * dot_nt(enter, cn_ref[span, :])
        y = inner + carried + skip * x
        y_ref[span, :] = dot_nt(wide_unit, y.astype(BF16)).astype(BF16)
        enter_t = dot_nt(unit, enter).astype(BF16)
        leave_t = dot_nt(unit, leave).astype(BF16)
        dcT_ref[:, span] += dot(enter_t, (gain * g).astype(BF16))
        dbT_ref[:, span] += dot(leave_t, weighted)
        dweighted = dot_nt(leave, bn_ref[span, :])
        dx = step * dxs + coef * dweighted + skip * g
        dxn_ref[span, :] = dot_nt(wide_unit, dx.astype(BF16))
        moved = dweighted * x
        direct = dxs * x
        cums = g * (inner + carried) - xs.astype(F32) * dxs
        skipped = g * x
        turned = leaves[k] * enters[k]
        last = iota((1, STRETCH), 1) == STRETCH - 1
        for h in range(2):
            part = slice(h * HEAD_DIM, (h + 1) * HEAD_DIM)
            pulled = jnp.sum(moved[part], axis=0, keepdims=True)
            ended = coefs[h] * pulled
            total = jnp.sum(ended, axis=1, keepdims=True)
            bend = jnp.sum(
                jnp.sum(turned[part], axis=0, keepdims=True), axis=1, keepdims=True
            )
            dcum = jnp.sum(cums[part], axis=0, keepdims=True) - ended
            dcum = dcum + jnp.where(last, total + gains[k][h] * bend, 0.0)
            rout_ref[0, h : h + 1, span] = (
                jnp.sum(direct[part], axis=0, keepdims=True) + ends[h] * pulled
            )
            rout_ref[0, 2 + h : 3 + h, span] = dcum
            rout_ref[0, 4 + h : 5 + h, span] = jnp.sum(skipped[part], axis=0, keepdims=True)
    rout_ref[0, 6:8, :] = jnp.zeros((2, ROWS), F32)

    moved, sums = conv_back(
        pad_ref, dpad_ref, x_ref, hx_ref, xt_ref[...], xb_ref[...], keep_ref, keeps_ref, dxn_ref[...]
    )
    sx_ref[...] = moved[0:8]
    tx_ref[...] = moved[ROWS:]
    dx_ref[...] = moved[8:].astype(BF16)
    px_ref[0] = sums

    @pl.when(i % GROUP_PAIRS == GROUP_PAIRS - 1)
    def _():
        for k in range(2):
            span = spans[k]
            dscore = dscore_ref[k].astype(BF16)
            dcT = dcT_ref[:, span] + dot_nt(bT_ref[:, span], dscore)
            dbT = dbT_ref[:, span] + dot(cT_ref[:, span], dscore)
            dcT_ref[:, span] = dcT
            dbT_ref[:, span] = dbT
        sides = (
            (dbT_ref, b_ref, hb_ref, bt_ref, bb_ref, db_ref, sb_ref, tb_ref, pb_ref),
            (dcT_ref, c_ref, hc_ref, ct_ref, cb_ref, dc_ref, sc_ref, tc_ref, pc_ref),
        )
        for grad_ref, in_ref, halo_ref, tap_ref, bias_ref, out_ref, s_ref, t_ref, p_ref in sides:
            for span in spans:
                dxn_ref[span, :] = dot_nt(wide_unit, grad_ref[:, span].astype(BF16))
            moved, sums = conv_back(
                pad_ref,
                dpad_ref,
                in_ref,
                halo_ref,
                tap_ref[0],
                bias_ref[0],
                keep_ref,
                keeps_ref,
                dxn_ref[...],
            )
            s_ref[...] = moved[0:8]
            t_ref[...] = moved[ROWS:]
            out_ref[...] = moved[8:].astype(BF16)
            p_ref[0] = sums


def main_pass(gs, skip, rows, conv_args, keeps, out_grad, xT, gT, bn, cn, ent, e0, t1, labr, labc):
    wide = lambda i: (i, 0)
    col = lambda i: (0, i)
    group = lambda i: (0, i // GROUP_PAIRS)
    triple = lambda i: (i, 0, 0)
    square = (2, STRETCH, STRETCH)
    return pl.pallas_call(
        main_kernel,
        grid=(PAIRS,),
        in_specs=[
            pl.BlockSpec(memory_space=pltpu.SMEM),
            pl.BlockSpec(memory_space=pltpu.SMEM),
            pl.BlockSpec((1, 8, ROWS), triple),
        ]
        + conv_specs()
        + [
            pl.BlockSpec((KERNEL - 1, ROWS + 8, LANES), lambda i: (0, 0, 0)),
            pl.BlockSpec((ROWS, LANES), col),
            pl.BlockSpec((LANES, ROWS), wide),
            pl.BlockSpec((LANES, ROWS), wide),
            pl.BlockSpec((ROWS, LANES), group),
            pl.BlockSpec((ROWS, LANES), group),
            pl.BlockSpec((1, 2 * LANES, STATE), triple),
            pl.BlockSpec((LANES, STATE), wide),
            pl.BlockSpec((LANES, STATE), wide),
            pl.BlockSpec((8, ROWS), lambda i: (0, 0)),
            pl.BlockSpec((ROWS, LANES), lambda i: (0, 0)),
        ],
        out_specs=[
            pl.BlockSpec((ROWS, LANES), col),
            pl.BlockSpec((ROWS, LANES), col),
            pl.BlockSpec((ROWS, LANES), group),
            pl.BlockSpec((ROWS, LANES), group),
            pl.BlockSpec((8, LANES), col),
            pl.BlockSpec((8, LANES), group),
            pl.BlockSpec((8, LANES), group),
            pl.BlockSpec((1, 8, LANES), triple),
            pl.BlockSpec((1, 8, LANES), lambda i: (i // GROUP_PAIRS, 0, 0)),
            pl.BlockSpec((1, 8, LANES), lambda i: (i // GROUP_PAIRS, 0, 0)),
            pl.BlockSpec((1, 8, ROWS), triple),
            pl.BlockSpec((8, LANES), col),
            pl.BlockSpec((8, LANES), group),
            pl.BlockSpec((8, LANES), group),
        ],
        out_shape=[
            jax.ShapeDtypeStruct((ROWS, XCOLS), BF16),
            jax.ShapeDtypeStruct((ROWS, XCOLS), BF16),
            jax.ShapeDtypeStruct((ROWS, BCOLS), BF16),
            jax.ShapeDtypeStruct((ROWS, BCOLS), BF16),
            jax.ShapeDtypeStruct((8, XCOLS), F32),
            jax.ShapeDtypeStruct((8, BCOLS), F32),
            jax.ShapeDtypeStruct((8, BCOLS), F32),
            jax.ShapeDtypeStruct((PAIRS, 8, LANES), F32),
            jax.ShapeDtypeStruct((2, 8, LANES), F32),
            jax.ShapeDtypeStruct((2, 8, LANES), F32),
            jax.ShapeDtypeStruct((PAIRS, 8, ROWS), F32),
            jax.ShapeDtypeStruct((8, XCOLS), F32),
            jax.ShapeDtypeStruct((8, BCOLS), F32),
            jax.ShapeDtypeStruct((8, BCOLS), F32),
        ],
        scratch_shapes=[
            pltpu.VMEM(square, F32),
            pltpu.VMEM(square, F32),
            pltpu.VMEM(square, F32),
            pltpu.VMEM((LANES, ROWS), BF16),
            pltpu.VMEM((LANES, ROWS), BF16),
            pltpu.VMEM((LANES, ROWS), F32),
            pltpu.VMEM((LANES, ROWS), F32),
            pltpu.VMEM((ROWS + 16, LANES), F32),
            pltpu.VMEM((ROWS + 16, LANES), F32),
            pltpu.VMEM((ROWS, LANES), F32),
        ],
        name="main_pass",
    )(gs, skip, rows, *conv_args, keeps, out_grad, xT, gT, bn, cn, ent, e0, t1, labr, labc)


def segment_of(ends, positions):
    return jnp.sum((positions[:, None] >= ends[None, :]).astype(jnp.int32), axis=1)


def exact(form, left, right):
    return jnp.einsum(form, left, right, precision=lax.Precision.HIGHEST)


def passed_along(value, axis, steps):
    count = lax.axis_size(axis)
    first, last = (max(0, -steps), min(count, count - steps))
    return lax.ppermute(value, axis, [(source, source + steps) for source in range(first, last)])


def on_device(
    x_rows,
    b_rows,
    c_rows,
    dt_rows,
    length_plan,
    trace_lengths,
    x_taps,
    bc_taps,
    x_bias,
    bc_bias,
    dt_bias,
    decay_rate,
    skip_gain,
    out_grad,
):
    contexts = lax.axis_size("ctx")
    owner = lax.axis_index("dp") * contexts + lax.axis_index("ctx")
    head_at = lax.axis_index("head")
    owned = LBLOCKS * WAYS
    plan = length_plan.reshape(OWNERS, WAYS, LBLOCKS)
    column = lax.dynamic_index_in_dim(plan, head_at, 1, keepdims=False)
    base = (owner * WAYS + head_at) * LBLOCKS
    blocks = jnp.arange(LBLOCKS, dtype=jnp.int32)
    hits = column.reshape(-1)[:, None] == base + blocks[None, :]
    seats = (jnp.arange(OWNERS * LBLOCKS, dtype=jnp.int32) // LBLOCKS)[:, None]
    target = jnp.sum(jnp.where(hits, seats, 0), axis=0)
    earlier = blocks[None, :] < blocks[:, None]
    rank = jnp.sum(((target[None, :] == target[:, None]) & earlier).astype(jnp.int32), axis=1)
    pairs = jnp.arange(BLK, dtype=jnp.int32)
    goes = (((target * DEPTH + rank) * BLK)[:, None] + pairs[None, :]).reshape(-1)
    mine = lax.dynamic_slice_in_dim(length_plan, owner * owned, owned).reshape(WAYS, LBLOCKS)
    source = mine // owned
    same = source[:, :, None] == source[:, None, :]
    lower = mine[:, None, :] < mine[:, :, None]
    place = jnp.sum((same & lower).astype(jnp.int32), axis=2)
    comes = ((source * DEPTH + place) * BLK)[:, :, None] + pairs
    comes = comes.reshape(WAYS, LBLOCKS * BLK)

    spread = send_rows(goes[None, :], x_rows, b_rows, c_rows, dt_rows)
    slots = spread.shape[1]
    devices = WAYS * OWNERS

    def exchange(value):
        value = value.reshape(devices, DEPTH * BLK, COLS)
        value = lax.all_to_all(value, ROUTE, split_axis=0, concat_axis=0, tiled=True)
        return value.reshape(WAYS, slots, COLS)

    packed = pack_rows(comes[:, :, None], exchange(spread))
    halo = passed_along(packed[-8:], "ctx", 1)

    start = lax.axis_index("ctx") * ROWS
    ends = jnp.cumsum(trace_lengths[0])
    positions = start - 8 + jnp.arange(ROWS + 16, dtype=jnp.int32)
    wide_labels = jnp.where(positions >= 0, segment_of(ends, positions), -1)
    labels = wide_labels[8 : 8 + ROWS]
    keep = jnp.stack([wide_labels[5 + k : 5 + k + ROWS] == labels for k in range(KERNEL - 1)])
    keep = jnp.broadcast_to(keep.astype(F32)[:, :, None], (KERNEL - 1, ROWS, LANES))
    front = wide_labels[: ROWS + 8]
    keeps = jnp.stack(
        [
            (wide_labels[3 - k : 3 - k + ROWS + 8] == front) & (front >= 0)
            for k in range(KERNEL - 1)
        ]
    )
    keeps = jnp.broadcast_to(keeps.astype(F32)[:, :, None], (KERNEL - 1, ROWS + 8, LANES))
    grid = labels.reshape(2, STRETCH)
    before = jnp.stack([wide_labels[7], labels[STRETCH - 1]])
    last_keep = (grid == grid[:, -1:]).astype(F32)
    first_keep = (grid == before[:, None]).astype(F32)
    carry_keep = (grid[:, -1] == before).astype(F32)
    labr = jnp.broadcast_to(labels[None, :], (8, ROWS))
    labc = jnp.broadcast_to(labels[:, None], (ROWS, LANES))

    heads_dev = dt_bias.shape[0]
    dt_in = packed[:, XCOLS + 2 * BCOLS : XCOLS + 2 * BCOLS + heads_dev].astype(F32).T
    logits = dt_in + dt_bias[:, None]
    step = jax.nn.softplus(logits)
    tri = jnp.tril(jnp.ones((STRETCH, STRETCH), F32))
    folded = step.reshape(heads_dev, 2, STRETCH)
    cum = exact("hks,rs->hkr", -decay_rate[:, None, None] * folded, tri)
    to_end = jnp.exp(cum[:, :, -1:] - cum) * last_keep[None]
    gain = jnp.exp(cum) * first_keep[None]
    gs = (jnp.exp(cum[:, :, -1]) * carry_keep[None]).reshape(-1)
    rows = jnp.stack([folded, cum, to_end, gain]).reshape(4, PAIRS, 2, ROWS)
    rows = jnp.swapaxes(rows, 0, 1).reshape(PAIRS, 8, ROWS)

    bias_bc = bc_bias[:, None, :]
    conv_args = (
        packed,
        packed,
        packed,
        halo,
        halo,
        halo,
        x_taps,
        x_bias[None, :],
        bc_taps,
        bias_bc,
        bc_taps,
        bias_bc,
        keep,
    )
    ep, xT, gT, bn, cn, e0, t1 = first_pass(gs, rows, conv_args, out_grad)

    per = PAIRS // contexts
    tall = 2 * LANES + EXTRA
    ep = lax.all_to_all(
        ep.reshape(contexts, per * tall, STATE), "ctx", split_axis=0, concat_axis=0, tiled=True
    )
    scanned = scan_states(ep.reshape(contexts, per, tall, STATE))
    scanned = lax.all_to_all(
        scanned.reshape(contexts, per * 2 * LANES, STATE),
        "ctx",
        split_axis=0,
        concat_axis=0,
        tiled=True,
    )
    ent = scanned.reshape(PAIRS, 2 * LANES, STATE)

    y, dx, db, dc, tx, tb, tc, px, pb, pc, rout, sx, sb, sc = main_pass(
        gs, skip_gain, rows, conv_args, keeps, out_grad, xT, gT, bn, cn, ent, e0, t1, labr, labc
    )
    back = passed_along(jnp.concatenate([sx, sb, sc], axis=1), "ctx", -1)

    parts = rout.reshape(PAIRS, 4, 2, 2, STRETCH)
    parts = jnp.swapaxes(parts, 0, 1).reshape(4, heads_dev, 2, STRETCH)
    after = exact("hks,sr->hkr", parts[1], tri)
    dstep = parts[0] - decay_rate[:, None, None] * after
    dlogit = dstep.reshape(heads_dev, ROWS) * jax.nn.sigmoid(logits)
    ddt = jnp.pad(dlogit.T.astype(BF16), ((0, 0), (0, LANES - heads_dev)))
    scalars = jnp.concatenate(
        [
            jnp.sum(dlogit, axis=1),
            -jnp.sum(after * folded, axis=(1, 2)),
            jnp.sum(parts[2], axis=(1, 2)),
            jnp.zeros((LANES - 3 * heads_dev,), F32),
        ]
    )

    stacked = jnp.concatenate(
        [
            px[:, :5].reshape(-1, LANES),
            pb[:, :5].reshape(-1, LANES),
            pc[:, :5].reshape(-1, LANES),
            scalars[None, :],
        ]
    )
    count = stacked.shape[0]
    chunk = 4
    stacked = jnp.pad(stacked, ((0, OWNERS * chunk - count), (0, 0)))

    returned = exchange(
        unpack_rows(comes[:, None, :], dx, db, dc, ddt, tx, tb, tc, back)
    )
    x_grad, b_grad, c_grad, dt_grad = home_rows(goes[:, None], returned)

    swap = functools.partial(
        lax.all_to_all, axis_name=("dp", "ctx"), split_axis=0, concat_axis=0, tiled=True
    )
    partial_sum = jnp.sum(swap(stacked.reshape(OWNERS, chunk, LANES)), axis=0)
    whole = swap(jnp.broadcast_to(partial_sum[None], (OWNERS, chunk, LANES)))
    whole = whole.reshape(OWNERS * chunk, LANES)
    at = PAIRS * 5
    sum_x = jnp.swapaxes(whole[:at].reshape(PAIRS, 5, LANES), 0, 1).reshape(5, XCOLS)
    sum_b = jnp.swapaxes(whole[at : at + 10].reshape(2, 5, LANES), 0, 1).reshape(5, BCOLS)
    sum_c = jnp.swapaxes(whole[at + 10 : at + 20].reshape(2, 5, LANES), 0, 1).reshape(5, BCOLS)
    tail = whole[at + 20]
    return (
        y,
        x_grad,
        b_grad,
        c_grad,
        dt_grad,
        sum_x[:4],
        jnp.stack([sum_b[:4], sum_c[:4]]),
        sum_x[4],
        jnp.stack([sum_b[4], sum_c[4]]),
        tail[:heads_dev],
        tail[heads_dev : 2 * heads_dev],
        tail[2 * heads_dev : 3 * heads_dev],
    )


def solution(mesh):
    rows = P(("dp", "ctx", "head"), None)
    return jax.shard_map(
        on_device,
        mesh=mesh,
        in_specs=(
            rows,
            rows,
            rows,
            rows,
            P(),
            P("dp", None),
            P(None, "head"),
            P(None, None, "head"),
            P("head"),
            P(None, "head"),
            P("head"),
            P("head"),
            P("head"),
            P(("dp", "ctx"), "head"),
        ),
        out_specs=(
            P(("dp", "ctx"), "head"),
            rows,
            rows,
            rows,
            rows,
            P(None, "head"),
            P(None, None, "head"),
            P("head"),
            P(None, "head"),
            P("head"),
            P("head"),
            P("head"),
        ),
        check_vma=False,
    )
```

```python
import functools

import jax
import jax.numpy as jnp
from jax import lax
from jax.experimental import pallas as pl
from jax.experimental.pallas import tpu as pltpu
from jax.sharding import PartitionSpec as P

HEADS = 128
HEAD_DIM = 64
GROUPS = 8
STATE = 128
KERNEL = 4
STRETCH = 256
BLK = 2
LANES = 128
OWNERS = 32
WAYS = 4
LBLOCKS = 64
DEPTH = 4
ROWS = 512
XCOLS = 2048
BCOLS = 256
COLS = XCOLS + 2 * BCOLS + LANES
PAIRS = 16
GROUP_PAIRS = 8
EXTRA = 16
CMAIN = XCOLS + 2 * BCOLS
OWN_HEADS = HEADS // WAYS
NEG = -1e30

F32 = jnp.float32
BF16 = jnp.bfloat16
ROUTE = ("head", "dp", "ctx")


def dot(left, right):
    return lax.dot_general(left, right, (((1,), (0,)), ((), ())), preferred_element_type=F32)


def dot_nt(left, right):
    return lax.dot_general(left, right, (((1,), (1,)), ((), ())), preferred_element_type=F32)


def iota(shape, dim):
    return lax.broadcasted_iota(jnp.int32, shape, dim)


def one_hot(condition):
    return jnp.where(condition, 1.0, 0.0).astype(BF16)


def eye(size):
    return one_hot(iota((size, size), 0) == iota((size, size), 1))


def send_kernel(d_ref, x_ref, b_ref, c_ref, dt_ref, out_ref):
    way = pl.program_id(0)
    rows = x_ref.shape[0]
    spread = one_hot(iota((OWNERS * DEPTH * BLK, rows), 0) == d_ref[...])
    out_ref[0, :, :XCOLS] = dot(spread, x_ref[...]).astype(BF16)
    out_ref[0, :, XCOLS : XCOLS + BCOLS] = dot(spread, b_ref[...]).astype(BF16)
    out_ref[0, :, XCOLS + BCOLS : XCOLS + 2 * BCOLS] = dot(spread, c_ref[...]).astype(BF16)
    width = HEADS // WAYS
    lane = iota((LANES, LANES), 1)
    pick = one_hot((iota((LANES, LANES), 0) == way * width + lane) & (lane < width))
    dt_part = dot(dt_ref[...], pick).astype(BF16)
    out_ref[0, :, XCOLS + 2 * BCOLS :] = dot(spread, dt_part).astype(BF16)


def send_rows(d_row, x_rows, b_rows, c_rows, dt_rows):
    rows = x_rows.shape[0]
    slots = OWNERS * DEPTH * BLK
    return pl.pallas_call(
        send_kernel,
        grid=(WAYS,),
        in_specs=[
            pl.BlockSpec((1, rows), lambda h: (0, 0)),
            pl.BlockSpec((rows, XCOLS), lambda h: (0, h)),
            pl.BlockSpec((rows, BCOLS), lambda h: (0, h)),
            pl.BlockSpec((rows, BCOLS), lambda h: (0, h)),
            pl.BlockSpec((rows, HEADS), lambda h: (0, 0)),
        ],
        out_specs=pl.BlockSpec((1, slots, COLS), lambda h: (h, 0, 0)),
        out_shape=jax.ShapeDtypeStruct((WAYS, slots, COLS), BF16),
        name="send_rows",
    )(d_row, x_rows, b_rows, c_rows, dt_rows)


def pack_kernel(q_ref, in_ref, out_ref):
    rows = out_ref.shape[0]
    slots = in_ref.shape[1]
    pick = one_hot(iota((rows, slots), 1) == q_ref[0])
    out_ref[...] = dot(pick, in_ref[0]).astype(BF16)


def pack_rows(q_col, landed):
    slots = landed.shape[1]
    rows = ROWS // WAYS
    return pl.pallas_call(
        pack_kernel,
        grid=(WAYS,),
        in_specs=[
            pl.BlockSpec((1, rows, 1), lambda j: (j, 0, 0)),
            pl.BlockSpec((1, slots, COLS), lambda j: (j, 0, 0)),
        ],
        out_specs=pl.BlockSpec((rows, COLS), lambda j: (j, 0)),
        out_shape=jax.ShapeDtypeStruct((ROWS, COLS), BF16),
        name="pack_rows",
    )(q_col, landed)


def unpack_kernel(q_ref, x_ref, b_ref, c_ref, dt_ref, tail_ref, back_ref, out_ref):
    j = pl.program_id(0)
    rows = x_ref.shape[0]
    slots = out_ref.shape[1]
    spread = one_hot(iota((slots, rows), 0) == q_ref[0])
    last = j == WAYS - 1

    def one(ref, low, high):
        whole = ref[...].astype(F32)
        tail = tail_ref[:, low:high] + back_ref[:, low:high]
        fixed = jnp.concatenate([whole[: rows - 8], jnp.where(last, tail, whole[rows - 8 :])])
        out_ref[0, :, low:high] = dot(spread, fixed.astype(BF16)).astype(BF16)

    one(x_ref, 0, XCOLS)
    one(b_ref, XCOLS, XCOLS + BCOLS)
    one(c_ref, XCOLS + BCOLS, XCOLS + 2 * BCOLS)
    out_ref[0, :, XCOLS + 2 * BCOLS :] = dot(spread, dt_ref[...]).astype(BF16)


def unpack_rows(q_row, dx, db, dc, ddt, tails, back):
    slots = OWNERS * DEPTH * BLK
    rows = ROWS // WAYS
    full = lambda j: (0, 0)
    return pl.pallas_call(
        unpack_kernel,
        grid=(WAYS,),
        in_specs=[
            pl.BlockSpec((1, 1, rows), lambda j: (j, 0, 0)),
            pl.BlockSpec((rows, XCOLS), lambda j: (j, 0)),
            pl.BlockSpec((rows, BCOLS), lambda j: (j, 0)),
            pl.BlockSpec((rows, BCOLS), lambda j: (j, 0)),
            pl.BlockSpec((rows, LANES), lambda j: (j, 0)),
            pl.BlockSpec((8, CMAIN), full),
            pl.BlockSpec((8, CMAIN), full),
        ],
        out_specs=pl.BlockSpec((1, slots, COLS), lambda j: (j, 0, 0)),
        out_shape=jax.ShapeDtypeStruct((WAYS, slots, COLS), BF16),
        name="unpack_rows",
    )(q_row, dx, db, dc, ddt, tails, back)


def home_kernel(d_ref, in_ref, x_ref, b_ref, c_ref, dt_ref, acc_ref):
    way = pl.program_id(0)
    rows = x_ref.shape[0]
    slots = in_ref.shape[1]
    pick = one_hot(iota((rows, slots), 1) == d_ref[...])
    x_ref[...] = dot(pick, in_ref[0, :, :XCOLS]).astype(BF16)
    b_ref[...] = dot(pick, in_ref[0, :, XCOLS : XCOLS + BCOLS]).astype(BF16)
    c_ref[...] = dot(pick, in_ref[0, :, XCOLS + BCOLS : XCOLS + 2 * BCOLS]).astype(BF16)
    width = HEADS // WAYS
    lane = iota((LANES, LANES), 0)
    put = one_hot((iota((LANES, LANES), 1) == way * width + lane) & (lane < width))
    dt_part = dot(pick, in_ref[0, :, XCOLS + 2 * BCOLS :]).astype(BF16)

    @pl.when(way == 0)
    def _():
        acc_ref[...] = jnp.zeros_like(acc_ref)

    acc_ref[...] += dot(dt_part, put)
    dt_ref[...] = acc_ref[...].astype(BF16)


def home_rows(d_col, landed):
    slots = landed.shape[1]
    rows = d_col.shape[0]
    return pl.pallas_call(
        home_kernel,
        grid=(WAYS,),
        in_specs=[
            pl.BlockSpec((rows, 1), lambda h: (0, 0)),
            pl.BlockSpec((1, slots, COLS), lambda h: (h, 0, 0)),
        ],
        out_specs=[
            pl.BlockSpec((rows, XCOLS), lambda h: (0, h)),
            pl.BlockSpec((rows, BCOLS), lambda h: (0, h)),
            pl.BlockSpec((rows, BCOLS), lambda h: (0, h)),
            pl.BlockSpec((rows, HEADS), lambda h: (0, 0)),
        ],
        out_shape=[
            jax.ShapeDtypeStruct((rows, WAYS * XCOLS), BF16),
            jax.ShapeDtypeStruct((rows, WAYS * BCOLS), BF16),
            jax.ShapeDtypeStruct((rows, WAYS * BCOLS), BF16),
            jax.ShapeDtypeStruct((rows, HEADS), BF16),
        ],
        scratch_shapes=[pltpu.VMEM((rows, HEADS), F32)],
        name="home_rows",
    )(d_col, landed)


def fill_pad(pad_ref, rows_ref, halo_ref):
    pad_ref[0:8, :] = halo_ref[...].astype(F32)
    pad_ref[8 : 8 + ROWS, :] = rows_ref[...].astype(F32)


def conv_sum(pad_ref, taps, bias, keep_ref):
    total = bias + taps[0:1] * pad_ref[5 : 5 + ROWS, :] * keep_ref[0]
    total = total + taps[1:2] * pad_ref[6 : 6 + ROWS, :] * keep_ref[1]
    total = total + taps[2:3] * pad_ref[7 : 7 + ROWS, :] * keep_ref[2]
    return total + taps[3:4] * pad_ref[8 : 8 + ROWS, :]


def conv_value(pad_ref, rows_ref, halo_ref, taps, bias, keep_ref):
    fill_pad(pad_ref, rows_ref, halo_ref)
    total = conv_sum(pad_ref, taps, bias, keep_ref)
    return (total * jax.nn.sigmoid(total)).astype(BF16)


def conv_back(pad_ref, dpad_ref, rows_ref, halo_ref, taps, bias, keep_ref, keeps_ref, grad):
    fill_pad(pad_ref, rows_ref, halo_ref)
    total = conv_sum(pad_ref, taps, bias, keep_ref)
    sig = jax.nn.sigmoid(total)
    dpre = grad * (sig * (1.0 + total * (1.0 - sig)))
    dpad_ref[8 : 8 + ROWS, :] = dpre
    sums = []
    for k in range(KERNEL):
        value = dpre * pad_ref[5 + k : 5 + k + ROWS, :]
        if k < KERNEL - 1:
            value = value * keep_ref[k]
        sums.append(jnp.sum(value, axis=0, keepdims=True))
    sums.append(jnp.sum(dpre, axis=0, keepdims=True))
    sums.append(jnp.zeros((3, LANES), F32))
    span = ROWS + 8
    moved = taps[3:4] * dpad_ref[0:span, :]
    for k in range(KERNEL - 1):
        moved = moved + taps[k : k + 1] * (keeps_ref[k] * dpad_ref[3 - k : 3 - k + span, :])
    return moved, jnp.concatenate(sums)


def pair_rows(first, second, count=HEAD_DIM):
    width = first.shape[1]
    return jnp.concatenate(
        [jnp.broadcast_to(first, (count, width)), jnp.broadcast_to(second, (count, width))]
    )


def pair_scale(first, second, shape):
    return jnp.where(iota(shape, 0) < HEAD_DIM, first, second)


def first_kernel(
    gs_ref,
    rows_ref,
    x_ref,
    b_ref,
    c_ref,
    hx_ref,
    hb_ref,
    hc_ref,
    xt_ref,
    xb_ref,
    bt_ref,
    bb_ref,
    ct_ref,
    cb_ref,
    keep_ref,
    og_ref,
    ep_ref,
    xT_ref,
    gT_ref,
    bn_ref,
    cn_ref,
    e0_ref,
    t1_ref,
    pad_ref,
):
    i = pl.program_id(0)

    @pl.when(i % GROUP_PAIRS == 0)
    def _():
        bn_ref[...] = conv_value(pad_ref, b_ref, hb_ref, bt_ref[0], bb_ref[0], keep_ref)
        cn_ref[...] = conv_value(pad_ref, c_ref, hc_ref, ct_ref[0], cb_ref[0], keep_ref)

    unit = eye(LANES)
    xc = conv_value(pad_ref, x_ref, hx_ref, xt_ref[...], xb_ref[...], keep_ref)
    x_all = dot_nt(unit, xc)
    g_all = dot_nt(unit, og_ref[...])
    xT_ref[...] = x_all.astype(BF16)
    gT_ref[...] = g_all.astype(BF16)
    rows = rows_ref[0]
    states = []
    touched = []
    for k in range(2):
        span = slice(k * STRETCH, (k + 1) * STRETCH)
        coef = pair_rows(rows[0:1, span] * rows[4:5, span], rows[1:2, span] * rows[5:6, span])
        gain = pair_rows(rows[6:7, span], rows[7:8, span])
        states.append(dot((coef * x_all[:, span]).astype(BF16), bn_ref[span, :]))
        touched.append(dot((gain * g_all[:, span]).astype(BF16), cn_ref[span, :]))
    shape = (LANES, STATE)
    ga0, ga1 = gs_ref[4 * i], gs_ref[4 * i + 1]
    gb0, gb1 = gs_ref[4 * i + 2], gs_ref[4 * i + 3]
    ep_ref[0, 0:LANES, :] = (pair_scale(ga1, gb1, shape) * states[0] + states[1]).astype(BF16)
    ep_ref[0, LANES : 2 * LANES, :] = (
        touched[0] + pair_scale(ga0, gb0, shape) * touched[1]
    ).astype(BF16)
    lane = iota((EXTRA, LANES), 1)
    whole = jnp.where(lane < HEAD_DIM, ga0 * ga1, gb0 * gb1)
    high = whole.astype(BF16).astype(F32)
    low = whole - high
    ep_ref[0, 2 * LANES :, :] = jnp.where(iota((EXTRA, LANES), 0) < 8, high, low).astype(BF16)
    e0_ref[...] = states[0]
    t1_ref[...] = touched[1]


def conv_specs():
    group = lambda i: i // GROUP_PAIRS
    base_b = XCOLS // LANES
    base_c = base_b + BCOLS // LANES
    return [
        pl.BlockSpec((ROWS, LANES), lambda i: (0, i)),
        pl.BlockSpec((ROWS, LANES), lambda i: (0, base_b + group(i))),
        pl.BlockSpec((ROWS, LANES), lambda i: (0, base_c + group(i))),
        pl.BlockSpec((8, LANES), lambda i: (0, i)),
        pl.BlockSpec((8, LANES), lambda i: (0, base_b + group(i))),
        pl.BlockSpec((8, LANES), lambda i: (0, base_c + group(i))),
        pl.BlockSpec((KERNEL, LANES), lambda i: (0, i)),
        pl.BlockSpec((1, LANES), lambda i: (0, i)),
        pl.BlockSpec((1, KERNEL, LANES), lambda i: (0, 0, group(i))),
        pl.BlockSpec((1, 1, LANES), lambda i: (0, 0, group(i))),
        pl.BlockSpec((1, KERNEL, LANES), lambda i: (1, 0, group(i))),
        pl.BlockSpec((1, 1, LANES), lambda i: (1, 0, group(i))),
        pl.BlockSpec((KERNEL - 1, ROWS, LANES), lambda i: (0, 0, 0)),
    ]


def first_pass(gs, rows, conv_args, out_grad):
    wide = lambda i: (i, 0)
    group = lambda i: (0, i // GROUP_PAIRS)
    return pl.pallas_call(
        first_kernel,
        grid=(PAIRS,),
        in_specs=[
            pl.BlockSpec(memory_space=pltpu.SMEM),
            pl.BlockSpec((1, 8, ROWS), lambda i: (i, 0, 0)),
        ]
        + conv_specs()
        + [pl.BlockSpec((ROWS, LANES), lambda i: (0, i))],
        out_specs=[
            pl.BlockSpec((1, 2 * LANES + EXTRA, STATE), lambda i: (i, 0, 0)),
            pl.BlockSpec((LANES, ROWS), wide),
            pl.BlockSpec((LANES, ROWS), wide),
            pl.BlockSpec((ROWS, LANES), group),
            pl.BlockSpec((ROWS, LANES), group),
            pl.BlockSpec((LANES, STATE), wide),
            pl.BlockSpec((LANES, STATE), wide),
        ],
        out_shape=[
            jax.ShapeDtypeStruct((PAIRS, 2 * LANES + EXTRA, STATE), BF16),
            jax.ShapeDtypeStruct((XCOLS, ROWS), BF16),
            jax.ShapeDtypeStruct((XCOLS, ROWS), BF16),
            jax.ShapeDtypeStruct((ROWS, BCOLS), BF16),
            jax.ShapeDtypeStruct((ROWS, BCOLS), BF16),
            jax.ShapeDtypeStruct((XCOLS, STATE), F32),
            jax.ShapeDtypeStruct((XCOLS, STATE), F32),
        ],
        scratch_shapes=[pltpu.VMEM((ROWS + 16, LANES), F32)],
        name="first_pass",
    )(gs, rows, *conv_args, out_grad)


def state_kernel(count, in_ref, out_ref, land_ref, part_ref, send, recv, send2, recv2, own, own2):
    me = lax.axis_index("ctx")
    dp, head = lax.axis_index("dp"), lax.axis_index("head")
    barrier = pltpu.get_barrier_semaphore()
    for d in range(1, count):
        pl.semaphore_signal(
            barrier,
            inc=1,
            device_id=(dp, lax.rem(me + d, count), head),
            device_id_type=pl.DeviceIdType.MESH,
        )
    pl.semaphore_wait(barrier, count - 1)

    def moved(source, target, sends, recvs, d):
        peer = lax.rem(me + d, count)
        return pltpu.make_async_remote_copy(
            src_ref=source.at[peer],
            dst_ref=target.at[me],
            send_sem=sends.at[d],
            recv_sem=recvs.at[d],
            device_id=(dp, peer, head),
            device_id_type=pl.DeviceIdType.MESH,
        )

    first = [moved(in_ref, land_ref, send, recv, d) for d in range(1, count)]
    for copy in first:
        copy.start()
    kept = pltpu.make_async_copy(in_ref.at[me], land_ref.at[me], own)
    kept.start()
    kept.wait()
    for copy in first:
        copy.wait()
    pairs = land_ref.shape[1]
    shape = (LANES, STATE)
    for pair in range(pairs):
        gains = []
        for at in range(count):
            extra = land_ref[at, pair, 2 * LANES :, :].astype(F32)
            gain = extra[0:1] + extra[8:9]
            gains.append(pair_scale(gain[:, 0:1], gain[:, HEAD_DIM : HEAD_DIM + 1], shape))
        state = jnp.zeros(shape, F32)
        for at in range(count):
            part_ref[at, pair, 0:LANES, :] = state.astype(BF16)
            state = gains[at] * state + land_ref[at, pair, 0:LANES, :].astype(F32)
        state = jnp.zeros(shape, F32)
        for at in reversed(range(count)):
            part_ref[at, pair, LANES : 2 * LANES, :] = state.astype(BF16)
            state = land_ref[at, pair, LANES : 2 * LANES, :].astype(F32) + gains[at] * state
    second = [moved(part_ref, out_ref, send2, recv2, d) for d in range(1, count)]
    for copy in second:
        copy.start()
    kept = pltpu.make_async_copy(part_ref.at[me], out_ref.at[me], own2)
    kept.start()
    kept.wait()
    for copy in second:
        copy.wait()


def exchange_states(parts):
    count, pairs = parts.shape[:2]
    return pl.pallas_call(
        functools.partial(state_kernel, count),
        in_specs=[pl.BlockSpec(memory_space=pltpu.VMEM)],
        out_specs=pl.BlockSpec(memory_space=pltpu.VMEM),
        out_shape=jax.ShapeDtypeStruct((count, pairs, 2 * LANES, STATE), BF16),
        scratch_shapes=[
            pltpu.VMEM(parts.shape, BF16),
            pltpu.VMEM((count, pairs, 2 * LANES, STATE), BF16),
            pltpu.SemaphoreType.DMA((count,)),
            pltpu.SemaphoreType.DMA((count,)),
            pltpu.SemaphoreType.DMA((count,)),
            pltpu.SemaphoreType.DMA((count,)),
            pltpu.SemaphoreType.DMA,
            pltpu.SemaphoreType.DMA,
        ],
        compiler_params=pltpu.CompilerParams(collective_id=0, has_side_effects=True),
        name="exchange_states",
    )(parts)


def main_kernel(
    gs_ref,
    skip_ref,
    rows_ref,
    x_ref,
    b_ref,
    c_ref,
    hx_ref,
    hb_ref,
    hc_ref,
    xt_ref,
    xb_ref,
    bt_ref,
    bb_ref,
    ct_ref,
    cb_ref,
    keep_ref,
    keeps_ref,
    og_ref,
    xT_ref,
    gT_ref,
    bn_ref,
    cn_ref,
    ent_ref,
    e0_ref,
    t1_ref,
    labr_ref,
    labc_ref,
    step_ref,
    sig_ref,
    rate_ref,
    y_ref,
    dx_ref,
    db_ref,
    dc_ref,
    ddt_ref,
    tail_ref,
    front_ref,
    sums_ref,
    dcum_ref,
    dstep_ref,
    dskip_ref,
    mask_ref,
    score_ref,
    dscore_ref,
    bT_ref,
    cT_ref,
    dbT_ref,
    dcT_ref,
    pad_ref,
    dpad_ref,
    dxn_ref,
):
    i = pl.program_id(0)
    unit = eye(LANES)
    wide_unit = eye(STRETCH)
    spans = [slice(k * STRETCH, (k + 1) * STRETCH) for k in range(2)]

    @pl.when(i == 0)
    def _():
        dpad_ref[...] = jnp.zeros_like(dpad_ref)
        dcum_ref[...] = jnp.zeros_like(dcum_ref)
        dstep_ref[...] = jnp.zeros_like(dstep_ref)
        dskip_ref[...] = jnp.zeros_like(dskip_ref)
        for k in range(2):
            for t in range(2):
                shape = (STRETCH, LANES)
                left = k * STRETCH + t * LANES
                same = labc_ref[spans[k], :] == labr_ref[0:1, left : left + LANES]
                lower = iota(shape, 0) >= iota(shape, 1) + t * LANES
                mask_ref[k, :, t * LANES : (t + 1) * LANES] = jnp.where(same & lower, 0.0, NEG)

    @pl.when(i % GROUP_PAIRS == 0)
    def _():
        bT_ref[...] = dot_nt(unit, bn_ref[...]).astype(BF16)
        cT_ref[...] = dot_nt(unit, cn_ref[...]).astype(BF16)
        dbT_ref[...] = jnp.zeros_like(dbT_ref)
        dcT_ref[...] = jnp.zeros_like(dcT_ref)
        dscore_ref[...] = jnp.zeros_like(dscore_ref)
        for k in range(2):
            score_ref[k] = dot_nt(cn_ref[spans[k], :], bn_ref[spans[k], :])

    rows = rows_ref[0]
    columns = jnp.transpose(rows)
    shape = (LANES, STATE)
    gains = [
        (gs_ref[4 * i + k], gs_ref[4 * i + 2 + k]) for k in range(2)
    ]
    skip = pair_scale(skip_ref[2 * i], skip_ref[2 * i + 1], (LANES, STRETCH))
    enter0 = ent_ref[0, 0:LANES, :].astype(F32)
    leave1 = ent_ref[0, LANES : 2 * LANES, :].astype(F32)
    enter1 = pair_scale(*gains[0], shape) * enter0 + e0_ref[...]
    leave0 = t1_ref[...] + pair_scale(*gains[1], shape) * leave1
    enters = (enter0, enter1)
    leaves = (leave0, leave1)
    seat = iota((OWN_HEADS, STRETCH), 0)
    for k in range(2):
        span = spans[k]
        x = xT_ref[:, span].astype(F32)
        g_low = gT_ref[:, span]
        g = g_low.astype(F32)
        og = og_ref[span, :]
        step = pair_rows(rows[0:1, span], rows[1:2, span])
        ends = (rows[4:5, span], rows[5:6, span])
        coefs = (rows[0:1, span] * ends[0], rows[1:2, span] * ends[1])
        coef = pair_rows(*coefs)
        gain = pair_rows(rows[6:7, span], rows[7:8, span])
        xs = (step * x).astype(BF16)
        weighted = (coef * x).astype(BF16)
        nothing = jnp.zeros((HEAD_DIM, STRETCH), BF16)
        inner = []
        dxs = []
        for h in range(2):
            part = slice(h * HEAD_DIM, (h + 1) * HEAD_DIM)
            gap = columns[span, 2 + h : 3 + h] - rows[2 + h : 3 + h, span]
            decay = jnp.exp(gap + mask_ref[k])
            mix = (score_ref[k] * decay).astype(BF16)
            own = (xs[part], nothing) if h == 0 else (nothing, xs[part])
            dmix = dot(og, jnp.concatenate(own))
            dscore_ref[k] += dmix * decay
            inner.append(dot_nt(xs[part], mix))
            dxs.append(dot(g_low[part], mix))
        inner = jnp.concatenate(inner)
        dxs = jnp.concatenate(dxs)
        enter = enters[k].astype(BF16)
        leave = leaves[k].astype(BF16)
        carried = gain * dot_nt(enter, cn_ref[span, :])
        y = inner + carried + skip * x
        y_ref[span, :] = dot_nt(wide_unit, y.astype(BF16)).astype(BF16)
        enter_t = dot_nt(unit, enter).astype(BF16)
        leave_t = dot_nt(unit, leave).astype(BF16)
        dcT_ref[:, span] += dot(enter_t, (gain * g).astype(BF16))
        dbT_ref[:, span] += dot(leave_t, weighted)
        dweighted = dot_nt(leave, bn_ref[span, :])
        dx = step * dxs + coef * dweighted + skip * g
        dxn_ref[span, :] = dot_nt(wide_unit, dx.astype(BF16))
        moved = dweighted * x
        direct = dxs * x
        cums = g * (inner + carried) - xs.astype(F32) * dxs
        skipped = g * x
        turned = leaves[k] * enters[k]
        last = iota((1, STRETCH), 1) == STRETCH - 1
        for h in range(2):
            part = slice(h * HEAD_DIM, (h + 1) * HEAD_DIM)
            pulled = jnp.sum(moved[part], axis=0, keepdims=True)
            ended = coefs[h] * pulled
            total = jnp.sum(ended, axis=1, keepdims=True)
            bend = jnp.sum(
                jnp.sum(turned[part], axis=0, keepdims=True), axis=1, keepdims=True
            )
            dcum = jnp.sum(cums[part], axis=0, keepdims=True) - ended
            dcum = dcum + jnp.where(last, total + gains[k][h] * bend, 0.0)
            dstep = jnp.sum(direct[part], axis=0, keepdims=True) + ends[h] * pulled
            dskip = jnp.sum(skipped[part], axis=0, keepdims=True)
            here = seat == 2 * i + h
            dcum_ref[:, span] += jnp.where(here, dcum, 0.0)
            dstep_ref[:, span] += jnp.where(here, dstep, 0.0)
            dskip_ref[:, span] += jnp.where(here, dskip, 0.0)

    moved, sums = conv_back(
        pad_ref, dpad_ref, x_ref, hx_ref, xt_ref[...], xb_ref[...], keep_ref, keeps_ref, dxn_ref[...]
    )
    lanes = pl.ds(pl.multiple_of(i * LANES, LANES), LANES)
    front_ref[:, lanes] = moved[0:8]
    tail_ref[:, lanes] = moved[ROWS:]
    dx_ref[...] = moved[8:].astype(BF16)
    sums_ref[:, lanes] = sums

    @pl.when(i % GROUP_PAIRS == GROUP_PAIRS - 1)
    def _():
        for k in range(2):
            span = spans[k]
            dscore = dscore_ref[k].astype(BF16)
            dcT = dcT_ref[:, span] + dot_nt(bT_ref[:, span], dscore)
            dbT = dbT_ref[:, span] + dot(cT_ref[:, span], dscore)
            dcT_ref[:, span] = dcT
            dbT_ref[:, span] = dbT
        sides = (
            (dbT_ref, b_ref, hb_ref, bt_ref, bb_ref, db_ref, XCOLS),
            (dcT_ref, c_ref, hc_ref, ct_ref, cb_ref, dc_ref, XCOLS + BCOLS),
        )
        for grad_ref, in_ref, halo_ref, tap_ref, bias_ref, out_ref, left in sides:
            for span in spans:
                dxn_ref[span, :] = dot_nt(wide_unit, grad_ref[:, span].astype(BF16))
            moved, sums = conv_back(
                pad_ref,
                dpad_ref,
                in_ref,
                halo_ref,
                tap_ref[0],
                bias_ref[0],
                keep_ref,
                keeps_ref,
                dxn_ref[...],
            )
            at = pl.multiple_of(left + (i // GROUP_PAIRS) * LANES, LANES)
            front_ref[:, pl.ds(at, LANES)] = moved[0:8]
            tail_ref[:, pl.ds(at, LANES)] = moved[ROWS:]
            out_ref[...] = moved[8:].astype(BF16)
            sums_ref[:, pl.ds(at, LANES)] = sums

    @pl.when(i == PAIRS - 1)
    def _():
        shape = (STRETCH, STRETCH)
        tri = jnp.where(iota(shape, 0) >= iota(shape, 1), 1.0, 0.0)
        bias_sum = jnp.zeros((OWN_HEADS, 1), F32)
        rate_sum = jnp.zeros((OWN_HEADS, 1), F32)
        for span in spans:
            after = lax.dot_general(
                dcum_ref[:, span],
                tri,
                (((1,), (0,)), ((), ())),
                precision=lax.Precision.HIGHEST,
                preferred_element_type=F32,
            )
            dlogit = (dstep_ref[:, span] - rate_ref[...] * after) * sig_ref[:, span]
            bias_sum += jnp.sum(dlogit, axis=1, keepdims=True)
            rate_sum -= jnp.sum(after * step_ref[:, span], axis=1, keepdims=True)
            tall = jnp.concatenate([dlogit, jnp.zeros((LANES - OWN_HEADS, STRETCH), F32)])
            ddt_ref[span, :] = dot_nt(wide_unit, tall.astype(BF16)).astype(BF16)
        skip_sum = jnp.sum(dskip_ref[...], axis=1, keepdims=True)
        diagonal = iota((OWN_HEADS, LANES), 0) == iota((OWN_HEADS, LANES), 1)
        lines = [
            jnp.sum(jnp.where(diagonal, value, 0.0), axis=0, keepdims=True)
            for value in (bias_sum, rate_sum, skip_sum)
        ]
        sums_ref[:, CMAIN:] = jnp.concatenate(lines + [jnp.zeros((5, LANES), F32)])


def main_pass(
    gs, skip, rows, conv_args, keeps, out_grad, xT, gT, bn, cn, ent, e0, t1, labr, labc, heads
):
    wide = lambda i: (i, 0)
    col = lambda i: (0, i)
    group = lambda i: (0, i // GROUP_PAIRS)
    triple = lambda i: (i, 0, 0)
    fixed = lambda i: (0, 0)
    square = (2, STRETCH, STRETCH)
    return pl.pallas_call(
        main_kernel,
        grid=(PAIRS,),
        in_specs=[
            pl.BlockSpec(memory_space=pltpu.SMEM),
            pl.BlockSpec(memory_space=pltpu.SMEM),
            pl.BlockSpec((1, 8, ROWS), triple),
        ]
        + conv_specs()
        + [
            pl.BlockSpec((KERNEL - 1, ROWS + 8, LANES), lambda i: (0, 0, 0)),
            pl.BlockSpec((ROWS, LANES), col),
            pl.BlockSpec((LANES, ROWS), wide),
            pl.BlockSpec((LANES, ROWS), wide),
            pl.BlockSpec((ROWS, LANES), group),
            pl.BlockSpec((ROWS, LANES), group),
            pl.BlockSpec((1, 2 * LANES, STATE), triple),
            pl.BlockSpec((LANES, STATE), wide),
            pl.BlockSpec((LANES, STATE), wide),
            pl.BlockSpec((8, ROWS), fixed),
            pl.BlockSpec((ROWS, LANES), fixed),
            pl.BlockSpec((OWN_HEADS, ROWS), fixed),
            pl.BlockSpec((OWN_HEADS, ROWS), fixed),
            pl.BlockSpec((OWN_HEADS, 1), fixed),
        ],
        out_specs=[
            pl.BlockSpec((ROWS, LANES), col),
            pl.BlockSpec((ROWS, LANES), col),
            pl.BlockSpec((ROWS, LANES), group),
            pl.BlockSpec((ROWS, LANES), group),
            pl.BlockSpec((ROWS, LANES), fixed),
            pl.BlockSpec((8, CMAIN), fixed),
            pl.BlockSpec((8, CMAIN), fixed),
            pl.BlockSpec((8, COLS), fixed),
        ],
        out_shape=[
            jax.ShapeDtypeStruct((ROWS, XCOLS), BF16),
            jax.ShapeDtypeStruct((ROWS, XCOLS), BF16),
            jax.ShapeDtypeStruct((ROWS, BCOLS), BF16),
            jax.ShapeDtypeStruct((ROWS, BCOLS), BF16),
            jax.ShapeDtypeStruct((ROWS, LANES), BF16),
            jax.ShapeDtypeStruct((8, CMAIN), F32),
            jax.ShapeDtypeStruct((8, CMAIN), F32),
            jax.ShapeDtypeStruct((8, COLS), F32),
        ],
        scratch_shapes=[
            pltpu.VMEM((OWN_HEADS, ROWS), F32),
            pltpu.VMEM((OWN_HEADS, ROWS), F32),
            pltpu.VMEM((OWN_HEADS, ROWS), F32),
            pltpu.VMEM(square, F32),
            pltpu.VMEM(square, F32),
            pltpu.VMEM(square, F32),
            pltpu.VMEM((LANES, ROWS), BF16),
            pltpu.VMEM((LANES, ROWS), BF16),
            pltpu.VMEM((LANES, ROWS), F32),
            pltpu.VMEM((LANES, ROWS), F32),
            pltpu.VMEM((ROWS + 16, LANES), F32),
            pltpu.VMEM((ROWS + 16, LANES), F32),
            pltpu.VMEM((ROWS, LANES), F32),
        ],
        name="main_pass",
    )(gs, skip, rows, *conv_args, keeps, out_grad, xT, gT, bn, cn, ent, e0, t1, labr, labc, *heads)


def segment_of(ends, positions):
    return jnp.sum((positions[:, None] >= ends[None, :]).astype(jnp.int32), axis=1)


def exact(form, left, right):
    return jnp.einsum(form, left, right, precision=lax.Precision.HIGHEST)


def passed_along(value, axis, steps):
    count = lax.axis_size(axis)
    first, last = (max(0, -steps), min(count, count - steps))
    return lax.ppermute(value, axis, [(source, source + steps) for source in range(first, last)])


def on_device(
    x_rows,
    b_rows,
    c_rows,
    dt_rows,
    length_plan,
    trace_lengths,
    x_taps,
    bc_taps,
    x_bias,
    bc_bias,
    dt_bias,
    decay_rate,
    skip_gain,
    out_grad,
):
    contexts = lax.axis_size("ctx")
    owner = lax.axis_index("dp") * contexts + lax.axis_index("ctx")
    head_at = lax.axis_index("head")
    owned = LBLOCKS * WAYS
    plan = length_plan.reshape(OWNERS, WAYS, LBLOCKS)
    column = lax.dynamic_index_in_dim(plan, head_at, 1, keepdims=False)
    base = (owner * WAYS + head_at) * LBLOCKS
    blocks = jnp.arange(LBLOCKS, dtype=jnp.int32)
    hits = column.reshape(-1)[:, None] == base + blocks[None, :]
    seats = (jnp.arange(OWNERS * LBLOCKS, dtype=jnp.int32) // LBLOCKS)[:, None]
    target = jnp.sum(jnp.where(hits, seats, 0), axis=0)
    earlier = blocks[None, :] < blocks[:, None]
    rank = jnp.sum(((target[None, :] == target[:, None]) & earlier).astype(jnp.int32), axis=1)
    pairs = jnp.arange(BLK, dtype=jnp.int32)
    goes = (((target * DEPTH + rank) * BLK)[:, None] + pairs[None, :]).reshape(-1)
    mine = lax.dynamic_slice_in_dim(length_plan, owner * owned, owned).reshape(WAYS, LBLOCKS)
    source = mine // owned
    same = source[:, :, None] == source[:, None, :]
    lower = mine[:, None, :] < mine[:, :, None]
    place = jnp.sum((same & lower).astype(jnp.int32), axis=2)
    comes = ((source * DEPTH + place) * BLK)[:, :, None] + pairs
    comes = comes.reshape(WAYS, LBLOCKS * BLK)

    spread = send_rows(goes[None, :], x_rows, b_rows, c_rows, dt_rows)
    slots = spread.shape[1]
    devices = WAYS * OWNERS

    def exchange(value):
        value = value.reshape(devices, DEPTH * BLK, COLS)
        value = lax.all_to_all(value, ROUTE, split_axis=0, concat_axis=0, tiled=True)
        return value.reshape(WAYS, slots, COLS)

    packed = pack_rows(comes[:, :, None], exchange(spread))
    halo = passed_along(packed[-8:], "ctx", 1)

    start = lax.axis_index("ctx") * ROWS
    ends = jnp.cumsum(trace_lengths[0])
    positions = start - 8 + jnp.arange(ROWS + 16, dtype=jnp.int32)
    wide_labels = jnp.where(positions >= 0, segment_of(ends, positions), -1)
    labels = wide_labels[8 : 8 + ROWS]
    keep = jnp.stack([wide_labels[5 + k : 5 + k + ROWS] == labels for k in range(KERNEL - 1)])
    keep = jnp.broadcast_to(keep.astype(F32)[:, :, None], (KERNEL - 1, ROWS, LANES))
    front = wide_labels[: ROWS + 8]
    keeps = jnp.stack(
        [
            (wide_labels[3 - k : 3 - k + ROWS + 8] == front) & (front >= 0)
            for k in range(KERNEL - 1)
        ]
    )
    keeps = jnp.broadcast_to(keeps.astype(F32)[:, :, None], (KERNEL - 1, ROWS + 8, LANES))
    grid = labels.reshape(2, STRETCH)
    before = jnp.stack([wide_labels[7], labels[STRETCH - 1]])
    last_keep = (grid == grid[:, -1:]).astype(F32)
    first_keep = (grid == before[:, None]).astype(F32)
    carry_keep = (grid[:, -1] == before).astype(F32)
    labr = jnp.broadcast_to(labels[None, :], (8, ROWS))
    labc = jnp.broadcast_to(labels[:, None], (ROWS, LANES))

    heads_dev = dt_bias.shape[0]
    dt_in = packed[:, XCOLS + 2 * BCOLS : XCOLS + 2 * BCOLS + heads_dev].astype(F32).T
    logits = dt_in + dt_bias[:, None]
    step = jax.nn.softplus(logits)
    sig = jax.nn.sigmoid(logits)
    tri = jnp.tril(jnp.ones((STRETCH, STRETCH), F32))
    folded = step.reshape(heads_dev, 2, STRETCH)
    cum = exact("hks,rs->hkr", -decay_rate[:, None, None] * folded, tri)
    to_end = jnp.exp(cum[:, :, -1:] - cum) * last_keep[None]
    gain = jnp.exp(cum) * first_keep[None]
    gs = (jnp.exp(cum[:, :, -1]) * carry_keep[None]).reshape(-1)
    rows = jnp.stack([folded, cum, to_end, gain]).reshape(4, PAIRS, 2, ROWS)
    rows = jnp.swapaxes(rows, 0, 1).reshape(PAIRS, 8, ROWS)

    bias_bc = bc_bias[:, None, :]
    conv_args = (
        packed,
        packed,
        packed,
        halo,
        halo,
        halo,
        x_taps,
        x_bias[None, :],
        bc_taps,
        bias_bc,
        bc_taps,
        bias_bc,
        keep,
    )
    ep, xT, gT, bn, cn, e0, t1 = first_pass(gs, rows, conv_args, out_grad)

    per = PAIRS // contexts
    tall = 2 * LANES + EXTRA
    ent = exchange_states(ep.reshape(contexts, per, tall, STATE))
    ent = ent.reshape(PAIRS, 2 * LANES, STATE)

    heads = (step, sig, decay_rate[:, None])
    y, dx, db, dc, ddt, tails, fronts, sums = main_pass(
        gs,
        skip_gain,
        rows,
        conv_args,
        keeps,
        out_grad,
        xT,
        gT,
        bn,
        cn,
        ent,
        e0,
        t1,
        labr,
        labc,
        heads,
    )
    back = passed_along(fronts, "ctx", -1)
    returned = exchange(unpack_rows(comes[:, None, :], dx, db, dc, ddt, tails, back))
    x_grad, b_grad, c_grad, dt_grad = home_rows(goes[:, None], returned)

    swap = functools.partial(
        lax.all_to_all, axis_name=("dp", "ctx"), split_axis=0, concat_axis=0, tiled=True
    )
    share = COLS // OWNERS
    partial_sum = jnp.sum(swap(jnp.swapaxes(sums.reshape(8, OWNERS, share), 0, 1)), axis=0)
    whole = swap(jnp.broadcast_to(partial_sum[None], (OWNERS, 8, share)))
    whole = jnp.swapaxes(whole, 0, 1).reshape(8, COLS)
    sum_x = whole[:, :XCOLS]
    sum_b = whole[:, XCOLS : XCOLS + BCOLS]
    sum_c = whole[:, XCOLS + BCOLS : CMAIN]
    tail = whole[:, CMAIN : CMAIN + heads_dev]
    return (
        y,
        x_grad,
        b_grad,
        c_grad,
        dt_grad,
        sum_x[:4],
        jnp.stack([sum_b[:4], sum_c[:4]]),
        sum_x[4],
        jnp.stack([sum_b[4], sum_c[4]]),
        tail[0],
        tail[1],
        tail[2],
    )


def solution(mesh):
    rows = P(("dp", "ctx", "head"), None)
    return jax.shard_map(
        on_device,
        mesh=mesh,
        in_specs=(
            rows,
            rows,
            rows,
            rows,
            P(),
            P("dp", None),
            P(None, "head"),
            P(None, None, "head"),
            P("head"),
            P(None, "head"),
            P("head"),
            P("head"),
            P("head"),
            P(("dp", "ctx"), "head"),
        ),
        out_specs=(
            P(("dp", "ctx"), "head"),
            rows,
            rows,
            rows,
            rows,
            P(None, "head"),
            P(None, None, "head"),
            P("head"),
            P(None, "head"),
            P("head"),
            P("head"),
            P("head"),
        ),
        check_vma=False,
    )
```

```python
import functools

import jax
import jax.numpy as jnp
from jax import lax
from jax.experimental import pallas as pl
from jax.experimental.pallas import tpu as pltpu
from jax.sharding import PartitionSpec as P

HEADS = 128
HEAD_DIM = 64
GROUPS = 8
STATE = 128
KERNEL = 4
STRETCH = 256
BLK = 2
LANES = 128
OWNERS = 32
WAYS = 4
LBLOCKS = 64
DEPTH = 4
ROWS = 512
XCOLS = 2048
BCOLS = 256
COLS = XCOLS + 2 * BCOLS + LANES
PAIRS = 16
GROUP_PAIRS = 8
EXTRA = 16
CMAIN = XCOLS + 2 * BCOLS
OWN_HEADS = HEADS // WAYS
NEG = -1e30
STRIDE = 37

F32 = jnp.float32
BF16 = jnp.bfloat16


def dot(left, right):
    return lax.dot_general(left, right, (((1,), (0,)), ((), ())), preferred_element_type=F32)


def dot_nt(left, right):
    return lax.dot_general(left, right, (((1,), (1,)), ((), ())), preferred_element_type=F32)


def iota(shape, dim):
    return lax.broadcasted_iota(jnp.int32, shape, dim)


def one_hot(condition):
    return jnp.where(condition, 1.0, 0.0).astype(BF16)


def eye(size):
    return one_hot(iota((size, size), 0) == iota((size, size), 1))


def device_of(slot, head):
    contexts = lax.axis_size("ctx")
    return (slot // contexts, lax.rem(slot, contexts), head)


def greet_all(barrier, owner, head):
    for s in range(WAYS):
        way = lax.rem(head + s, WAYS)

        def greet(t, carry, way=way):
            pl.semaphore_signal(
                barrier,
                inc=1,
                device_id=device_of(lax.rem(owner + t, OWNERS), way),
                device_id_type=pl.DeviceIdType.MESH,
            )
            return carry

        lax.fori_loop(0 if s else 1, OWNERS, greet, 0)


def slot_rows(at):
    return pl.ds(pl.multiple_of(at * DEPTH * BLK, DEPTH * BLK), DEPTH * BLK)


def block_copy(stage_ref, land_ref, send, recv, owner, head, s, t):
    way = lax.rem(head + s, WAYS)
    slot = lax.rem(owner + t, OWNERS)
    return pltpu.make_async_remote_copy(
        src_ref=stage_ref.at[way, slot_rows(slot), :],
        dst_ref=land_ref.at[head, slot_rows(owner), :],
        send_sem=send.at[s, t],
        recv_sem=recv.at[s, t],
        device_id=device_of(slot, way),
        device_id_type=pl.DeviceIdType.MESH,
    )


def over_slots(act):
    def body(t, carry):
        act(t)
        return carry

    lax.fori_loop(1, OWNERS, body, 0)


def over_blocks(act):
    count = WAYS * OWNERS

    def body(m, carry):
        at = lax.rem(m * STRIDE, count)
        act(lax.rem(at, WAYS), at // WAYS)
        return carry

    lax.fori_loop(1, count, body, 0)


def route_in_kernel(
    d_ref, q_ref, x_ref, b_ref, c_ref, dt_ref, out_ref, stage_ref, land_ref, send, recv, own
):
    head = lax.axis_index("head")
    owner = lax.axis_index("dp") * lax.axis_size("ctx") + lax.axis_index("ctx")
    barrier = pltpu.get_barrier_semaphore()
    greet_all(barrier, owner, head)
    rows = x_ref.shape[0]
    slots = OWNERS * DEPTH * BLK
    spread = one_hot(iota((slots, rows), 0) == d_ref[...])
    copies = functools.partial(block_copy, stage_ref, land_ref, send, recv, owner, head)
    for s in range(WAYS):
        way = lax.rem(head + s, WAYS)

        def columns(size):
            return pl.ds(pl.multiple_of(way * size, size), size)

        stage_ref[way, :, :XCOLS] = dot(spread, x_ref[:, columns(XCOLS)]).astype(BF16)
        stage_ref[way, :, XCOLS : XCOLS + BCOLS] = dot(spread, b_ref[:, columns(BCOLS)]).astype(
            BF16
        )
        stage_ref[way, :, XCOLS + BCOLS : CMAIN] = dot(spread, c_ref[:, columns(BCOLS)]).astype(
            BF16
        )
        lane = iota((LANES, LANES), 1)
        pick = one_hot(
            (iota((LANES, LANES), 0) == way * OWN_HEADS + lane) & (lane < OWN_HEADS)
        )
        dt_part = dot(dt_ref[...], pick).astype(BF16)
        stage_ref[way, :, CMAIN:] = dot(spread, dt_part).astype(BF16)
    pl.semaphore_wait(barrier, WAYS * OWNERS - 1)
    over_blocks(lambda s, t: copies(s, t).start())
    kept = pltpu.make_async_copy(
        stage_ref.at[head, slot_rows(owner), :], land_ref.at[head, slot_rows(owner), :], own
    )
    kept.start()
    kept.wait()
    part = ROWS // WAYS
    over_blocks(lambda s, t: copies(s, t).wait_recv())
    for s in range(WAYS):
        way = lax.rem(head + WAYS - s, WAYS)
        pick = one_hot(iota((part, slots), 1) == q_ref[way])
        out_ref[pl.ds(pl.multiple_of(way * part, part), part), :] = dot(
            pick, land_ref[way]
        ).astype(BF16)
    over_blocks(lambda s, t: copies(s, t).wait_send())


def route_in(d_row, q_col, x_rows, b_rows, c_rows, dt_rows):
    slots = OWNERS * DEPTH * BLK
    return pl.pallas_call(
        route_in_kernel,
        in_specs=[pl.BlockSpec(memory_space=pltpu.VMEM)] * 6,
        out_specs=pl.BlockSpec(memory_space=pltpu.VMEM),
        out_shape=jax.ShapeDtypeStruct((ROWS, COLS), BF16),
        scratch_shapes=[
            pltpu.VMEM((WAYS, slots, COLS), BF16),
            pltpu.VMEM((WAYS, slots, COLS), BF16),
            pltpu.SemaphoreType.DMA((WAYS, OWNERS)),
            pltpu.SemaphoreType.DMA((WAYS, OWNERS)),
            pltpu.SemaphoreType.DMA,
        ],
        compiler_params=pltpu.CompilerParams(collective_id=1, has_side_effects=True),
        name="route_in",
    )(d_row, q_col, x_rows, b_rows, c_rows, dt_rows)


def route_out_kernel(
    q_ref,
    d_ref,
    dx_ref,
    db_ref,
    dc_ref,
    ddt_ref,
    tail_ref,
    back_ref,
    sums_ref,
    x_ref,
    b_ref,
    c_ref,
    dt_ref,
    total_ref,
    stage_ref,
    land_ref,
    held_ref,
    part_ref,
    send,
    recv,
    send1,
    recv1,
    send2,
    recv2,
    own,
):
    head = lax.axis_index("head")
    owner = lax.axis_index("dp") * lax.axis_size("ctx") + lax.axis_index("ctx")
    barrier = pltpu.get_barrier_semaphore()
    greet_all(barrier, owner, head)
    rows = ROWS // WAYS
    slots = OWNERS * DEPTH * BLK
    copies = functools.partial(block_copy, stage_ref, land_ref, send, recv, owner, head)

    def sum_copy(t):
        slot = lax.rem(owner + t, OWNERS)
        return pltpu.make_async_remote_copy(
            src_ref=sums_ref.at[slot],
            dst_ref=held_ref.at[owner],
            send_sem=send1.at[t],
            recv_sem=recv1.at[t],
            device_id=device_of(slot, head),
            device_id_type=pl.DeviceIdType.MESH,
        )

    def total_copy(t):
        return pltpu.make_async_remote_copy(
            src_ref=part_ref,
            dst_ref=total_ref.at[owner],
            send_sem=send2.at[t],
            recv_sem=recv2.at[t],
            device_id=device_of(lax.rem(owner + t, OWNERS), head),
            device_id_type=pl.DeviceIdType.MESH,
        )

    for s in range(WAYS):
        way = lax.rem(head + s, WAYS)
        here = pl.ds(pl.multiple_of(way * rows, rows), rows)
        spread = one_hot(iota((slots, rows), 0) == q_ref[way])

        def one(ref, low, high):
            whole = ref[here, :].astype(F32)
            tail = tail_ref[:, low:high] + back_ref[:, low:high]
            tail = jnp.where(way == WAYS - 1, tail, whole[rows - 8 :])
            fixed = jnp.concatenate([whole[: rows - 8], tail])
            stage_ref[way, :, low:high] = dot(spread, fixed.astype(BF16)).astype(BF16)

        one(dx_ref, 0, XCOLS)
        one(db_ref, XCOLS, XCOLS + BCOLS)
        one(dc_ref, XCOLS + BCOLS, CMAIN)
        stage_ref[way, :, CMAIN:] = dot(spread, ddt_ref[here, :]).astype(BF16)
    pl.semaphore_wait(barrier, WAYS * OWNERS - 1)
    over_slots(lambda t: sum_copy(t).start())
    over_blocks(lambda s, t: copies(s, t).start())
    kept = pltpu.make_async_copy(
        stage_ref.at[head, slot_rows(owner), :], land_ref.at[head, slot_rows(owner), :], own
    )
    kept.start()
    kept.wait()
    held_ref[owner] = sums_ref[owner]
    over_slots(lambda t: sum_copy(t).wait_recv())
    total = jnp.sum(held_ref[...], axis=0)
    part_ref[...] = total
    total_ref[owner] = total
    over_slots(lambda t: total_copy(t).start())
    rows = d_ref.shape[0]
    pick = one_hot(iota((rows, slots), 1) == d_ref[...])
    times = jnp.zeros((rows, HEADS), F32)
    over_blocks(lambda s, t: copies(s, t).wait_recv())
    for s in range(WAYS):
        way = lax.rem(head + WAYS - s, WAYS)

        def columns(size):
            return pl.ds(pl.multiple_of(way * size, size), size)

        x_ref[:, columns(XCOLS)] = dot(pick, land_ref[way, :, :XCOLS]).astype(BF16)
        b_ref[:, columns(BCOLS)] = dot(pick, land_ref[way, :, XCOLS : XCOLS + BCOLS]).astype(BF16)
        c_ref[:, columns(BCOLS)] = dot(pick, land_ref[way, :, XCOLS + BCOLS : CMAIN]).astype(BF16)
        lane = iota((LANES, LANES), 0)
        put = one_hot(
            (iota((LANES, LANES), 1) == way * OWN_HEADS + lane) & (lane < OWN_HEADS)
        )
        times += dot(dot(pick, land_ref[way, :, CMAIN:]).astype(BF16), put)
    dt_ref[...] = times.astype(BF16)
    over_slots(lambda t: total_copy(t).wait_recv())
    over_slots(lambda t: sum_copy(t).wait_send())
    over_slots(lambda t: total_copy(t).wait_send())
    over_blocks(lambda s, t: copies(s, t).wait_send())


def route_out(q_row, d_col, dx, db, dc, ddt, tails, back, sums):
    slots = OWNERS * DEPTH * BLK
    rows = d_col.shape[0]
    space = pl.BlockSpec(memory_space=pltpu.VMEM)
    return pl.pallas_call(
        route_out_kernel,
        in_specs=[space] * 9,
        out_specs=[space] * 5,
        out_shape=[
            jax.ShapeDtypeStruct((rows, WAYS * XCOLS), BF16),
            jax.ShapeDtypeStruct((rows, WAYS * BCOLS), BF16),
            jax.ShapeDtypeStruct((rows, WAYS * BCOLS), BF16),
            jax.ShapeDtypeStruct((rows, HEADS), BF16),
            jax.ShapeDtypeStruct((OWNERS, 8, LANES), F32),
        ],
        scratch_shapes=[
            pltpu.VMEM((WAYS, slots, COLS), BF16),
            pltpu.VMEM((WAYS, slots, COLS), BF16),
            pltpu.VMEM((OWNERS, 8, LANES), F32),
            pltpu.VMEM((8, LANES), F32),
            pltpu.SemaphoreType.DMA((WAYS, OWNERS)),
            pltpu.SemaphoreType.DMA((WAYS, OWNERS)),
            pltpu.SemaphoreType.DMA((OWNERS,)),
            pltpu.SemaphoreType.DMA((OWNERS,)),
            pltpu.SemaphoreType.DMA((OWNERS,)),
            pltpu.SemaphoreType.DMA((OWNERS,)),
            pltpu.SemaphoreType.DMA,
        ],
        compiler_params=pltpu.CompilerParams(collective_id=2, has_side_effects=True),
        name="route_out",
    )(q_row, d_col, dx, db, dc, ddt, tails, back, sums)


def fill_pad(pad_ref, rows_ref, halo_ref):
    pad_ref[0:8, :] = halo_ref[...].astype(F32)
    pad_ref[8 : 8 + ROWS, :] = rows_ref[...].astype(F32)


def conv_sum(pad_ref, taps, bias, keep_ref):
    total = bias + taps[0:1] * pad_ref[5 : 5 + ROWS, :] * keep_ref[0]
    total = total + taps[1:2] * pad_ref[6 : 6 + ROWS, :] * keep_ref[1]
    total = total + taps[2:3] * pad_ref[7 : 7 + ROWS, :] * keep_ref[2]
    return total + taps[3:4] * pad_ref[8 : 8 + ROWS, :]


def conv_value(pad_ref, rows_ref, halo_ref, taps, bias, keep_ref):
    fill_pad(pad_ref, rows_ref, halo_ref)
    total = conv_sum(pad_ref, taps, bias, keep_ref)
    return (total * jax.nn.sigmoid(total)).astype(BF16)


def conv_back(pad_ref, dpad_ref, rows_ref, halo_ref, taps, bias, keep_ref, keeps_ref, grad):
    fill_pad(pad_ref, rows_ref, halo_ref)
    total = conv_sum(pad_ref, taps, bias, keep_ref)
    sig = jax.nn.sigmoid(total)
    dpre = grad * (sig * (1.0 + total * (1.0 - sig)))
    dpad_ref[8 : 8 + ROWS, :] = dpre
    sums = []
    for k in range(KERNEL):
        value = dpre * pad_ref[5 + k : 5 + k + ROWS, :]
        if k < KERNEL - 1:
            value = value * keep_ref[k]
        sums.append(jnp.sum(value, axis=0, keepdims=True))
    sums.append(jnp.sum(dpre, axis=0, keepdims=True))
    sums.append(jnp.zeros((3, LANES), F32))
    span = ROWS + 8
    moved = taps[3:4] * dpad_ref[0:span, :]
    for k in range(KERNEL - 1):
        moved = moved + taps[k : k + 1] * (keeps_ref[k] * dpad_ref[3 - k : 3 - k + span, :])
    return moved, jnp.concatenate(sums)


def pair_rows(first, second, count=HEAD_DIM):
    width = first.shape[1]
    return jnp.concatenate(
        [jnp.broadcast_to(first, (count, width)), jnp.broadcast_to(second, (count, width))]
    )


def pair_scale(first, second, shape):
    return jnp.where(iota(shape, 0) < HEAD_DIM, first, second)


def first_kernel(
    gs_ref,
    rows_ref,
    x_ref,
    b_ref,
    c_ref,
    hx_ref,
    hb_ref,
    hc_ref,
    xt_ref,
    xb_ref,
    bt_ref,
    bb_ref,
    ct_ref,
    cb_ref,
    keep_ref,
    og_ref,
    ep_ref,
    xT_ref,
    gT_ref,
    bn_ref,
    cn_ref,
    e0_ref,
    t1_ref,
    pad_ref,
):
    i = pl.program_id(0)

    @pl.when(i % GROUP_PAIRS == 0)
    def _():
        bn_ref[...] = conv_value(pad_ref, b_ref, hb_ref, bt_ref[0], bb_ref[0], keep_ref)
        cn_ref[...] = conv_value(pad_ref, c_ref, hc_ref, ct_ref[0], cb_ref[0], keep_ref)

    unit = eye(LANES)
    xc = conv_value(pad_ref, x_ref, hx_ref, xt_ref[...], xb_ref[...], keep_ref)
    x_all = dot_nt(unit, xc)
    g_all = dot_nt(unit, og_ref[...])
    xT_ref[...] = x_all.astype(BF16)
    gT_ref[...] = g_all.astype(BF16)
    rows = rows_ref[0]
    states = []
    touched = []
    for k in range(2):
        span = slice(k * STRETCH, (k + 1) * STRETCH)
        coef = pair_rows(rows[0:1, span] * rows[4:5, span], rows[1:2, span] * rows[5:6, span])
        gain = pair_rows(rows[6:7, span], rows[7:8, span])
        states.append(dot((coef * x_all[:, span]).astype(BF16), bn_ref[span, :]))
        touched.append(dot((gain * g_all[:, span]).astype(BF16), cn_ref[span, :]))
    shape = (LANES, STATE)
    ga0, ga1 = gs_ref[4 * i], gs_ref[4 * i + 1]
    gb0, gb1 = gs_ref[4 * i + 2], gs_ref[4 * i + 3]
    ep_ref[0, 0:LANES, :] = (pair_scale(ga1, gb1, shape) * states[0] + states[1]).astype(BF16)
    ep_ref[0, LANES : 2 * LANES, :] = (
        touched[0] + pair_scale(ga0, gb0, shape) * touched[1]
    ).astype(BF16)
    lane = iota((EXTRA, LANES), 1)
    whole = jnp.where(lane < HEAD_DIM, ga0 * ga1, gb0 * gb1)
    high = whole.astype(BF16).astype(F32)
    low = whole - high
    ep_ref[0, 2 * LANES :, :] = jnp.where(iota((EXTRA, LANES), 0) < 8, high, low).astype(BF16)
    e0_ref[...] = states[0]
    t1_ref[...] = touched[1]


def conv_specs():
    group = lambda i: i // GROUP_PAIRS
    base_b = XCOLS // LANES
    base_c = base_b + BCOLS // LANES
    return [
        pl.BlockSpec((ROWS, LANES), lambda i: (0, i)),
        pl.BlockSpec((ROWS, LANES), lambda i: (0, base_b + group(i))),
        pl.BlockSpec((ROWS, LANES), lambda i: (0, base_c + group(i))),
        pl.BlockSpec((8, LANES), lambda i: (0, i)),
        pl.BlockSpec((8, LANES), lambda i: (0, base_b + group(i))),
        pl.BlockSpec((8, LANES), lambda i: (0, base_c + group(i))),
        pl.BlockSpec((KERNEL, LANES), lambda i: (0, i)),
        pl.BlockSpec((1, LANES), lambda i: (0, i)),
        pl.BlockSpec((1, KERNEL, LANES), lambda i: (0, 0, group(i))),
        pl.BlockSpec((1, 1, LANES), lambda i: (0, 0, group(i))),
        pl.BlockSpec((1, KERNEL, LANES), lambda i: (1, 0, group(i))),
        pl.BlockSpec((1, 1, LANES), lambda i: (1, 0, group(i))),
        pl.BlockSpec((KERNEL - 1, ROWS, LANES), lambda i: (0, 0, 0)),
    ]


def first_pass(gs, rows, conv_args, out_grad):
    wide = lambda i: (i, 0)
    group = lambda i: (0, i // GROUP_PAIRS)
    return pl.pallas_call(
        first_kernel,
        grid=(PAIRS,),
        in_specs=[
            pl.BlockSpec(memory_space=pltpu.SMEM),
            pl.BlockSpec((1, 8, ROWS), lambda i: (i, 0, 0)),
        ]
        + conv_specs()
        + [pl.BlockSpec((ROWS, LANES), lambda i: (0, i))],
        out_specs=[
            pl.BlockSpec((1, 2 * LANES + EXTRA, STATE), lambda i: (i, 0, 0)),
            pl.BlockSpec((LANES, ROWS), wide),
            pl.BlockSpec((LANES, ROWS), wide),
            pl.BlockSpec((ROWS, LANES), group),
            pl.BlockSpec((ROWS, LANES), group),
            pl.BlockSpec((LANES, STATE), wide),
            pl.BlockSpec((LANES, STATE), wide),
        ],
        out_shape=[
            jax.ShapeDtypeStruct((PAIRS, 2 * LANES + EXTRA, STATE), BF16),
            jax.ShapeDtypeStruct((XCOLS, ROWS), BF16),
            jax.ShapeDtypeStruct((XCOLS, ROWS), BF16),
            jax.ShapeDtypeStruct((ROWS, BCOLS), BF16),
            jax.ShapeDtypeStruct((ROWS, BCOLS), BF16),
            jax.ShapeDtypeStruct((XCOLS, STATE), F32),
            jax.ShapeDtypeStruct((XCOLS, STATE), F32),
        ],
        scratch_shapes=[pltpu.VMEM((ROWS + 16, LANES), F32)],
        name="first_pass",
    )(gs, rows, *conv_args, out_grad)


def state_kernel(count, in_ref, out_ref, land_ref, part_ref, send, recv, send2, recv2, own, own2):
    me = lax.axis_index("ctx")
    dp, head = lax.axis_index("dp"), lax.axis_index("head")
    barrier = pltpu.get_barrier_semaphore()
    for d in range(1, count):
        pl.semaphore_signal(
            barrier,
            inc=1,
            device_id=(dp, lax.rem(me + d, count), head),
            device_id_type=pl.DeviceIdType.MESH,
        )
    pl.semaphore_wait(barrier, count - 1)

    def moved(source, target, sends, recvs, d):
        peer = lax.rem(me + d, count)
        return pltpu.make_async_remote_copy(
            src_ref=source.at[peer],
            dst_ref=target.at[me],
            send_sem=sends.at[d],
            recv_sem=recvs.at[d],
            device_id=(dp, peer, head),
            device_id_type=pl.DeviceIdType.MESH,
        )

    first = [moved(in_ref, land_ref, send, recv, d) for d in range(1, count)]
    for copy in first:
        copy.start()
    kept = pltpu.make_async_copy(in_ref.at[me], land_ref.at[me], own)
    kept.start()
    kept.wait()
    for copy in first:
        copy.wait()
    pairs = land_ref.shape[1]
    shape = (LANES, STATE)
    for pair in range(pairs):
        gains = []
        for at in range(count):
            extra = land_ref[at, pair, 2 * LANES :, :].astype(F32)
            gain = extra[0:1] + extra[8:9]
            gains.append(pair_scale(gain[:, 0:1], gain[:, HEAD_DIM : HEAD_DIM + 1], shape))
        state = jnp.zeros(shape, F32)
        for at in range(count):
            part_ref[at, pair, 0:LANES, :] = state.astype(BF16)
            state = gains[at] * state + land_ref[at, pair, 0:LANES, :].astype(F32)
        state = jnp.zeros(shape, F32)
        for at in reversed(range(count)):
            part_ref[at, pair, LANES : 2 * LANES, :] = state.astype(BF16)
            state = land_ref[at, pair, LANES : 2 * LANES, :].astype(F32) + gains[at] * state
    second = [moved(part_ref, out_ref, send2, recv2, d) for d in range(1, count)]
    for copy in second:
        copy.start()
    kept = pltpu.make_async_copy(part_ref.at[me], out_ref.at[me], own2)
    kept.start()
    kept.wait()
    for copy in second:
        copy.wait()


def exchange_states(parts):
    count, pairs = parts.shape[:2]
    return pl.pallas_call(
        functools.partial(state_kernel, count),
        in_specs=[pl.BlockSpec(memory_space=pltpu.VMEM)],
        out_specs=pl.BlockSpec(memory_space=pltpu.VMEM),
        out_shape=jax.ShapeDtypeStruct((count, pairs, 2 * LANES, STATE), BF16),
        scratch_shapes=[
            pltpu.VMEM(parts.shape, BF16),
            pltpu.VMEM((count, pairs, 2 * LANES, STATE), BF16),
            pltpu.SemaphoreType.DMA((count,)),
            pltpu.SemaphoreType.DMA((count,)),
            pltpu.SemaphoreType.DMA((count,)),
            pltpu.SemaphoreType.DMA((count,)),
            pltpu.SemaphoreType.DMA,
            pltpu.SemaphoreType.DMA,
        ],
        compiler_params=pltpu.CompilerParams(collective_id=0, has_side_effects=True),
        name="exchange_states",
    )(parts)


def main_kernel(
    gs_ref,
    skip_ref,
    rows_ref,
    x_ref,
    b_ref,
    c_ref,
    hx_ref,
    hb_ref,
    hc_ref,
    xt_ref,
    xb_ref,
    bt_ref,
    bb_ref,
    ct_ref,
    cb_ref,
    keep_ref,
    keeps_ref,
    og_ref,
    xT_ref,
    gT_ref,
    bn_ref,
    cn_ref,
    ent_ref,
    e0_ref,
    t1_ref,
    labr_ref,
    labc_ref,
    step_ref,
    sig_ref,
    rate_ref,
    y_ref,
    dx_ref,
    db_ref,
    dc_ref,
    ddt_ref,
    tail_ref,
    front_ref,
    sums_ref,
    dcum_ref,
    dstep_ref,
    dskip_ref,
    mask_ref,
    score_ref,
    dscore_ref,
    bT_ref,
    cT_ref,
    dbT_ref,
    dcT_ref,
    pad_ref,
    dpad_ref,
    dxn_ref,
):
    i = pl.program_id(0)
    unit = eye(LANES)
    wide_unit = eye(STRETCH)
    spans = [slice(k * STRETCH, (k + 1) * STRETCH) for k in range(2)]

    @pl.when(i == 0)
    def _():
        dpad_ref[...] = jnp.zeros_like(dpad_ref)
        sums_ref[...] = jnp.zeros_like(sums_ref)
        dcum_ref[...] = jnp.zeros_like(dcum_ref)
        dstep_ref[...] = jnp.zeros_like(dstep_ref)
        dskip_ref[...] = jnp.zeros_like(dskip_ref)
        for k in range(2):
            for t in range(2):
                shape = (STRETCH, LANES)
                left = k * STRETCH + t * LANES
                same = labc_ref[spans[k], :] == labr_ref[0:1, left : left + LANES]
                lower = iota(shape, 0) >= iota(shape, 1) + t * LANES
                mask_ref[k, :, t * LANES : (t + 1) * LANES] = jnp.where(same & lower, 0.0, NEG)

    @pl.when(i % GROUP_PAIRS == 0)
    def _():
        bT_ref[...] = dot_nt(unit, bn_ref[...]).astype(BF16)
        cT_ref[...] = dot_nt(unit, cn_ref[...]).astype(BF16)
        dbT_ref[...] = jnp.zeros_like(dbT_ref)
        dcT_ref[...] = jnp.zeros_like(dcT_ref)
        dscore_ref[...] = jnp.zeros_like(dscore_ref)
        for k in range(2):
            score_ref[k] = dot_nt(cn_ref[spans[k], :], bn_ref[spans[k], :])

    rows = rows_ref[0]
    columns = jnp.transpose(rows)
    shape = (LANES, STATE)
    gains = [
        (gs_ref[4 * i + k], gs_ref[4 * i + 2 + k]) for k in range(2)
    ]
    skip = pair_scale(skip_ref[2 * i], skip_ref[2 * i + 1], (LANES, STRETCH))
    enter0 = ent_ref[0, 0:LANES, :].astype(F32)
    leave1 = ent_ref[0, LANES : 2 * LANES, :].astype(F32)
    enter1 = pair_scale(*gains[0], shape) * enter0 + e0_ref[...]
    leave0 = t1_ref[...] + pair_scale(*gains[1], shape) * leave1
    enters = (enter0, enter1)
    leaves = (leave0, leave1)
    seat = iota((OWN_HEADS, STRETCH), 0)
    for k in range(2):
        span = spans[k]
        x = xT_ref[:, span].astype(F32)
        g_low = gT_ref[:, span]
        g = g_low.astype(F32)
        og = og_ref[span, :]
        step = pair_rows(rows[0:1, span], rows[1:2, span])
        ends = (rows[4:5, span], rows[5:6, span])
        coefs = (rows[0:1, span] * ends[0], rows[1:2, span] * ends[1])
        coef = pair_rows(*coefs)
        gain = pair_rows(rows[6:7, span], rows[7:8, span])
        xs = (step * x).astype(BF16)
        weighted = (coef * x).astype(BF16)
        nothing = jnp.zeros((HEAD_DIM, STRETCH), BF16)
        inner = []
        dxs = []
        for h in range(2):
            part = slice(h * HEAD_DIM, (h + 1) * HEAD_DIM)
            gap = columns[span, 2 + h : 3 + h] - rows[2 + h : 3 + h, span]
            decay = jnp.exp(gap + mask_ref[k])
            mix = (score_ref[k] * decay).astype(BF16)
            own = (xs[part], nothing) if h == 0 else (nothing, xs[part])
            dmix = dot(og, jnp.concatenate(own))
            dscore_ref[k] += dmix * decay
            inner.append(dot_nt(xs[part], mix))
            dxs.append(dot(g_low[part], mix))
        inner = jnp.concatenate(inner)
        dxs = jnp.concatenate(dxs)
        enter = enters[k].astype(BF16)
        leave = leaves[k].astype(BF16)
        carried = gain * dot_nt(enter, cn_ref[span, :])
        y = inner + carried + skip * x
        y_ref[span, :] = dot_nt(wide_unit, y.astype(BF16)).astype(BF16)
        enter_t = dot_nt(unit, enter).astype(BF16)
        leave_t = dot_nt(unit, leave).astype(BF16)
        dcT_ref[:, span] += dot(enter_t, (gain * g).astype(BF16))
        dbT_ref[:, span] += dot(leave_t, weighted)
        dweighted = dot_nt(leave, bn_ref[span, :])
        dx = step * dxs + coef * dweighted + skip * g
        dxn_ref[span, :] = dot_nt(wide_unit, dx.astype(BF16))
        moved = dweighted * x
        direct = dxs * x
        cums = g * (inner + carried) - xs.astype(F32) * dxs
        skipped = g * x
        turned = leaves[k] * enters[k]
        last = iota((1, STRETCH), 1) == STRETCH - 1
        for h in range(2):
            part = slice(h * HEAD_DIM, (h + 1) * HEAD_DIM)
            pulled = jnp.sum(moved[part], axis=0, keepdims=True)
            ended = coefs[h] * pulled
            total = jnp.sum(ended, axis=1, keepdims=True)
            bend = jnp.sum(
                jnp.sum(turned[part], axis=0, keepdims=True), axis=1, keepdims=True
            )
            dcum = jnp.sum(cums[part], axis=0, keepdims=True) - ended
            dcum = dcum + jnp.where(last, total + gains[k][h] * bend, 0.0)
            dstep = jnp.sum(direct[part], axis=0, keepdims=True) + ends[h] * pulled
            dskip = jnp.sum(skipped[part], axis=0, keepdims=True)
            here = seat == 2 * i + h
            dcum_ref[:, span] += jnp.where(here, dcum, 0.0)
            dstep_ref[:, span] += jnp.where(here, dstep, 0.0)
            dskip_ref[:, span] += jnp.where(here, dskip, 0.0)

    moved, sums = conv_back(
        pad_ref, dpad_ref, x_ref, hx_ref, xt_ref[...], xb_ref[...], keep_ref, keeps_ref, dxn_ref[...]
    )
    lanes = pl.ds(pl.multiple_of(i * LANES, LANES), LANES)
    front_ref[:, lanes] = moved[0:8]
    tail_ref[:, lanes] = moved[ROWS:]
    dx_ref[...] = moved[8:].astype(BF16)
    sums_ref[i] = sums

    @pl.when(i % GROUP_PAIRS == GROUP_PAIRS - 1)
    def _():
        for k in range(2):
            span = spans[k]
            dscore = dscore_ref[k].astype(BF16)
            dcT = dcT_ref[:, span] + dot_nt(bT_ref[:, span], dscore)
            dbT = dbT_ref[:, span] + dot(cT_ref[:, span], dscore)
            dcT_ref[:, span] = dcT
            dbT_ref[:, span] = dbT
        sides = (
            (dbT_ref, b_ref, hb_ref, bt_ref, bb_ref, db_ref, XCOLS),
            (dcT_ref, c_ref, hc_ref, ct_ref, cb_ref, dc_ref, XCOLS + BCOLS),
        )
        for grad_ref, in_ref, halo_ref, tap_ref, bias_ref, out_ref, left in sides:
            for span in spans:
                dxn_ref[span, :] = dot_nt(wide_unit, grad_ref[:, span].astype(BF16))
            moved, sums = conv_back(
                pad_ref,
                dpad_ref,
                in_ref,
                halo_ref,
                tap_ref[0],
                bias_ref[0],
                keep_ref,
                keeps_ref,
                dxn_ref[...],
            )
            at = pl.multiple_of(left + (i // GROUP_PAIRS) * LANES, LANES)
            front_ref[:, pl.ds(at, LANES)] = moved[0:8]
            tail_ref[:, pl.ds(at, LANES)] = moved[ROWS:]
            out_ref[...] = moved[8:].astype(BF16)
            sums_ref[left // LANES + i // GROUP_PAIRS] = sums

    @pl.when(i == PAIRS - 1)
    def _():
        shape = (STRETCH, STRETCH)
        tri = jnp.where(iota(shape, 0) >= iota(shape, 1), 1.0, 0.0)
        bias_sum = jnp.zeros((OWN_HEADS, 1), F32)
        rate_sum = jnp.zeros((OWN_HEADS, 1), F32)
        for span in spans:
            after = lax.dot_general(
                dcum_ref[:, span],
                tri,
                (((1,), (0,)), ((), ())),
                precision=lax.Precision.HIGHEST,
                preferred_element_type=F32,
            )
            dlogit = (dstep_ref[:, span] - rate_ref[...] * after) * sig_ref[:, span]
            bias_sum += jnp.sum(dlogit, axis=1, keepdims=True)
            rate_sum -= jnp.sum(after * step_ref[:, span], axis=1, keepdims=True)
            tall = jnp.concatenate([dlogit, jnp.zeros((LANES - OWN_HEADS, STRETCH), F32)])
            ddt_ref[span, :] = dot_nt(wide_unit, tall.astype(BF16)).astype(BF16)
        skip_sum = jnp.sum(dskip_ref[...], axis=1, keepdims=True)
        diagonal = iota((OWN_HEADS, LANES), 0) == iota((OWN_HEADS, LANES), 1)
        lines = [
            jnp.sum(jnp.where(diagonal, value, 0.0), axis=0, keepdims=True)
            for value in (bias_sum, rate_sum, skip_sum)
        ]
        sums_ref[CMAIN // LANES] = jnp.concatenate(lines + [jnp.zeros((5, LANES), F32)])


def main_pass(
    gs, skip, rows, conv_args, keeps, out_grad, xT, gT, bn, cn, ent, e0, t1, labr, labc, heads
):
    wide = lambda i: (i, 0)
    col = lambda i: (0, i)
    group = lambda i: (0, i // GROUP_PAIRS)
    triple = lambda i: (i, 0, 0)
    fixed = lambda i: (0, 0)
    square = (2, STRETCH, STRETCH)
    return pl.pallas_call(
        main_kernel,
        grid=(PAIRS,),
        in_specs=[
            pl.BlockSpec(memory_space=pltpu.SMEM),
            pl.BlockSpec(memory_space=pltpu.SMEM),
            pl.BlockSpec((1, 8, ROWS), triple),
        ]
        + conv_specs()
        + [
            pl.BlockSpec((KERNEL - 1, ROWS + 8, LANES), lambda i: (0, 0, 0)),
            pl.BlockSpec((ROWS, LANES), col),
            pl.BlockSpec((LANES, ROWS), wide),
            pl.BlockSpec((LANES, ROWS), wide),
            pl.BlockSpec((ROWS, LANES), group),
            pl.BlockSpec((ROWS, LANES), group),
            pl.BlockSpec((1, 2 * LANES, STATE), triple),
            pl.BlockSpec((LANES, STATE), wide),
            pl.BlockSpec((LANES, STATE), wide),
            pl.BlockSpec((8, ROWS), fixed),
            pl.BlockSpec((ROWS, LANES), fixed),
            pl.BlockSpec((OWN_HEADS, ROWS), fixed),
            pl.BlockSpec((OWN_HEADS, ROWS), fixed),
            pl.BlockSpec((OWN_HEADS, 1), fixed),
        ],
        out_specs=[
            pl.BlockSpec((ROWS, LANES), col),
            pl.BlockSpec((ROWS, LANES), col),
            pl.BlockSpec((ROWS, LANES), group),
            pl.BlockSpec((ROWS, LANES), group),
            pl.BlockSpec((ROWS, LANES), fixed),
            pl.BlockSpec((8, CMAIN), fixed),
            pl.BlockSpec((8, CMAIN), fixed),
            pl.BlockSpec((OWNERS, 8, LANES), lambda i: (0, 0, 0)),
        ],
        out_shape=[
            jax.ShapeDtypeStruct((ROWS, XCOLS), BF16),
            jax.ShapeDtypeStruct((ROWS, XCOLS), BF16),
            jax.ShapeDtypeStruct((ROWS, BCOLS), BF16),
            jax.ShapeDtypeStruct((ROWS, BCOLS), BF16),
            jax.ShapeDtypeStruct((ROWS, LANES), BF16),
            jax.ShapeDtypeStruct((8, CMAIN), F32),
            jax.ShapeDtypeStruct((8, CMAIN), F32),
            jax.ShapeDtypeStruct((OWNERS, 8, LANES), F32),
        ],
        scratch_shapes=[
            pltpu.VMEM((OWN_HEADS, ROWS), F32),
            pltpu.VMEM((OWN_HEADS, ROWS), F32),
            pltpu.VMEM((OWN_HEADS, ROWS), F32),
            pltpu.VMEM(square, F32),
            pltpu.VMEM(square, F32),
            pltpu.VMEM(square, F32),
            pltpu.VMEM((LANES, ROWS), BF16),
            pltpu.VMEM((LANES, ROWS), BF16),
            pltpu.VMEM((LANES, ROWS), F32),
            pltpu.VMEM((LANES, ROWS), F32),
            pltpu.VMEM((ROWS + 16, LANES), F32),
            pltpu.VMEM((ROWS + 16, LANES), F32),
            pltpu.VMEM((ROWS, LANES), F32),
        ],
        name="main_pass",
    )(gs, skip, rows, *conv_args, keeps, out_grad, xT, gT, bn, cn, ent, e0, t1, labr, labc, *heads)


def segment_of(ends, positions):
    return jnp.sum((positions[:, None] >= ends[None, :]).astype(jnp.int32), axis=1)


def exact(form, left, right):
    return jnp.einsum(form, left, right, precision=lax.Precision.HIGHEST)


def passed_along(value, axis, steps):
    count = lax.axis_size(axis)
    first, last = (max(0, -steps), min(count, count - steps))
    return lax.ppermute(value, axis, [(source, source + steps) for source in range(first, last)])


def on_device(
    x_rows,
    b_rows,
    c_rows,
    dt_rows,
    length_plan,
    trace_lengths,
    x_taps,
    bc_taps,
    x_bias,
    bc_bias,
    dt_bias,
    decay_rate,
    skip_gain,
    out_grad,
):
    contexts = lax.axis_size("ctx")
    owner = lax.axis_index("dp") * contexts + lax.axis_index("ctx")
    head_at = lax.axis_index("head")
    owned = LBLOCKS * WAYS
    plan = length_plan.reshape(OWNERS, WAYS, LBLOCKS)
    column = lax.dynamic_index_in_dim(plan, head_at, 1, keepdims=False)
    base = (owner * WAYS + head_at) * LBLOCKS
    blocks = jnp.arange(LBLOCKS, dtype=jnp.int32)
    hits = column.reshape(-1)[:, None] == base + blocks[None, :]
    seats = (jnp.arange(OWNERS * LBLOCKS, dtype=jnp.int32) // LBLOCKS)[:, None]
    target = jnp.sum(jnp.where(hits, seats, 0), axis=0)
    earlier = blocks[None, :] < blocks[:, None]
    rank = jnp.sum(((target[None, :] == target[:, None]) & earlier).astype(jnp.int32), axis=1)
    pairs = jnp.arange(BLK, dtype=jnp.int32)
    goes = (((target * DEPTH + rank) * BLK)[:, None] + pairs[None, :]).reshape(-1)
    mine = lax.dynamic_slice_in_dim(length_plan, owner * owned, owned).reshape(WAYS, LBLOCKS)
    source = mine // owned
    same = source[:, :, None] == source[:, None, :]
    lower = mine[:, None, :] < mine[:, :, None]
    place = jnp.sum((same & lower).astype(jnp.int32), axis=2)
    comes = ((source * DEPTH + place) * BLK)[:, :, None] + pairs
    comes = comes.reshape(WAYS, LBLOCKS * BLK)

    packed = route_in(goes[None, :], comes[:, :, None], x_rows, b_rows, c_rows, dt_rows)
    halo = passed_along(packed[-8:], "ctx", 1)

    start = lax.axis_index("ctx") * ROWS
    ends = jnp.cumsum(trace_lengths[0])
    positions = start - 8 + jnp.arange(ROWS + 16, dtype=jnp.int32)
    wide_labels = jnp.where(positions >= 0, segment_of(ends, positions), -1)
    labels = wide_labels[8 : 8 + ROWS]
    keep = jnp.stack([wide_labels[5 + k : 5 + k + ROWS] == labels for k in range(KERNEL - 1)])
    keep = jnp.broadcast_to(keep.astype(F32)[:, :, None], (KERNEL - 1, ROWS, LANES))
    front = wide_labels[: ROWS + 8]
    keeps = jnp.stack(
        [
            (wide_labels[3 - k : 3 - k + ROWS + 8] == front) & (front >= 0)
            for k in range(KERNEL - 1)
        ]
    )
    keeps = jnp.broadcast_to(keeps.astype(F32)[:, :, None], (KERNEL - 1, ROWS + 8, LANES))
    grid = labels.reshape(2, STRETCH)
    before = jnp.stack([wide_labels[7], labels[STRETCH - 1]])
    last_keep = (grid == grid[:, -1:]).astype(F32)
    first_keep = (grid == before[:, None]).astype(F32)
    carry_keep = (grid[:, -1] == before).astype(F32)
    labr = jnp.broadcast_to(labels[None, :], (8, ROWS))
    labc = jnp.broadcast_to(labels[:, None], (ROWS, LANES))

    heads_dev = dt_bias.shape[0]
    dt_in = packed[:, XCOLS + 2 * BCOLS : XCOLS + 2 * BCOLS + heads_dev].astype(F32).T
    logits = dt_in + dt_bias[:, None]
    step = jax.nn.softplus(logits)
    sig = jax.nn.sigmoid(logits)
    tri = jnp.tril(jnp.ones((STRETCH, STRETCH), F32))
    folded = step.reshape(heads_dev, 2, STRETCH)
    cum = exact("hks,rs->hkr", -decay_rate[:, None, None] * folded, tri)
    to_end = jnp.exp(cum[:, :, -1:] - cum) * last_keep[None]
    gain = jnp.exp(cum) * first_keep[None]
    gs = (jnp.exp(cum[:, :, -1]) * carry_keep[None]).reshape(-1)
    rows = jnp.stack([folded, cum, to_end, gain]).reshape(4, PAIRS, 2, ROWS)
    rows = jnp.swapaxes(rows, 0, 1).reshape(PAIRS, 8, ROWS)

    bias_bc = bc_bias[:, None, :]
    conv_args = (
        packed,
        packed,
        packed,
        halo,
        halo,
        halo,
        x_taps,
        x_bias[None, :],
        bc_taps,
        bias_bc,
        bc_taps,
        bias_bc,
        keep,
    )
    ep, xT, gT, bn, cn, e0, t1 = first_pass(gs, rows, conv_args, out_grad)

    per = PAIRS // contexts
    tall = 2 * LANES + EXTRA
    ent = exchange_states(ep.reshape(contexts, per, tall, STATE))
    ent = ent.reshape(PAIRS, 2 * LANES, STATE)

    heads = (step, sig, decay_rate[:, None])
    y, dx, db, dc, ddt, tails, fronts, sums = main_pass(
        gs,
        skip_gain,
        rows,
        conv_args,
        keeps,
        out_grad,
        xT,
        gT,
        bn,
        cn,
        ent,
        e0,
        t1,
        labr,
        labc,
        heads,
    )
    back = passed_along(fronts, "ctx", -1)
    x_grad, b_grad, c_grad, dt_grad, whole = route_out(
        comes[:, None, :], goes[:, None], dx, db, dc, ddt, tails, back, sums
    )
    whole = jnp.swapaxes(whole, 0, 1).reshape(8, OWNERS * LANES)
    sum_x = whole[:, :XCOLS]
    sum_b = whole[:, XCOLS : XCOLS + BCOLS]
    sum_c = whole[:, XCOLS + BCOLS : CMAIN]
    tail = whole[:, CMAIN : CMAIN + heads_dev]
    return (
        y,
        x_grad,
        b_grad,
        c_grad,
        dt_grad,
        sum_x[:4],
        jnp.stack([sum_b[:4], sum_c[:4]]),
        sum_x[4],
        jnp.stack([sum_b[4], sum_c[4]]),
        tail[0],
        tail[1],
        tail[2],
    )


def solution(mesh):
    rows = P(("dp", "ctx", "head"), None)
    return jax.shard_map(
        on_device,
        mesh=mesh,
        in_specs=(
            rows,
            rows,
            rows,
            rows,
            P(),
            P("dp", None),
            P(None, "head"),
            P(None, None, "head"),
            P("head"),
            P(None, "head"),
            P("head"),
            P("head"),
            P("head"),
            P(("dp", "ctx"), "head"),
        ),
        out_specs=(
            P(("dp", "ctx"), "head"),
            rows,
            rows,
            rows,
            rows,
            P(None, "head"),
            P(None, None, "head"),
            P("head"),
            P(None, "head"),
            P("head"),
            P("head"),
            P("head"),
        ),
        check_vma=False,
    )
```

```python
import functools

import jax
import jax.numpy as jnp
from jax import lax
from jax.experimental import pallas as pl
from jax.experimental.pallas import tpu as pltpu
from jax.sharding import PartitionSpec as P

HEADS = 128
HEAD_DIM = 64
GROUPS = 8
STATE = 128
KERNEL = 4
STRETCH = 256
BLK = 2
LANES = 128
OWNERS = 32
WAYS = 4
LBLOCKS = 64
DEPTH = 4
ROWS = 512
XCOLS = 2048
BCOLS = 256
COLS = XCOLS + 2 * BCOLS + LANES
PAIRS = 16
GROUP_PAIRS = 8
EXTRA = 16
CMAIN = XCOLS + 2 * BCOLS
OWN_HEADS = HEADS // WAYS
NEG = -1e30
STRIDE = 37

F32 = jnp.float32
BF16 = jnp.bfloat16


def dot(left, right):
    return lax.dot_general(left, right, (((1,), (0,)), ((), ())), preferred_element_type=F32)


def dot_nt(left, right):
    return lax.dot_general(left, right, (((1,), (1,)), ((), ())), preferred_element_type=F32)


def iota(shape, dim):
    return lax.broadcasted_iota(jnp.int32, shape, dim)


def one_hot(condition):
    return jnp.where(condition, 1.0, 0.0).astype(BF16)


def eye(size):
    return one_hot(iota((size, size), 0) == iota((size, size), 1))


def device_of(slot, head):
    contexts = lax.axis_size("ctx")
    return (slot // contexts, lax.rem(slot, contexts), head)


def greet_all(barrier, owner, head):
    for s in range(WAYS):
        way = lax.rem(head + s, WAYS)

        def greet(t, carry, way=way):
            pl.semaphore_signal(
                barrier,
                inc=1,
                device_id=device_of(lax.rem(owner + t, OWNERS), way),
                device_id_type=pl.DeviceIdType.MESH,
            )
            return carry

        lax.fori_loop(0 if s else 1, OWNERS, greet, 0)


def slot_rows(at):
    return pl.ds(pl.multiple_of(at * DEPTH * BLK, DEPTH * BLK), DEPTH * BLK)


def block_copy(stage_ref, land_ref, send, recv, owner, head, s, t):
    way = lax.rem(head + s, WAYS)
    slot = lax.rem(owner + t, OWNERS)
    return pltpu.make_async_remote_copy(
        src_ref=stage_ref.at[way, slot_rows(slot), :],
        dst_ref=land_ref.at[head, slot_rows(owner), :],
        send_sem=send.at[s, t],
        recv_sem=recv.at[s, t],
        device_id=device_of(slot, way),
        device_id_type=pl.DeviceIdType.MESH,
    )


def over_slots(act):
    def body(t, carry):
        act(t)
        return carry

    lax.fori_loop(1, OWNERS, body, 0)


def over_blocks(act):
    count = WAYS * OWNERS

    def body(m, carry):
        at = lax.rem(m * STRIDE, count)
        act(lax.rem(at, WAYS), at // WAYS)
        return carry

    lax.fori_loop(1, count, body, 0)


def as_column(row):
    size = row.shape[1]
    diagonal = iota((size, size), 0) == iota((size, size), 1)
    return jnp.sum(jnp.where(diagonal, row, 0.0), axis=1, keepdims=True)


def route_in_kernel(
    d_ref,
    q_ref,
    x_ref,
    b_ref,
    c_ref,
    dt_ref,
    bias_ref,
    rate_ref,
    lengths_ref,
    out_ref,
    halo_ref,
    rows_ref,
    step_ref,
    sig_ref,
    gain_ref,
    label_ref,
    labr_ref,
    stage_ref,
    land_ref,
    send,
    recv,
    own,
    send_halo,
    recv_halo,
):
    head = lax.axis_index("head")
    owner = lax.axis_index("dp") * lax.axis_size("ctx") + lax.axis_index("ctx")
    barrier = pltpu.get_barrier_semaphore()
    greet_all(barrier, owner, head)
    rows = x_ref.shape[0]
    slots = OWNERS * DEPTH * BLK
    spread = one_hot(iota((slots, rows), 0) == d_ref[...])
    copies = functools.partial(block_copy, stage_ref, land_ref, send, recv, owner, head)
    for s in range(WAYS):
        way = lax.rem(head + s, WAYS)

        def columns(size):
            return pl.ds(pl.multiple_of(way * size, size), size)

        stage_ref[way, :, :XCOLS] = dot(spread, x_ref[:, columns(XCOLS)]).astype(BF16)
        stage_ref[way, :, XCOLS : XCOLS + BCOLS] = dot(spread, b_ref[:, columns(BCOLS)]).astype(
            BF16
        )
        stage_ref[way, :, XCOLS + BCOLS : CMAIN] = dot(spread, c_ref[:, columns(BCOLS)]).astype(
            BF16
        )
        lane = iota((LANES, LANES), 1)
        pick = one_hot(
            (iota((LANES, LANES), 0) == way * OWN_HEADS + lane) & (lane < OWN_HEADS)
        )
        dt_part = dot(dt_ref[...], pick).astype(BF16)
        stage_ref[way, :, CMAIN:] = dot(spread, dt_part).astype(BF16)
    pl.semaphore_wait(barrier, WAYS * OWNERS - 1)
    over_blocks(lambda s, t: copies(s, t).start())
    kept = pltpu.make_async_copy(
        stage_ref.at[head, slot_rows(owner), :], land_ref.at[head, slot_rows(owner), :], own
    )
    kept.start()
    kept.wait()
    start = lax.axis_index("ctx") * ROWS
    ends = []
    for at in range(lengths_ref.shape[1]):
        ends.append(lengths_ref[0, at] + (ends[-1] if ends else 0))

    def label_of(places):
        total = jnp.zeros(places.shape, jnp.int32)
        for end in ends:
            total = total + jnp.where(places >= end, 1, 0)
        return jnp.where(places >= 0, total, -1)

    label_ref[...] = label_of(iota(label_ref.shape, 0) + (start - 8))
    labr_ref[...] = label_of(iota(labr_ref.shape, 1) + start)
    labels = labr_ref[0:1, :]
    lasts = [labels[:, STRETCH - 1 : STRETCH], labels[:, ROWS - 1 : ROWS]]
    befores = [label_of(iota((1, LANES), 0) + (start - 1))[:, 0:1], lasts[0]]
    bias, rate = as_column(bias_ref[...]), as_column(rate_ref[...])
    part = ROWS // WAYS
    over_blocks(lambda s, t: copies(s, t).wait_recv())
    for s in range(WAYS):
        way = lax.rem(head + WAYS - s, WAYS)
        places = as_column(q_ref[way].astype(F32))
        pick = one_hot(iota((part, slots), 1).astype(F32) == places)
        out_ref[pl.ds(pl.multiple_of(way * part, part), part), :] = dot(
            pick, land_ref[way]
        ).astype(BF16)
    context = lax.axis_index("ctx")
    contexts = lax.axis_size("ctx")
    passed = pltpu.make_async_remote_copy(
        src_ref=out_ref.at[pl.ds(ROWS - 8, 8), :],
        dst_ref=halo_ref,
        send_sem=send_halo,
        recv_sem=recv_halo,
        device_id=(lax.axis_index("dp"), lax.rem(context + 1, contexts), head),
        device_id_type=pl.DeviceIdType.MESH,
    )

    @pl.when(context < contexts - 1)
    def _():
        passed.start()

    @pl.when(context == 0)
    def _():
        halo_ref[...] = jnp.zeros_like(halo_ref)

    logits = dot_nt(eye(LANES), out_ref[:, CMAIN:])[:OWN_HEADS] + bias
    step = jnp.maximum(logits, 0.0) + jnp.log1p(jnp.exp(-jnp.abs(logits)))
    step_ref[...] = step
    sig_ref[...] = jax.nn.sigmoid(logits)
    falls = -rate * step
    shape = (STRETCH, STRETCH)
    tri = jnp.where(iota(shape, 0) <= iota(shape, 1), 1.0, 0.0)
    lane = iota((OWN_HEADS, LANES), 1)
    gains = jnp.zeros((OWN_HEADS, LANES), F32)
    for k in range(2):
        span = slice(k * STRETCH, (k + 1) * STRETCH)
        cum = lax.dot_general(
            falls[:, span],
            tri,
            (((1,), (0,)), ((), ())),
            precision=lax.Precision.HIGHEST,
            preferred_element_type=F32,
        )
        end = cum[:, STRETCH - 1 :]
        own_last = jnp.where(labels[:, span] == lasts[k], 1.0, 0.0)
        own_first = jnp.where(labels[:, span] == befores[k], 1.0, 0.0)
        carried = jnp.where(lasts[k] == befores[k], 1.0, 0.0)
        values = (
            step[:, span],
            cum,
            jnp.exp(end - cum) * own_last,
            jnp.exp(cum) * own_first,
        )
        whole = jnp.exp(end) * carried
        gains = gains + jnp.where(lane == k, whole, 0.0)
        for i in range(PAIRS):
            for at, value in enumerate(values):
                rows_ref[i, 2 * at : 2 * at + 2, span] = value[2 * i : 2 * i + 2]
    gain_ref[...] = gains

    @pl.when(context > 0)
    def _():
        passed.wait_recv()

    @pl.when(context < contexts - 1)
    def _():
        passed.wait_send()

    over_blocks(lambda s, t: copies(s, t).wait_send())


def route_in(d_row, q_row, x_rows, b_rows, c_rows, dt_rows, bias, rate, lengths):
    slots = OWNERS * DEPTH * BLK
    return pl.pallas_call(
        route_in_kernel,
        in_specs=[pl.BlockSpec(memory_space=pltpu.VMEM)] * 8
        + [pl.BlockSpec(memory_space=pltpu.SMEM)],
        out_specs=[pl.BlockSpec(memory_space=pltpu.VMEM)] * 8,
        out_shape=[
            jax.ShapeDtypeStruct((ROWS, COLS), BF16),
            jax.ShapeDtypeStruct((8, COLS), BF16),
            jax.ShapeDtypeStruct((PAIRS, 8, ROWS), F32),
            jax.ShapeDtypeStruct((OWN_HEADS, ROWS), F32),
            jax.ShapeDtypeStruct((OWN_HEADS, ROWS), F32),
            jax.ShapeDtypeStruct((OWN_HEADS, LANES), F32),
            jax.ShapeDtypeStruct((ROWS + 16, LANES), jnp.int32),
            jax.ShapeDtypeStruct((8, ROWS), jnp.int32),
        ],
        scratch_shapes=[
            pltpu.VMEM((WAYS, slots, COLS), BF16),
            pltpu.VMEM((WAYS, slots, COLS), BF16),
            pltpu.SemaphoreType.DMA((WAYS, OWNERS)),
            pltpu.SemaphoreType.DMA((WAYS, OWNERS)),
            pltpu.SemaphoreType.DMA,
            pltpu.SemaphoreType.DMA,
            pltpu.SemaphoreType.DMA,
        ],
        compiler_params=pltpu.CompilerParams(collective_id=1, has_side_effects=True),
        name="route_in",
    )(d_row, q_row, x_rows, b_rows, c_rows, dt_rows, bias, rate, lengths)


def route_out_kernel(
    q_ref,
    d_ref,
    dx_ref,
    db_ref,
    dc_ref,
    ddt_ref,
    tail_ref,
    front_ref,
    sums_ref,
    x_ref,
    b_ref,
    c_ref,
    dt_ref,
    xt_ref,
    bct_ref,
    xb_ref,
    bcb_ref,
    heads_ref,
    total_ref,
    stage_ref,
    land_ref,
    held_ref,
    part_ref,
    send,
    recv,
    send1,
    recv1,
    send2,
    recv2,
    own,
    back_ref,
    send3,
    recv3,
):
    head = lax.axis_index("head")
    owner = lax.axis_index("dp") * lax.axis_size("ctx") + lax.axis_index("ctx")
    barrier = pltpu.get_barrier_semaphore()
    greet_all(barrier, owner, head)
    rows = ROWS // WAYS
    slots = OWNERS * DEPTH * BLK
    copies = functools.partial(block_copy, stage_ref, land_ref, send, recv, owner, head)

    def sum_copy(t):
        slot = lax.rem(owner + t, OWNERS)
        return pltpu.make_async_remote_copy(
            src_ref=sums_ref.at[slot],
            dst_ref=held_ref.at[owner],
            send_sem=send1.at[t],
            recv_sem=recv1.at[t],
            device_id=device_of(slot, head),
            device_id_type=pl.DeviceIdType.MESH,
        )

    def total_copy(t):
        return pltpu.make_async_remote_copy(
            src_ref=part_ref,
            dst_ref=total_ref.at[owner],
            send_sem=send2.at[t],
            recv_sem=recv2.at[t],
            device_id=device_of(lax.rem(owner + t, OWNERS), head),
            device_id_type=pl.DeviceIdType.MESH,
        )

    context = lax.axis_index("ctx")
    contexts = lax.axis_size("ctx")
    passed = pltpu.make_async_remote_copy(
        src_ref=front_ref,
        dst_ref=back_ref,
        send_sem=send3,
        recv_sem=recv3,
        device_id=(lax.axis_index("dp"), lax.rem(context + contexts - 1, contexts), head),
        device_id_type=pl.DeviceIdType.MESH,
    )
    for way in range(WAYS):
        here = slice(way * rows, (way + 1) * rows)
        spread = one_hot(iota((slots, rows), 0) == q_ref[way])
        if way == WAYS - 1:

            @pl.when(context < contexts - 1)
            def _():
                passed.wait_recv()

            @pl.when(context == contexts - 1)
            def _():
                back_ref[...] = jnp.zeros_like(back_ref)

        def one(ref, low, high):
            fixed = ref[here, :]
            if way == WAYS - 1:
                whole = fixed.astype(F32)
                tail = tail_ref[:, low:high] + back_ref[:, low:high]
                fixed = jnp.concatenate([whole[: rows - 8], tail]).astype(BF16)
            stage_ref[way, :, low:high] = dot(spread, fixed).astype(BF16)

        one(dx_ref, 0, XCOLS)
        one(db_ref, XCOLS, XCOLS + BCOLS)
        one(dc_ref, XCOLS + BCOLS, CMAIN)
        stage_ref[way, :, CMAIN:] = dot(spread, ddt_ref[here, :]).astype(BF16)
        if way == 0:
            pl.semaphore_wait(barrier, WAYS * OWNERS - 1)

            @pl.when(context > 0)
            def _():
                passed.start()

            over_slots(lambda t: sum_copy(t).start())
    over_blocks(lambda s, t: copies(s, t).start())
    kept = pltpu.make_async_copy(
        stage_ref.at[head, slot_rows(owner), :], land_ref.at[head, slot_rows(owner), :], own
    )
    kept.start()
    kept.wait()
    held_ref[owner] = sums_ref[owner]
    over_slots(lambda t: sum_copy(t).wait_recv())
    total = jnp.sum(held_ref[...], axis=0)
    part_ref[...] = total
    total_ref[owner] = total
    over_slots(lambda t: total_copy(t).start())
    rows = d_ref.shape[0]
    pick = one_hot(iota((rows, slots), 1) == d_ref[...])
    times = jnp.zeros((rows, HEADS), F32)
    over_blocks(lambda s, t: copies(s, t).wait_recv())
    for s in range(WAYS):
        way = lax.rem(head + WAYS - s, WAYS)

        def columns(size):
            return pl.ds(pl.multiple_of(way * size, size), size)

        x_ref[:, columns(XCOLS)] = dot(pick, land_ref[way, :, :XCOLS]).astype(BF16)
        b_ref[:, columns(BCOLS)] = dot(pick, land_ref[way, :, XCOLS : XCOLS + BCOLS]).astype(BF16)
        c_ref[:, columns(BCOLS)] = dot(pick, land_ref[way, :, XCOLS + BCOLS : CMAIN]).astype(BF16)
        lane = iota((LANES, LANES), 0)
        put = one_hot(
            (iota((LANES, LANES), 1) == way * OWN_HEADS + lane) & (lane < OWN_HEADS)
        )
        times += dot(dot(pick, land_ref[way, :, CMAIN:]).astype(BF16), put)
    dt_ref[...] = times.astype(BF16)
    over_slots(lambda t: total_copy(t).wait_recv())
    for i in range(PAIRS):
        lanes = slice(i * LANES, (i + 1) * LANES)
        xt_ref[:, lanes] = total_ref[i, 0:KERNEL, :]
        xb_ref[:, lanes] = total_ref[i, KERNEL : KERNEL + 1, :]
    for side in range(2):
        for g in range(BCOLS // LANES):
            lanes = slice(g * LANES, (g + 1) * LANES)
            at = (XCOLS + side * BCOLS) // LANES + g
            bct_ref[side, :, lanes] = total_ref[at, 0:KERNEL, :]
            bcb_ref[side : side + 1, lanes] = total_ref[at, KERNEL : KERNEL + 1, :]
    heads_ref[...] = total_ref[CMAIN // LANES, 0:3, 0:OWN_HEADS]
    over_slots(lambda t: sum_copy(t).wait_send())
    over_slots(lambda t: total_copy(t).wait_send())

    @pl.when(context > 0)
    def _():
        passed.wait_send()

    over_blocks(lambda s, t: copies(s, t).wait_send())


def route_out(q_row, d_col, dx, db, dc, ddt, tails, fronts, sums):
    slots = OWNERS * DEPTH * BLK
    rows = d_col.shape[0]
    space = pl.BlockSpec(memory_space=pltpu.VMEM)
    return pl.pallas_call(
        route_out_kernel,
        in_specs=[space] * 9,
        out_specs=[space] * 9,
        out_shape=[
            jax.ShapeDtypeStruct((rows, WAYS * XCOLS), BF16),
            jax.ShapeDtypeStruct((rows, WAYS * BCOLS), BF16),
            jax.ShapeDtypeStruct((rows, WAYS * BCOLS), BF16),
            jax.ShapeDtypeStruct((rows, HEADS), BF16),
            jax.ShapeDtypeStruct((KERNEL, XCOLS), F32),
            jax.ShapeDtypeStruct((2, KERNEL, BCOLS), F32),
            jax.ShapeDtypeStruct((1, XCOLS), F32),
            jax.ShapeDtypeStruct((2, BCOLS), F32),
            jax.ShapeDtypeStruct((3, OWN_HEADS), F32),
        ],
        scratch_shapes=[
            pltpu.VMEM((OWNERS, 8, LANES), F32),
            pltpu.VMEM((WAYS, slots, COLS), BF16),
            pltpu.VMEM((WAYS, slots, COLS), BF16),
            pltpu.VMEM((OWNERS, 8, LANES), F32),
            pltpu.VMEM((8, LANES), F32),
            pltpu.SemaphoreType.DMA((WAYS, OWNERS)),
            pltpu.SemaphoreType.DMA((WAYS, OWNERS)),
            pltpu.SemaphoreType.DMA((OWNERS,)),
            pltpu.SemaphoreType.DMA((OWNERS,)),
            pltpu.SemaphoreType.DMA((OWNERS,)),
            pltpu.SemaphoreType.DMA((OWNERS,)),
            pltpu.SemaphoreType.DMA,
            pltpu.VMEM((8, CMAIN), F32),
            pltpu.SemaphoreType.DMA,
            pltpu.SemaphoreType.DMA,
        ],
        compiler_params=pltpu.CompilerParams(collective_id=2, has_side_effects=True),
        name="route_out",
    )(q_row, d_col, dx, db, dc, ddt, tails, fronts, sums)


def fill_pad(pad_ref, rows_ref, halo_ref):
    pad_ref[0:8, :] = halo_ref[...].astype(F32)
    pad_ref[8 : 8 + ROWS, :] = rows_ref[...].astype(F32)


def fill_keep(keep_ref, label_ref):
    labels = label_ref[8 : 8 + ROWS, :]
    for k in range(KERNEL - 1):
        same = label_ref[5 + k : 5 + k + ROWS, :] == labels
        keep_ref[k] = jnp.where(same, 1.0, 0.0)


def fill_keeps(keeps_ref, label_ref):
    span = ROWS + 8
    front = label_ref[0:span, :]
    for k in range(KERNEL - 1):
        same = label_ref[3 - k : 3 - k + span, :] == front
        keeps_ref[k] = jnp.where(same & (front >= 0), 1.0, 0.0)


def conv_sum(pad_ref, taps, bias, keep_ref):
    total = bias + taps[0:1] * pad_ref[5 : 5 + ROWS, :] * keep_ref[0]
    total = total + taps[1:2] * pad_ref[6 : 6 + ROWS, :] * keep_ref[1]
    total = total + taps[2:3] * pad_ref[7 : 7 + ROWS, :] * keep_ref[2]
    return total + taps[3:4] * pad_ref[8 : 8 + ROWS, :]


def conv_value(pad_ref, rows_ref, halo_ref, taps, bias, keep_ref):
    fill_pad(pad_ref, rows_ref, halo_ref)
    total = conv_sum(pad_ref, taps, bias, keep_ref)
    return (total * jax.nn.sigmoid(total)).astype(BF16)


def conv_back(pad_ref, dpad_ref, rows_ref, halo_ref, taps, bias, keep_ref, keeps_ref, grad):
    fill_pad(pad_ref, rows_ref, halo_ref)
    total = conv_sum(pad_ref, taps, bias, keep_ref)
    sig = jax.nn.sigmoid(total)
    dpre = grad * (sig * (1.0 + total * (1.0 - sig)))
    dpad_ref[8 : 8 + ROWS, :] = dpre
    sums = []
    for k in range(KERNEL):
        value = dpre * pad_ref[5 + k : 5 + k + ROWS, :]
        if k < KERNEL - 1:
            value = value * keep_ref[k]
        sums.append(jnp.sum(value, axis=0, keepdims=True))
    sums.append(jnp.sum(dpre, axis=0, keepdims=True))
    sums.append(jnp.zeros((3, LANES), F32))
    span = ROWS + 8
    moved = taps[3:4] * dpad_ref[0:span, :]
    for k in range(KERNEL - 1):
        moved = moved + taps[k : k + 1] * (keeps_ref[k] * dpad_ref[3 - k : 3 - k + span, :])
    return moved, jnp.concatenate(sums)


def pair_rows(first, second, count=HEAD_DIM):
    width = first.shape[1]
    return jnp.concatenate(
        [jnp.broadcast_to(first, (count, width)), jnp.broadcast_to(second, (count, width))]
    )


def pair_scale(first, second, shape):
    return jnp.where(iota(shape, 0) < HEAD_DIM, first, second)


def first_kernel(
    gs_ref,
    rows_ref,
    x_ref,
    b_ref,
    c_ref,
    hx_ref,
    hb_ref,
    hc_ref,
    xt_ref,
    xb_ref,
    bt_ref,
    bb_ref,
    ct_ref,
    cb_ref,
    label_ref,
    og_ref,
    ep_ref,
    xT_ref,
    gT_ref,
    bn_ref,
    cn_ref,
    e0_ref,
    t1_ref,
    pad_ref,
    keep_ref,
):
    i = pl.program_id(0)

    @pl.when(i == 0)
    def _():
        fill_keep(keep_ref, label_ref)

    @pl.when(i % GROUP_PAIRS == 0)
    def _():
        bn_ref[...] = conv_value(pad_ref, b_ref, hb_ref, bt_ref[0], bb_ref[0:1], keep_ref)
        cn_ref[...] = conv_value(pad_ref, c_ref, hc_ref, ct_ref[0], cb_ref[1:2], keep_ref)

    unit = eye(LANES)
    xc = conv_value(pad_ref, x_ref, hx_ref, xt_ref[...], xb_ref[...], keep_ref)
    x_all = dot_nt(unit, xc)
    g_all = dot_nt(unit, og_ref[...])
    xT_ref[...] = x_all.astype(BF16)
    gT_ref[...] = g_all.astype(BF16)
    rows = rows_ref[0]
    states = []
    touched = []
    for k in range(2):
        span = slice(k * STRETCH, (k + 1) * STRETCH)
        coef = pair_rows(rows[0:1, span] * rows[4:5, span], rows[1:2, span] * rows[5:6, span])
        gain = pair_rows(rows[6:7, span], rows[7:8, span])
        states.append(dot((coef * x_all[:, span]).astype(BF16), bn_ref[span, :]))
        touched.append(dot((gain * g_all[:, span]).astype(BF16), cn_ref[span, :]))
    shape = (LANES, STATE)
    ga0, ga1 = gs_ref[2 * i, 0], gs_ref[2 * i, 1]
    gb0, gb1 = gs_ref[2 * i + 1, 0], gs_ref[2 * i + 1, 1]
    ep_ref[0, 0:LANES, :] = (pair_scale(ga1, gb1, shape) * states[0] + states[1]).astype(BF16)
    ep_ref[0, LANES : 2 * LANES, :] = (
        touched[0] + pair_scale(ga0, gb0, shape) * touched[1]
    ).astype(BF16)
    lane = iota((EXTRA, LANES), 1)
    whole = jnp.where(lane < HEAD_DIM, ga0 * ga1, gb0 * gb1)
    high = whole.astype(BF16).astype(F32)
    low = whole - high
    ep_ref[0, 2 * LANES :, :] = jnp.where(iota((EXTRA, LANES), 0) < 8, high, low).astype(BF16)
    e0_ref[...] = states[0]
    t1_ref[...] = touched[1]


def conv_specs():
    group = lambda i: i // GROUP_PAIRS
    base_b = XCOLS // LANES
    base_c = base_b + BCOLS // LANES
    return [
        pl.BlockSpec((ROWS, LANES), lambda i: (0, i)),
        pl.BlockSpec((ROWS, LANES), lambda i: (0, base_b + group(i))),
        pl.BlockSpec((ROWS, LANES), lambda i: (0, base_c + group(i))),
        pl.BlockSpec((8, LANES), lambda i: (0, i)),
        pl.BlockSpec((8, LANES), lambda i: (0, base_b + group(i))),
        pl.BlockSpec((8, LANES), lambda i: (0, base_c + group(i))),
        pl.BlockSpec((KERNEL, LANES), lambda i: (0, i)),
        pl.BlockSpec((1, LANES), lambda i: (0, i)),
        pl.BlockSpec((1, KERNEL, LANES), lambda i: (0, 0, group(i))),
        pl.BlockSpec((2, LANES), lambda i: (0, group(i))),
        pl.BlockSpec((1, KERNEL, LANES), lambda i: (1, 0, group(i))),
        pl.BlockSpec((2, LANES), lambda i: (0, group(i))),
        pl.BlockSpec((ROWS + 16, LANES), lambda i: (0, 0)),
    ]


def first_pass(gs, rows, conv_args, out_grad):
    wide = lambda i: (i, 0)
    group = lambda i: (0, i // GROUP_PAIRS)
    return pl.pallas_call(
        first_kernel,
        grid=(PAIRS,),
        in_specs=[
            pl.BlockSpec(memory_space=pltpu.SMEM),
            pl.BlockSpec((1, 8, ROWS), lambda i: (i, 0, 0)),
        ]
        + conv_specs()
        + [pl.BlockSpec((ROWS, LANES), lambda i: (0, i))],
        out_specs=[
            pl.BlockSpec((1, 2 * LANES + EXTRA, STATE), lambda i: (i, 0, 0)),
            pl.BlockSpec((LANES, ROWS), wide),
            pl.BlockSpec((LANES, ROWS), wide),
            pl.BlockSpec((ROWS, LANES), group),
            pl.BlockSpec((ROWS, LANES), group),
            pl.BlockSpec((LANES, STATE), wide),
            pl.BlockSpec((LANES, STATE), wide),
        ],
        out_shape=[
            jax.ShapeDtypeStruct((PAIRS, 2 * LANES + EXTRA, STATE), BF16),
            jax.ShapeDtypeStruct((XCOLS, ROWS), BF16),
            jax.ShapeDtypeStruct((XCOLS, ROWS), BF16),
            jax.ShapeDtypeStruct((ROWS, BCOLS), BF16),
            jax.ShapeDtypeStruct((ROWS, BCOLS), BF16),
            jax.ShapeDtypeStruct((XCOLS, STATE), F32),
            jax.ShapeDtypeStruct((XCOLS, STATE), F32),
        ],
        scratch_shapes=[
            pltpu.VMEM((ROWS + 16, LANES), F32),
            pltpu.VMEM((KERNEL - 1, ROWS, LANES), F32),
        ],
        name="first_pass",
    )(gs, rows, *conv_args, out_grad)


def gain_row(ref, at, pair):
    extra = ref[at, pair, 2 * LANES :, :].astype(F32)
    return extra[0:1] + extra[8:9]


def gain_scale(row):
    return pair_scale(row[:, 0:1], row[:, HEAD_DIM : HEAD_DIM + 1], (LANES, STATE))


ENTER = slice(0, LANES)
LEAVE = slice(LANES, 2 * LANES)


def state_kernel(
    chips, in_ref, out_ref, near_ref, join_ref, land_ref, part_ref, got_ref, give_ref, send, recv
):
    me = lax.axis_index("ctx")
    dp, head = lax.axis_index("dp"), lax.axis_index("head")
    chip, side = me // 2, lax.rem(me, 2)
    partner = me + 1 - 2 * side
    pairs = in_ref.shape[1]

    def place(context):
        return dict(
            device_id=(dp, context, head), device_id_type=pl.DeviceIdType.MESH
        )

    def chip_at(d):
        return lax.rem(chip + d, chips)

    barrier = pltpu.get_barrier_semaphore()
    pl.semaphore_signal(barrier, inc=1, **place(partner))
    for d in range(1, chips):
        pl.semaphore_signal(barrier, inc=1, **place(2 * chip_at(d) + side))
    pl.semaphore_wait(barrier, chips)

    def copy(source, target, stage, d, context):
        return pltpu.make_async_remote_copy(
            src_ref=source,
            dst_ref=target,
            send_sem=send.at[stage, d],
            recv_sem=recv.at[stage, d],
            **place(context),
        )

    def shared(y):
        return copy(in_ref.at[2 * y + 1 - side], near_ref.at[y], 0, y, partner)

    for y in range(chips):
        shared(y).start()
    for y in range(chips):
        shared(y).wait()

    def both(y, pair, rows):
        own = in_ref[2 * y + side, pair, rows, :].astype(F32)
        other = near_ref[y, pair, rows, :].astype(F32)
        return jnp.where(side == 0, own, other), jnp.where(side == 0, other, own)

    def gain_rows(y, pair):
        own, other = gain_row(in_ref, 2 * y + side, pair), gain_row(near_ref, y, pair)
        return jnp.where(side == 0, own, other), jnp.where(side == 0, other, own)

    def joined(d):
        y = chip_at(d)
        return copy(join_ref.at[y], land_ref.at[chip], 1, d, 2 * y + side)

    for d in list(range(1, chips)) + [0]:
        y = chip_at(d)
        target = join_ref if d else land_ref
        for pair in range(pairs):
            first, second = gain_rows(y, pair)
            e_first, e_second = both(y, pair, ENTER)
            p_first, p_second = both(y, pair, LEAVE)
            target[y, pair, ENTER, :] = (gain_scale(second) * e_first + e_second).astype(BF16)
            target[y, pair, LEAVE, :] = (p_first + gain_scale(first) * p_second).astype(BF16)
            whole = first * second
            high = whole.astype(BF16).astype(F32)
            upper = iota((EXTRA, LANES), 0) < 8
            target[y, pair, 2 * LANES :, :] = jnp.where(upper, high, whole - high).astype(BF16)
        if d:
            joined(d).start()
    for d in range(1, chips):
        joined(d).wait()

    for pair in range(pairs):
        gains = [gain_scale(gain_row(land_ref, at, pair)) for at in range(chips)]
        state = jnp.zeros((LANES, STATE), F32)
        for at in range(chips):
            part_ref[at, pair, ENTER, :] = state.astype(BF16)
            state = gains[at] * state + land_ref[at, pair, ENTER, :].astype(F32)
        state = jnp.zeros((LANES, STATE), F32)
        for at in reversed(range(chips)):
            part_ref[at, pair, LEAVE, :] = state.astype(BF16)
            state = land_ref[at, pair, LEAVE, :].astype(F32) + gains[at] * state

    def scanned(d):
        y = chip_at(d)
        return copy(part_ref.at[y], got_ref.at[chip], 2, d, 2 * y + side)

    for d in range(1, chips):
        scanned(d).start()
    got_ref[chip] = part_ref[chip]
    for d in range(1, chips):
        scanned(d).wait()

    def given(y):
        return copy(give_ref.at[y], out_ref.at[2 * y + side], 3, y, partner)

    for y in range(chips):
        for pair in range(pairs):
            first, second = gain_rows(y, pair)
            e_first, _ = both(y, pair, ENTER)
            _, p_second = both(y, pair, LEAVE)
            enter = got_ref[y, pair, ENTER, :].astype(F32)
            leave = got_ref[y, pair, LEAVE, :].astype(F32)
            enter_second = gain_scale(first) * enter + e_first
            leave_first = p_second + gain_scale(second) * leave
            for rows, one, two in ((ENTER, enter, enter_second), (LEAVE, leave_first, leave)):
                out_ref[2 * y + side, pair, rows, :] = jnp.where(side == 0, one, two).astype(BF16)
                give_ref[y, pair, rows, :] = jnp.where(side == 0, two, one).astype(BF16)
        given(y).start()
    for y in range(chips):
        given(y).wait()


def exchange_states(parts):
    count, pairs, tall = parts.shape[:3]
    chips = count // 2
    wide = pltpu.VMEM((chips, pairs, tall, STATE), BF16)
    slim = pltpu.VMEM((chips, pairs, 2 * LANES, STATE), BF16)
    return pl.pallas_call(
        functools.partial(state_kernel, chips),
        in_specs=[pl.BlockSpec(memory_space=pltpu.VMEM)],
        out_specs=pl.BlockSpec(memory_space=pltpu.VMEM),
        out_shape=jax.ShapeDtypeStruct((count, pairs, 2 * LANES, STATE), BF16),
        scratch_shapes=[
            wide,
            wide,
            wide,
            slim,
            slim,
            slim,
            pltpu.SemaphoreType.DMA((4, chips)),
            pltpu.SemaphoreType.DMA((4, chips)),
        ],
        compiler_params=pltpu.CompilerParams(collective_id=0, has_side_effects=True),
        name="exchange_states",
    )(parts)


def main_kernel(
    gs_ref,
    skip_ref,
    rows_ref,
    x_ref,
    b_ref,
    c_ref,
    hx_ref,
    hb_ref,
    hc_ref,
    xt_ref,
    xb_ref,
    bt_ref,
    bb_ref,
    ct_ref,
    cb_ref,
    label_ref,
    og_ref,
    xT_ref,
    gT_ref,
    bn_ref,
    cn_ref,
    ent_ref,
    e0_ref,
    t1_ref,
    labr_ref,
    step_ref,
    sig_ref,
    rate_ref,
    y_ref,
    dx_ref,
    db_ref,
    dc_ref,
    ddt_ref,
    tail_ref,
    front_ref,
    sums_ref,
    dcum_ref,
    dstep_ref,
    dskip_ref,
    mask_ref,
    score_ref,
    dscore_ref,
    bT_ref,
    cT_ref,
    dbT_ref,
    dcT_ref,
    pad_ref,
    dpad_ref,
    dxn_ref,
    keep_ref,
    keeps_ref,
):
    i = pl.program_id(0)
    unit = eye(LANES)
    wide_unit = eye(STRETCH)
    spans = [slice(k * STRETCH, (k + 1) * STRETCH) for k in range(2)]

    @pl.when(i == 0)
    def _():
        fill_keep(keep_ref, label_ref)
        fill_keeps(keeps_ref, label_ref)
        dpad_ref[...] = jnp.zeros_like(dpad_ref)
        sums_ref[...] = jnp.zeros_like(sums_ref)
        dcum_ref[...] = jnp.zeros_like(dcum_ref)
        dstep_ref[...] = jnp.zeros_like(dstep_ref)
        dskip_ref[...] = jnp.zeros_like(dskip_ref)
        for k in range(2):
            for t in range(2):
                shape = (STRETCH, LANES)
                left = k * STRETCH + t * LANES
                low = 8 + k * STRETCH
                same = label_ref[low : low + STRETCH, :] == labr_ref[0:1, left : left + LANES]
                lower = iota(shape, 0) >= iota(shape, 1) + t * LANES
                mask_ref[k, :, t * LANES : (t + 1) * LANES] = jnp.where(same & lower, 0.0, NEG)

    @pl.when(i % GROUP_PAIRS == 0)
    def _():
        bT_ref[...] = dot_nt(unit, bn_ref[...]).astype(BF16)
        cT_ref[...] = dot_nt(unit, cn_ref[...]).astype(BF16)
        dbT_ref[...] = jnp.zeros_like(dbT_ref)
        dcT_ref[...] = jnp.zeros_like(dcT_ref)
        dscore_ref[...] = jnp.zeros_like(dscore_ref)
        for k in range(2):
            score_ref[k] = dot_nt(cn_ref[spans[k], :], bn_ref[spans[k], :])

    rows = rows_ref[0]
    columns = jnp.transpose(rows)
    shape = (LANES, STATE)
    gains = [
        (gs_ref[2 * i, k], gs_ref[2 * i + 1, k]) for k in range(2)
    ]
    skip = pair_scale(skip_ref[2 * i], skip_ref[2 * i + 1], (LANES, STRETCH))
    enter0 = ent_ref[0, 0:LANES, :].astype(F32)
    leave1 = ent_ref[0, LANES : 2 * LANES, :].astype(F32)
    enter1 = pair_scale(*gains[0], shape) * enter0 + e0_ref[...]
    leave0 = t1_ref[...] + pair_scale(*gains[1], shape) * leave1
    enters = (enter0, enter1)
    leaves = (leave0, leave1)
    seat = iota((OWN_HEADS, STRETCH), 0)
    for k in range(2):
        span = spans[k]
        x = xT_ref[:, span].astype(F32)
        g_low = gT_ref[:, span]
        g = g_low.astype(F32)
        og = og_ref[span, :]
        step = pair_rows(rows[0:1, span], rows[1:2, span])
        ends = (rows[4:5, span], rows[5:6, span])
        coefs = (rows[0:1, span] * ends[0], rows[1:2, span] * ends[1])
        coef = pair_rows(*coefs)
        gain = pair_rows(rows[6:7, span], rows[7:8, span])
        xs = (step * x).astype(BF16)
        weighted = (coef * x).astype(BF16)
        nothing = jnp.zeros((HEAD_DIM, STRETCH), BF16)
        inner = []
        dxs = []
        for h in range(2):
            part = slice(h * HEAD_DIM, (h + 1) * HEAD_DIM)
            gap = columns[span, 2 + h : 3 + h] - rows[2 + h : 3 + h, span]
            decay = jnp.exp(gap + mask_ref[k])
            mix = (score_ref[k] * decay).astype(BF16)
            own = (xs[part], nothing) if h == 0 else (nothing, xs[part])
            dmix = dot(og, jnp.concatenate(own))
            dscore_ref[k] += dmix * decay
            inner.append(dot_nt(xs[part], mix))
            dxs.append(dot(g_low[part], mix))
        inner = jnp.concatenate(inner)
        dxs = jnp.concatenate(dxs)
        enter = enters[k].astype(BF16)
        leave = leaves[k].astype(BF16)
        carried = gain * dot_nt(enter, cn_ref[span, :])
        y = inner + carried + skip * x
        y_ref[span, :] = dot_nt(wide_unit, y.astype(BF16)).astype(BF16)
        enter_t = dot_nt(unit, enter).astype(BF16)
        leave_t = dot_nt(unit, leave).astype(BF16)
        dcT_ref[:, span] += dot(enter_t, (gain * g).astype(BF16))
        dbT_ref[:, span] += dot(leave_t, weighted)
        dweighted = dot_nt(leave, bn_ref[span, :])
        dx = step * dxs + coef * dweighted + skip * g
        dxn_ref[span, :] = dot_nt(wide_unit, dx.astype(BF16))
        moved = dweighted * x
        direct = dxs * x
        cums = g * (inner + carried) - xs.astype(F32) * dxs
        skipped = g * x
        turned = leaves[k] * enters[k]
        last = iota((1, STRETCH), 1) == STRETCH - 1
        for h in range(2):
            part = slice(h * HEAD_DIM, (h + 1) * HEAD_DIM)
            pulled = jnp.sum(moved[part], axis=0, keepdims=True)
            ended = coefs[h] * pulled
            total = jnp.sum(ended, axis=1, keepdims=True)
            bend = jnp.sum(
                jnp.sum(turned[part], axis=0, keepdims=True), axis=1, keepdims=True
            )
            dcum = jnp.sum(cums[part], axis=0, keepdims=True) - ended
            dcum = dcum + jnp.where(last, total + gains[k][h] * bend, 0.0)
            dstep = jnp.sum(direct[part], axis=0, keepdims=True) + ends[h] * pulled
            dskip = jnp.sum(skipped[part], axis=0, keepdims=True)
            here = seat == 2 * i + h
            dcum_ref[:, span] += jnp.where(here, dcum, 0.0)
            dstep_ref[:, span] += jnp.where(here, dstep, 0.0)
            dskip_ref[:, span] += jnp.where(here, dskip, 0.0)

    moved, sums = conv_back(
        pad_ref, dpad_ref, x_ref, hx_ref, xt_ref[...], xb_ref[...], keep_ref, keeps_ref, dxn_ref[...]
    )
    lanes = pl.ds(pl.multiple_of(i * LANES, LANES), LANES)
    front_ref[:, lanes] = moved[0:8]
    tail_ref[:, lanes] = moved[ROWS:]
    dx_ref[...] = moved[8:].astype(BF16)
    sums_ref[i] = sums

    @pl.when(i % GROUP_PAIRS == GROUP_PAIRS - 1)
    def _():
        for k in range(2):
            span = spans[k]
            dscore = dscore_ref[k].astype(BF16)
            dcT = dcT_ref[:, span] + dot_nt(bT_ref[:, span], dscore)
            dbT = dbT_ref[:, span] + dot(cT_ref[:, span], dscore)
            dcT_ref[:, span] = dcT
            dbT_ref[:, span] = dbT
        sides = (
            (dbT_ref, b_ref, hb_ref, bt_ref, bb_ref[0:1], db_ref, XCOLS),
            (dcT_ref, c_ref, hc_ref, ct_ref, cb_ref[1:2], dc_ref, XCOLS + BCOLS),
        )
        for grad_ref, in_ref, halo_ref, tap_ref, bias, out_ref, left in sides:
            for span in spans:
                dxn_ref[span, :] = dot_nt(wide_unit, grad_ref[:, span].astype(BF16))
            moved, sums = conv_back(
                pad_ref,
                dpad_ref,
                in_ref,
                halo_ref,
                tap_ref[0],
                bias,
                keep_ref,
                keeps_ref,
                dxn_ref[...],
            )
            at = pl.multiple_of(left + (i // GROUP_PAIRS) * LANES, LANES)
            front_ref[:, pl.ds(at, LANES)] = moved[0:8]
            tail_ref[:, pl.ds(at, LANES)] = moved[ROWS:]
            out_ref[...] = moved[8:].astype(BF16)
            sums_ref[left // LANES + i // GROUP_PAIRS] = sums

    @pl.when(i == PAIRS - 1)
    def _():
        shape = (STRETCH, STRETCH)
        tri = jnp.where(iota(shape, 0) >= iota(shape, 1), 1.0, 0.0)
        rate = as_column(rate_ref[...])
        bias_sum = jnp.zeros((OWN_HEADS, 1), F32)
        rate_sum = jnp.zeros((OWN_HEADS, 1), F32)
        for span in spans:
            after = lax.dot_general(
                dcum_ref[:, span],
                tri,
                (((1,), (0,)), ((), ())),
                precision=lax.Precision.HIGHEST,
                preferred_element_type=F32,
            )
            dlogit = (dstep_ref[:, span] - rate * after) * sig_ref[:, span]
            bias_sum += jnp.sum(dlogit, axis=1, keepdims=True)
            rate_sum -= jnp.sum(after * step_ref[:, span], axis=1, keepdims=True)
            tall = jnp.concatenate([dlogit, jnp.zeros((LANES - OWN_HEADS, STRETCH), F32)])
            ddt_ref[span, :] = dot_nt(wide_unit, tall.astype(BF16)).astype(BF16)
        skip_sum = jnp.sum(dskip_ref[...], axis=1, keepdims=True)
        diagonal = iota((OWN_HEADS, LANES), 0) == iota((OWN_HEADS, LANES), 1)
        lines = [
            jnp.sum(jnp.where(diagonal, value, 0.0), axis=0, keepdims=True)
            for value in (bias_sum, rate_sum, skip_sum)
        ]
        sums_ref[CMAIN // LANES] = jnp.concatenate(lines + [jnp.zeros((5, LANES), F32)])


def main_pass(
    gs, skip, rows, conv_args, out_grad, xT, gT, bn, cn, ent, e0, t1, labr, heads
):
    wide = lambda i: (i, 0)
    col = lambda i: (0, i)
    group = lambda i: (0, i // GROUP_PAIRS)
    triple = lambda i: (i, 0, 0)
    fixed = lambda i: (0, 0)
    square = (2, STRETCH, STRETCH)
    return pl.pallas_call(
        main_kernel,
        grid=(PAIRS,),
        in_specs=[
            pl.BlockSpec(memory_space=pltpu.SMEM),
            pl.BlockSpec(memory_space=pltpu.SMEM),
            pl.BlockSpec((1, 8, ROWS), triple),
        ]
        + conv_specs()
        + [
            pl.BlockSpec((ROWS, LANES), col),
            pl.BlockSpec((LANES, ROWS), wide),
            pl.BlockSpec((LANES, ROWS), wide),
            pl.BlockSpec((ROWS, LANES), group),
            pl.BlockSpec((ROWS, LANES), group),
            pl.BlockSpec((1, 2 * LANES, STATE), triple),
            pl.BlockSpec((LANES, STATE), wide),
            pl.BlockSpec((LANES, STATE), wide),
            pl.BlockSpec((8, ROWS), fixed),
            pl.BlockSpec((OWN_HEADS, ROWS), fixed),
            pl.BlockSpec((OWN_HEADS, ROWS), fixed),
            pl.BlockSpec((1, OWN_HEADS), fixed),
        ],
        out_specs=[
            pl.BlockSpec((ROWS, LANES), col),
            pl.BlockSpec((ROWS, LANES), col),
            pl.BlockSpec((ROWS, LANES), group),
            pl.BlockSpec((ROWS, LANES), group),
            pl.BlockSpec((ROWS, LANES), fixed),
            pl.BlockSpec((8, CMAIN), fixed),
            pl.BlockSpec((8, CMAIN), fixed),
            pl.BlockSpec((OWNERS, 8, LANES), lambda i: (0, 0, 0)),
        ],
        out_shape=[
            jax.ShapeDtypeStruct((ROWS, XCOLS), BF16),
            jax.ShapeDtypeStruct((ROWS, XCOLS), BF16),
            jax.ShapeDtypeStruct((ROWS, BCOLS), BF16),
            jax.ShapeDtypeStruct((ROWS, BCOLS), BF16),
            jax.ShapeDtypeStruct((ROWS, LANES), BF16),
            jax.ShapeDtypeStruct((8, CMAIN), F32),
            jax.ShapeDtypeStruct((8, CMAIN), F32),
            jax.ShapeDtypeStruct((OWNERS, 8, LANES), F32),
        ],
        scratch_shapes=[
            pltpu.VMEM((OWN_HEADS, ROWS), F32),
            pltpu.VMEM((OWN_HEADS, ROWS), F32),
            pltpu.VMEM((OWN_HEADS, ROWS), F32),
            pltpu.VMEM(square, F32),
            pltpu.VMEM(square, F32),
            pltpu.VMEM(square, F32),
            pltpu.VMEM((LANES, ROWS), BF16),
            pltpu.VMEM((LANES, ROWS), BF16),
            pltpu.VMEM((LANES, ROWS), F32),
            pltpu.VMEM((LANES, ROWS), F32),
            pltpu.VMEM((ROWS + 16, LANES), F32),
            pltpu.VMEM((ROWS + 16, LANES), F32),
            pltpu.VMEM((ROWS, LANES), F32),
            pltpu.VMEM((KERNEL - 1, ROWS, LANES), F32),
            pltpu.VMEM((KERNEL - 1, ROWS + 8, LANES), F32),
        ],
        name="main_pass",
    )(gs, skip, rows, *conv_args, out_grad, xT, gT, bn, cn, ent, e0, t1, labr, *heads)


def on_device(
    x_rows,
    b_rows,
    c_rows,
    dt_rows,
    length_plan,
    trace_lengths,
    x_taps,
    bc_taps,
    x_bias,
    bc_bias,
    dt_bias,
    decay_rate,
    skip_gain,
    out_grad,
):
    contexts = lax.axis_size("ctx")
    owner = lax.axis_index("dp") * contexts + lax.axis_index("ctx")
    head_at = lax.axis_index("head")
    owned = LBLOCKS * WAYS
    plan = length_plan.reshape(OWNERS, WAYS, LBLOCKS)
    column = lax.dynamic_index_in_dim(plan, head_at, 1, keepdims=False)
    base = (owner * WAYS + head_at) * LBLOCKS
    blocks = jnp.arange(LBLOCKS, dtype=jnp.int32)
    hits = column.reshape(-1)[:, None] == base + blocks[None, :]
    seats = (jnp.arange(OWNERS * LBLOCKS, dtype=jnp.int32) // LBLOCKS)[:, None]
    target = jnp.sum(jnp.where(hits, seats, 0), axis=0)
    earlier = blocks[None, :] < blocks[:, None]
    rank = jnp.sum(((target[None, :] == target[:, None]) & earlier).astype(jnp.int32), axis=1)
    pairs = jnp.arange(BLK, dtype=jnp.int32)
    goes = (((target * DEPTH + rank) * BLK)[:, None] + pairs[None, :]).reshape(-1)
    mine = lax.dynamic_slice_in_dim(length_plan, owner * owned, owned).reshape(WAYS, LBLOCKS)
    source = mine // owned
    same = source[:, :, None] == source[:, None, :]
    lower = mine[:, None, :] < mine[:, :, None]
    place = jnp.sum((same & lower).astype(jnp.int32), axis=2)
    comes = ((source * DEPTH + place) * BLK)[:, :, None] + pairs
    comes = comes.reshape(WAYS, LBLOCKS * BLK)

    heads_dev = dt_bias.shape[0]
    packed, halo, rows, step, sig, gs, label, labr = route_in(
        goes[None, :],
        comes[:, None, :],
        x_rows,
        b_rows,
        c_rows,
        dt_rows,
        dt_bias[None, :],
        decay_rate[None, :],
        trace_lengths,
    )

    conv_args = (
        packed,
        packed,
        packed,
        halo,
        halo,
        halo,
        x_taps,
        x_bias[None, :],
        bc_taps,
        bc_bias,
        bc_taps,
        bc_bias,
        label,
    )
    ep, xT, gT, bn, cn, e0, t1 = first_pass(gs, rows, conv_args, out_grad)

    per = PAIRS // contexts
    tall = 2 * LANES + EXTRA
    ent = exchange_states(ep.reshape(contexts, per, tall, STATE))
    ent = ent.reshape(PAIRS, 2 * LANES, STATE)

    heads = (step, sig, decay_rate[None, :])
    y, dx, db, dc, ddt, tails, fronts, sums = main_pass(
        gs,
        skip_gain,
        rows,
        conv_args,
        out_grad,
        xT,
        gT,
        bn,
        cn,
        ent,
        e0,
        t1,
        labr,
        heads,
    )
    x_grad, b_grad, c_grad, dt_grad, xt_grad, bct_grad, xb_grad, bcb_grad, heads_grad = route_out(
        comes[:, None, :], goes[:, None], dx, db, dc, ddt, tails, fronts, sums
    )
    return (
        y,
        x_grad,
        b_grad,
        c_grad,
        dt_grad,
        xt_grad,
        bct_grad,
        xb_grad.reshape(-1),
        bcb_grad,
        heads_grad[0],
        heads_grad[1],
        heads_grad[2],
    )


def solution(mesh):
    rows = P(("dp", "ctx", "head"), None)
    return jax.shard_map(
        on_device,
        mesh=mesh,
        in_specs=(
            rows,
            rows,
            rows,
            rows,
            P(),
            P("dp", None),
            P(None, "head"),
            P(None, None, "head"),
            P("head"),
            P(None, "head"),
            P("head"),
            P("head"),
            P("head"),
            P(("dp", "ctx"), "head"),
        ),
        out_specs=(
            P(("dp", "ctx"), "head"),
            rows,
            rows,
            rows,
            rows,
            P(None, "head"),
            P(None, None, "head"),
            P("head"),
            P(None, "head"),
            P("head"),
            P("head"),
            P("head"),
        ),
        check_vma=False,
    )
```

```python
import functools

import jax
import jax.numpy as jnp
from jax import lax
from jax.experimental import pallas as pl
from jax.experimental.pallas import tpu as pltpu
from jax.sharding import PartitionSpec as P

HEADS = 128
HEAD_DIM = 64
GROUPS = 8
STATE = 128
KERNEL = 4
STRETCH = 256
BLK = 2
LANES = 128
OWNERS = 32
WAYS = 4
LBLOCKS = 64
DEPTH = 4
ROWS = 512
XCOLS = 2048
BCOLS = 256
COLS = XCOLS + 2 * BCOLS + LANES
PAIRS = 16
GROUP_PAIRS = 8
EXTRA = 16
CMAIN = XCOLS + 2 * BCOLS
OWN_HEADS = HEADS // WAYS
NEG = -1e30
STRIDE = 11

F32 = jnp.float32
BF16 = jnp.bfloat16


def dot(left, right):
    return lax.dot_general(left, right, (((1,), (0,)), ((), ())), preferred_element_type=F32)


def dot_nt(left, right):
    return lax.dot_general(left, right, (((1,), (1,)), ((), ())), preferred_element_type=F32)


def iota(shape, dim):
    return lax.broadcasted_iota(jnp.int32, shape, dim)


def one_hot(condition):
    return jnp.where(condition, 1.0, 0.0).astype(BF16)


def eye(size):
    return one_hot(iota((size, size), 0) == iota((size, size), 1))


def device_of(slot, head):
    contexts = lax.axis_size("ctx")
    return (slot // contexts, lax.rem(slot, contexts), head)


def greet_all(barrier, owner, head):
    for s in range(WAYS):
        way = lax.rem(head + s, WAYS)

        def greet(t, carry, way=way):
            pl.semaphore_signal(
                barrier,
                inc=1,
                device_id=device_of(lax.rem(owner + t, OWNERS), way),
                device_id_type=pl.DeviceIdType.MESH,
            )
            return carry

        lax.fori_loop(0 if s else 1, OWNERS, greet, 0)


def slot_rows(at):
    return pl.ds(pl.multiple_of(at * DEPTH * BLK, DEPTH * BLK), DEPTH * BLK)


def block_copy(stage_ref, land_ref, send, recv, owner, head, s, t):
    way = lax.rem(head + s, WAYS)
    slot = lax.rem(owner + t, OWNERS)
    return pltpu.make_async_remote_copy(
        src_ref=stage_ref.at[way, slot_rows(slot), :],
        dst_ref=land_ref.at[head, slot_rows(owner), :],
        send_sem=send.at[s, t],
        recv_sem=recv.at[s, t],
        device_id=device_of(slot, way),
        device_id_type=pl.DeviceIdType.MESH,
    )


def over_slots(act):
    def body(t, carry):
        act(t)
        return carry

    lax.fori_loop(1, OWNERS, body, 0)


def over_blocks(act):
    count = WAYS * OWNERS

    def body(m, carry):
        at = lax.rem(m * STRIDE, count)
        act(lax.rem(at, WAYS), at // WAYS)
        return carry

    lax.fori_loop(1, count, body, 0)


def as_column(row):
    size = row.shape[1]
    diagonal = iota((size, size), 0) == iota((size, size), 1)
    return jnp.sum(jnp.where(diagonal, row, 0.0), axis=1, keepdims=True)


def route_in_kernel(
    d_ref,
    q_ref,
    x_ref,
    b_ref,
    c_ref,
    dt_ref,
    bias_ref,
    rate_ref,
    lengths_ref,
    out_ref,
    halo_ref,
    rows_ref,
    step_ref,
    sig_ref,
    gain_ref,
    label_ref,
    labr_ref,
    stage_ref,
    land_ref,
    send,
    recv,
    own,
    send_halo,
    recv_halo,
):
    head = lax.axis_index("head")
    owner = lax.axis_index("dp") * lax.axis_size("ctx") + lax.axis_index("ctx")
    barrier = pltpu.get_barrier_semaphore()
    greet_all(barrier, owner, head)
    rows = x_ref.shape[0]
    slots = OWNERS * DEPTH * BLK
    spread = one_hot(iota((slots, rows), 0) == d_ref[...])
    copies = functools.partial(block_copy, stage_ref, land_ref, send, recv, owner, head)
    for s in range(WAYS):
        way = lax.rem(head + s, WAYS)

        def columns(size):
            return pl.ds(pl.multiple_of(way * size, size), size)

        stage_ref[way, :, :XCOLS] = dot(spread, x_ref[:, columns(XCOLS)]).astype(BF16)
        stage_ref[way, :, XCOLS : XCOLS + BCOLS] = dot(spread, b_ref[:, columns(BCOLS)]).astype(
            BF16
        )
        stage_ref[way, :, XCOLS + BCOLS : CMAIN] = dot(spread, c_ref[:, columns(BCOLS)]).astype(
            BF16
        )
        lane = iota((LANES, LANES), 1)
        pick = one_hot(
            (iota((LANES, LANES), 0) == way * OWN_HEADS + lane) & (lane < OWN_HEADS)
        )
        dt_part = dot(dt_ref[...], pick).astype(BF16)
        stage_ref[way, :, CMAIN:] = dot(spread, dt_part).astype(BF16)
    pl.semaphore_wait(barrier, WAYS * OWNERS - 1)
    over_blocks(lambda s, t: copies(s, t).start())
    kept = pltpu.make_async_copy(
        stage_ref.at[head, slot_rows(owner), :], land_ref.at[head, slot_rows(owner), :], own
    )
    kept.start()
    kept.wait()
    start = lax.axis_index("ctx") * ROWS
    ends = []
    for at in range(lengths_ref.shape[1]):
        ends.append(lengths_ref[0, at] + (ends[-1] if ends else 0))

    def label_of(places):
        total = jnp.zeros(places.shape, jnp.int32)
        for end in ends:
            total = total + jnp.where(places >= end, 1, 0)
        return jnp.where(places >= 0, total, -1)

    label_ref[...] = label_of(iota(label_ref.shape, 0) + (start - 8))
    labr_ref[...] = label_of(iota(labr_ref.shape, 1) + start)
    labels = labr_ref[0:1, :]
    lasts = [labels[:, STRETCH - 1 : STRETCH], labels[:, ROWS - 1 : ROWS]]
    befores = [label_of(iota((1, LANES), 0) + (start - 1))[:, 0:1], lasts[0]]
    bias, rate = as_column(bias_ref[...]), as_column(rate_ref[...])
    part = ROWS // WAYS
    over_blocks(lambda s, t: copies(s, t).wait_recv())
    for s in range(WAYS):
        way = lax.rem(head + WAYS - s, WAYS)
        places = as_column(q_ref[way].astype(F32))
        pick = one_hot(iota((part, slots), 1).astype(F32) == places)
        out_ref[pl.ds(pl.multiple_of(way * part, part), part), :] = dot(
            pick, land_ref[way]
        ).astype(BF16)
    context = lax.axis_index("ctx")
    contexts = lax.axis_size("ctx")
    passed = pltpu.make_async_remote_copy(
        src_ref=out_ref.at[pl.ds(ROWS - 8, 8), :],
        dst_ref=halo_ref,
        send_sem=send_halo,
        recv_sem=recv_halo,
        device_id=(lax.axis_index("dp"), lax.rem(context + 1, contexts), head),
        device_id_type=pl.DeviceIdType.MESH,
    )

    @pl.when(context < contexts - 1)
    def _():
        passed.start()

    @pl.when(context == 0)
    def _():
        halo_ref[...] = jnp.zeros_like(halo_ref)

    logits = dot_nt(eye(LANES), out_ref[:, CMAIN:])[:OWN_HEADS] + bias
    step = jnp.maximum(logits, 0.0) + jnp.log1p(jnp.exp(-jnp.abs(logits)))
    step_ref[...] = step
    sig_ref[...] = jax.nn.sigmoid(logits)
    falls = -rate * step
    shape = (STRETCH, STRETCH)
    tri = jnp.where(iota(shape, 0) <= iota(shape, 1), 1.0, 0.0)
    lane = iota((OWN_HEADS, LANES), 1)
    gains = jnp.zeros((OWN_HEADS, LANES), F32)
    for k in range(2):
        span = slice(k * STRETCH, (k + 1) * STRETCH)
        cum = lax.dot_general(
            falls[:, span],
            tri,
            (((1,), (0,)), ((), ())),
            precision=lax.Precision.HIGHEST,
            preferred_element_type=F32,
        )
        end = cum[:, STRETCH - 1 :]
        own_last = jnp.where(labels[:, span] == lasts[k], 1.0, 0.0)
        own_first = jnp.where(labels[:, span] == befores[k], 1.0, 0.0)
        carried = jnp.where(lasts[k] == befores[k], 1.0, 0.0)
        values = (
            step[:, span],
            cum,
            jnp.exp(end - cum) * own_last,
            jnp.exp(cum) * own_first,
        )
        whole = jnp.exp(end) * carried
        gains = gains + jnp.where(lane == k, whole, 0.0)
        for i in range(PAIRS):
            for at, value in enumerate(values):
                rows_ref[i, 2 * at : 2 * at + 2, span] = value[2 * i : 2 * i + 2]
    gain_ref[...] = gains

    @pl.when(context > 0)
    def _():
        passed.wait_recv()

    @pl.when(context < contexts - 1)
    def _():
        passed.wait_send()

    over_blocks(lambda s, t: copies(s, t).wait_send())


def route_in(d_row, q_row, x_rows, b_rows, c_rows, dt_rows, bias, rate, lengths):
    slots = OWNERS * DEPTH * BLK
    return pl.pallas_call(
        route_in_kernel,
        in_specs=[pl.BlockSpec(memory_space=pltpu.VMEM)] * 8
        + [pl.BlockSpec(memory_space=pltpu.SMEM)],
        out_specs=[pl.BlockSpec(memory_space=pltpu.VMEM)] * 8,
        out_shape=[
            jax.ShapeDtypeStruct((ROWS, COLS), BF16),
            jax.ShapeDtypeStruct((8, COLS), BF16),
            jax.ShapeDtypeStruct((PAIRS, 8, ROWS), F32),
            jax.ShapeDtypeStruct((OWN_HEADS, ROWS), F32),
            jax.ShapeDtypeStruct((OWN_HEADS, ROWS), F32),
            jax.ShapeDtypeStruct((OWN_HEADS, LANES), F32),
            jax.ShapeDtypeStruct((ROWS + 16, LANES), jnp.int32),
            jax.ShapeDtypeStruct((8, ROWS), jnp.int32),
        ],
        scratch_shapes=[
            pltpu.VMEM((WAYS, slots, COLS), BF16),
            pltpu.VMEM((WAYS, slots, COLS), BF16),
            pltpu.SemaphoreType.DMA((WAYS, OWNERS)),
            pltpu.SemaphoreType.DMA((WAYS, OWNERS)),
            pltpu.SemaphoreType.DMA,
            pltpu.SemaphoreType.DMA,
            pltpu.SemaphoreType.DMA,
        ],
        compiler_params=pltpu.CompilerParams(collective_id=1, has_side_effects=True),
        name="route_in",
    )(d_row, q_row, x_rows, b_rows, c_rows, dt_rows, bias, rate, lengths)


def route_out_kernel(
    q_ref,
    d_ref,
    dx_ref,
    db_ref,
    dc_ref,
    ddt_ref,
    tail_ref,
    front_ref,
    sums_ref,
    x_ref,
    b_ref,
    c_ref,
    dt_ref,
    xt_ref,
    bct_ref,
    xb_ref,
    bcb_ref,
    heads_ref,
    total_ref,
    stage_ref,
    land_ref,
    held_ref,
    part_ref,
    send,
    recv,
    send1,
    recv1,
    send2,
    recv2,
    own,
    back_ref,
    send3,
    recv3,
):
    head = lax.axis_index("head")
    owner = lax.axis_index("dp") * lax.axis_size("ctx") + lax.axis_index("ctx")
    barrier = pltpu.get_barrier_semaphore()
    greet_all(barrier, owner, head)
    rows = ROWS // WAYS
    slots = OWNERS * DEPTH * BLK
    copies = functools.partial(block_copy, stage_ref, land_ref, send, recv, owner, head)

    def sum_copy(t):
        slot = lax.rem(owner + t, OWNERS)
        return pltpu.make_async_remote_copy(
            src_ref=sums_ref.at[slot],
            dst_ref=held_ref.at[owner],
            send_sem=send1.at[t],
            recv_sem=recv1.at[t],
            device_id=device_of(slot, head),
            device_id_type=pl.DeviceIdType.MESH,
        )

    def total_copy(t):
        return pltpu.make_async_remote_copy(
            src_ref=part_ref,
            dst_ref=total_ref.at[owner],
            send_sem=send2.at[t],
            recv_sem=recv2.at[t],
            device_id=device_of(lax.rem(owner + t, OWNERS), head),
            device_id_type=pl.DeviceIdType.MESH,
        )

    context = lax.axis_index("ctx")
    contexts = lax.axis_size("ctx")
    passed = pltpu.make_async_remote_copy(
        src_ref=front_ref,
        dst_ref=back_ref,
        send_sem=send3,
        recv_sem=recv3,
        device_id=(lax.axis_index("dp"), lax.rem(context + contexts - 1, contexts), head),
        device_id_type=pl.DeviceIdType.MESH,
    )
    for way in range(WAYS):
        here = slice(way * rows, (way + 1) * rows)
        spread = one_hot(iota((slots, rows), 0) == q_ref[way])
        if way == WAYS - 1:

            @pl.when(context < contexts - 1)
            def _():
                passed.wait_recv()

            @pl.when(context == contexts - 1)
            def _():
                back_ref[...] = jnp.zeros_like(back_ref)

        def one(ref, low, high):
            fixed = ref[here, :]
            if way == WAYS - 1:
                whole = fixed.astype(F32)
                tail = tail_ref[:, low:high] + back_ref[:, low:high]
                fixed = jnp.concatenate([whole[: rows - 8], tail]).astype(BF16)
            stage_ref[way, :, low:high] = dot(spread, fixed).astype(BF16)

        one(dx_ref, 0, XCOLS)
        one(db_ref, XCOLS, XCOLS + BCOLS)
        one(dc_ref, XCOLS + BCOLS, CMAIN)
        stage_ref[way, :, CMAIN:] = dot(spread, ddt_ref[here, :]).astype(BF16)
        if way == 0:
            pl.semaphore_wait(barrier, WAYS * OWNERS - 1)

            @pl.when(context > 0)
            def _():
                passed.start()

            over_slots(lambda t: sum_copy(t).start())
    over_blocks(lambda s, t: copies(s, t).start())
    kept = pltpu.make_async_copy(
        stage_ref.at[head, slot_rows(owner), :], land_ref.at[head, slot_rows(owner), :], own
    )
    kept.start()
    kept.wait()
    held_ref[owner] = sums_ref[owner]
    over_slots(lambda t: sum_copy(t).wait_recv())
    total = jnp.sum(held_ref[...], axis=0)
    part_ref[...] = total
    total_ref[owner] = total
    over_slots(lambda t: total_copy(t).start())
    rows = d_ref.shape[0]
    pick = one_hot(iota((rows, slots), 1) == d_ref[...])
    times = jnp.zeros((rows, HEADS), F32)
    over_blocks(lambda s, t: copies(s, t).wait_recv())
    for s in range(WAYS):
        way = lax.rem(head + WAYS - s, WAYS)

        def columns(size):
            return pl.ds(pl.multiple_of(way * size, size), size)

        x_ref[:, columns(XCOLS)] = dot(pick, land_ref[way, :, :XCOLS]).astype(BF16)
        b_ref[:, columns(BCOLS)] = dot(pick, land_ref[way, :, XCOLS : XCOLS + BCOLS]).astype(BF16)
        c_ref[:, columns(BCOLS)] = dot(pick, land_ref[way, :, XCOLS + BCOLS : CMAIN]).astype(BF16)
        lane = iota((LANES, LANES), 0)
        put = one_hot(
            (iota((LANES, LANES), 1) == way * OWN_HEADS + lane) & (lane < OWN_HEADS)
        )
        times += dot(dot(pick, land_ref[way, :, CMAIN:]).astype(BF16), put)
    dt_ref[...] = times.astype(BF16)
    over_slots(lambda t: total_copy(t).wait_recv())
    for i in range(PAIRS):
        lanes = slice(i * LANES, (i + 1) * LANES)
        xt_ref[:, lanes] = total_ref[i, 0:KERNEL, :]
        xb_ref[:, lanes] = total_ref[i, KERNEL : KERNEL + 1, :]
    for side in range(2):
        for g in range(BCOLS // LANES):
            lanes = slice(g * LANES, (g + 1) * LANES)
            at = (XCOLS + side * BCOLS) // LANES + g
            bct_ref[side, :, lanes] = total_ref[at, 0:KERNEL, :]
            bcb_ref[side : side + 1, lanes] = total_ref[at, KERNEL : KERNEL + 1, :]
    heads_ref[...] = total_ref[CMAIN // LANES, 0:3, 0:OWN_HEADS]
    over_slots(lambda t: sum_copy(t).wait_send())
    over_slots(lambda t: total_copy(t).wait_send())

    @pl.when(context > 0)
    def _():
        passed.wait_send()

    over_blocks(lambda s, t: copies(s, t).wait_send())


def route_out(q_row, d_col, dx, db, dc, ddt, tails, fronts, sums):
    slots = OWNERS * DEPTH * BLK
    rows = d_col.shape[0]
    space = pl.BlockSpec(memory_space=pltpu.VMEM)
    return pl.pallas_call(
        route_out_kernel,
        in_specs=[space] * 9,
        out_specs=[space] * 9,
        out_shape=[
            jax.ShapeDtypeStruct((rows, WAYS * XCOLS), BF16),
            jax.ShapeDtypeStruct((rows, WAYS * BCOLS), BF16),
            jax.ShapeDtypeStruct((rows, WAYS * BCOLS), BF16),
            jax.ShapeDtypeStruct((rows, HEADS), BF16),
            jax.ShapeDtypeStruct((KERNEL, XCOLS), F32),
            jax.ShapeDtypeStruct((2, KERNEL, BCOLS), F32),
            jax.ShapeDtypeStruct((1, XCOLS), F32),
            jax.ShapeDtypeStruct((2, BCOLS), F32),
            jax.ShapeDtypeStruct((3, OWN_HEADS), F32),
        ],
        scratch_shapes=[
            pltpu.VMEM((OWNERS, 8, LANES), F32),
            pltpu.VMEM((WAYS, slots, COLS), BF16),
            pltpu.VMEM((WAYS, slots, COLS), BF16),
            pltpu.VMEM((OWNERS, 8, LANES), F32),
            pltpu.VMEM((8, LANES), F32),
            pltpu.SemaphoreType.DMA((WAYS, OWNERS)),
            pltpu.SemaphoreType.DMA((WAYS, OWNERS)),
            pltpu.SemaphoreType.DMA((OWNERS,)),
            pltpu.SemaphoreType.DMA((OWNERS,)),
            pltpu.SemaphoreType.DMA((OWNERS,)),
            pltpu.SemaphoreType.DMA((OWNERS,)),
            pltpu.SemaphoreType.DMA,
            pltpu.VMEM((8, CMAIN), F32),
            pltpu.SemaphoreType.DMA,
            pltpu.SemaphoreType.DMA,
        ],
        compiler_params=pltpu.CompilerParams(collective_id=2, has_side_effects=True),
        name="route_out",
    )(q_row, d_col, dx, db, dc, ddt, tails, fronts, sums)


def fill_pad(pad_ref, rows_ref, halo_ref):
    pad_ref[0:8, :] = halo_ref[...].astype(F32)
    pad_ref[8 : 8 + ROWS, :] = rows_ref[...].astype(F32)


def fill_keep(keep_ref, label_ref):
    labels = label_ref[8 : 8 + ROWS, :]
    for k in range(KERNEL - 1):
        same = label_ref[5 + k : 5 + k + ROWS, :] == labels
        keep_ref[k] = jnp.where(same, 1.0, 0.0)


def fill_keeps(keeps_ref, label_ref):
    span = ROWS + 8
    front = label_ref[0:span, :]
    for k in range(KERNEL - 1):
        same = label_ref[3 - k : 3 - k + span, :] == front
        keeps_ref[k] = jnp.where(same & (front >= 0), 1.0, 0.0)


def conv_sum(pad_ref, taps, bias, keep_ref):
    total = bias + taps[0:1] * pad_ref[5 : 5 + ROWS, :] * keep_ref[0]
    total = total + taps[1:2] * pad_ref[6 : 6 + ROWS, :] * keep_ref[1]
    total = total + taps[2:3] * pad_ref[7 : 7 + ROWS, :] * keep_ref[2]
    return total + taps[3:4] * pad_ref[8 : 8 + ROWS, :]


def conv_value(pad_ref, rows_ref, halo_ref, taps, bias, keep_ref):
    fill_pad(pad_ref, rows_ref, halo_ref)
    total = conv_sum(pad_ref, taps, bias, keep_ref)
    return (total * jax.nn.sigmoid(total)).astype(BF16)


def conv_back(pad_ref, dpad_ref, rows_ref, halo_ref, taps, bias, keep_ref, keeps_ref, grad):
    fill_pad(pad_ref, rows_ref, halo_ref)
    total = conv_sum(pad_ref, taps, bias, keep_ref)
    sig = jax.nn.sigmoid(total)
    dpre = grad * (sig * (1.0 + total * (1.0 - sig)))
    dpad_ref[8 : 8 + ROWS, :] = dpre
    sums = []
    for k in range(KERNEL):
        value = dpre * pad_ref[5 + k : 5 + k + ROWS, :]
        if k < KERNEL - 1:
            value = value * keep_ref[k]
        sums.append(jnp.sum(value, axis=0, keepdims=True))
    sums.append(jnp.sum(dpre, axis=0, keepdims=True))
    sums.append(jnp.zeros((3, LANES), F32))
    span = ROWS + 8
    moved = taps[3:4] * dpad_ref[0:span, :]
    for k in range(KERNEL - 1):
        moved = moved + taps[k : k + 1] * (keeps_ref[k] * dpad_ref[3 - k : 3 - k + span, :])
    return moved, jnp.concatenate(sums)


def pair_rows(first, second, count=HEAD_DIM):
    width = first.shape[1]
    return jnp.concatenate(
        [jnp.broadcast_to(first, (count, width)), jnp.broadcast_to(second, (count, width))]
    )


def pair_scale(first, second, shape):
    return jnp.where(iota(shape, 0) < HEAD_DIM, first, second)


def first_kernel(
    gs_ref,
    rows_ref,
    x_ref,
    b_ref,
    c_ref,
    hx_ref,
    hb_ref,
    hc_ref,
    xt_ref,
    xb_ref,
    bt_ref,
    bb_ref,
    ct_ref,
    cb_ref,
    label_ref,
    og_ref,
    ep_ref,
    xT_ref,
    gT_ref,
    bn_ref,
    cn_ref,
    e0_ref,
    t1_ref,
    pad_ref,
    keep_ref,
):
    i = pl.program_id(0)

    @pl.when(i == 0)
    def _():
        fill_keep(keep_ref, label_ref)

    @pl.when(i % GROUP_PAIRS == 0)
    def _():
        bn_ref[...] = conv_value(pad_ref, b_ref, hb_ref, bt_ref[0], bb_ref[0:1], keep_ref)
        cn_ref[...] = conv_value(pad_ref, c_ref, hc_ref, ct_ref[0], cb_ref[1:2], keep_ref)

    unit = eye(LANES)
    xc = conv_value(pad_ref, x_ref, hx_ref, xt_ref[...], xb_ref[...], keep_ref)
    x_all = dot_nt(unit, xc)
    g_all = dot_nt(unit, og_ref[...])
    xT_ref[...] = x_all.astype(BF16)
    gT_ref[...] = g_all.astype(BF16)
    rows = rows_ref[0]
    states = []
    touched = []
    for k in range(2):
        span = slice(k * STRETCH, (k + 1) * STRETCH)
        coef = pair_rows(rows[0:1, span] * rows[4:5, span], rows[1:2, span] * rows[5:6, span])
        gain = pair_rows(rows[6:7, span], rows[7:8, span])
        states.append(dot((coef * x_all[:, span]).astype(BF16), bn_ref[span, :]))
        touched.append(dot((gain * g_all[:, span]).astype(BF16), cn_ref[span, :]))
    shape = (LANES, STATE)
    ga0, ga1 = gs_ref[2 * i, 0], gs_ref[2 * i, 1]
    gb0, gb1 = gs_ref[2 * i + 1, 0], gs_ref[2 * i + 1, 1]
    ep_ref[0, 0:LANES, :] = (pair_scale(ga1, gb1, shape) * states[0] + states[1]).astype(BF16)
    ep_ref[0, LANES : 2 * LANES, :] = (
        touched[0] + pair_scale(ga0, gb0, shape) * touched[1]
    ).astype(BF16)
    lane = iota((EXTRA, LANES), 1)
    whole = jnp.where(lane < HEAD_DIM, ga0 * ga1, gb0 * gb1)
    high = whole.astype(BF16).astype(F32)
    low = whole - high
    ep_ref[0, 2 * LANES :, :] = jnp.where(iota((EXTRA, LANES), 0) < 8, high, low).astype(BF16)
    e0_ref[...] = states[0]
    t1_ref[...] = touched[1]


def conv_specs():
    group = lambda i: i // GROUP_PAIRS
    base_b = XCOLS // LANES
    base_c = base_b + BCOLS // LANES
    return [
        pl.BlockSpec((ROWS, LANES), lambda i: (0, i)),
        pl.BlockSpec((ROWS, LANES), lambda i: (0, base_b + group(i))),
        pl.BlockSpec((ROWS, LANES), lambda i: (0, base_c + group(i))),
        pl.BlockSpec((8, LANES), lambda i: (0, i)),
        pl.BlockSpec((8, LANES), lambda i: (0, base_b + group(i))),
        pl.BlockSpec((8, LANES), lambda i: (0, base_c + group(i))),
        pl.BlockSpec((KERNEL, LANES), lambda i: (0, i)),
        pl.BlockSpec((1, LANES), lambda i: (0, i)),
        pl.BlockSpec((1, KERNEL, LANES), lambda i: (0, 0, group(i))),
        pl.BlockSpec((2, LANES), lambda i: (0, group(i))),
        pl.BlockSpec((1, KERNEL, LANES), lambda i: (1, 0, group(i))),
        pl.BlockSpec((2, LANES), lambda i: (0, group(i))),
        pl.BlockSpec((ROWS + 16, LANES), lambda i: (0, 0)),
    ]


def first_pass(gs, rows, conv_args, out_grad):
    wide = lambda i: (i, 0)
    group = lambda i: (0, i // GROUP_PAIRS)
    return pl.pallas_call(
        first_kernel,
        grid=(PAIRS,),
        in_specs=[
            pl.BlockSpec(memory_space=pltpu.SMEM),
            pl.BlockSpec((1, 8, ROWS), lambda i: (i, 0, 0)),
        ]
        + conv_specs()
        + [pl.BlockSpec((ROWS, LANES), lambda i: (0, i))],
        out_specs=[
            pl.BlockSpec((1, 2 * LANES + EXTRA, STATE), lambda i: (i, 0, 0)),
            pl.BlockSpec((LANES, ROWS), wide),
            pl.BlockSpec((LANES, ROWS), wide),
            pl.BlockSpec((ROWS, LANES), group),
            pl.BlockSpec((ROWS, LANES), group),
            pl.BlockSpec((LANES, STATE), wide),
            pl.BlockSpec((LANES, STATE), wide),
        ],
        out_shape=[
            jax.ShapeDtypeStruct((PAIRS, 2 * LANES + EXTRA, STATE), BF16),
            jax.ShapeDtypeStruct((XCOLS, ROWS), BF16),
            jax.ShapeDtypeStruct((XCOLS, ROWS), BF16),
            jax.ShapeDtypeStruct((ROWS, BCOLS), BF16),
            jax.ShapeDtypeStruct((ROWS, BCOLS), BF16),
            jax.ShapeDtypeStruct((XCOLS, STATE), F32),
            jax.ShapeDtypeStruct((XCOLS, STATE), F32),
        ],
        scratch_shapes=[
            pltpu.VMEM((ROWS + 16, LANES), F32),
            pltpu.VMEM((KERNEL - 1, ROWS, LANES), F32),
        ],
        name="first_pass",
    )(gs, rows, *conv_args, out_grad)


def gain_row(ref, at, pair):
    extra = ref[at, pair, 2 * LANES :, :].astype(F32)
    return extra[0:1] + extra[8:9]


def gain_scale(row):
    return pair_scale(row[:, 0:1], row[:, HEAD_DIM : HEAD_DIM + 1], (LANES, STATE))


ENTER = slice(0, LANES)
LEAVE = slice(LANES, 2 * LANES)


def state_kernel(
    chips, in_ref, out_ref, near_ref, join_ref, land_ref, part_ref, got_ref, give_ref, send, recv
):
    me = lax.axis_index("ctx")
    dp, head = lax.axis_index("dp"), lax.axis_index("head")
    chip, side = me // 2, lax.rem(me, 2)
    partner = me + 1 - 2 * side
    pairs = in_ref.shape[1]

    def place(context):
        return dict(
            device_id=(dp, context, head), device_id_type=pl.DeviceIdType.MESH
        )

    def chip_at(d):
        return lax.rem(chip + d, chips)

    barrier = pltpu.get_barrier_semaphore()
    pl.semaphore_signal(barrier, inc=1, **place(partner))
    for d in range(1, chips):
        pl.semaphore_signal(barrier, inc=1, **place(2 * chip_at(d) + side))
    pl.semaphore_wait(barrier, chips)

    def copy(source, target, stage, d, context):
        return pltpu.make_async_remote_copy(
            src_ref=source,
            dst_ref=target,
            send_sem=send.at[stage, d],
            recv_sem=recv.at[stage, d],
            **place(context),
        )

    def shared(y):
        return copy(in_ref.at[2 * y + 1 - side], near_ref.at[y], 0, y, partner)

    for y in range(chips):
        shared(y).start()
    for y in range(chips):
        shared(y).wait()

    def both(y, pair, rows):
        own = in_ref[2 * y + side, pair, rows, :].astype(F32)
        other = near_ref[y, pair, rows, :].astype(F32)
        return jnp.where(side == 0, own, other), jnp.where(side == 0, other, own)

    def gain_rows(y, pair):
        own, other = gain_row(in_ref, 2 * y + side, pair), gain_row(near_ref, y, pair)
        return jnp.where(side == 0, own, other), jnp.where(side == 0, other, own)

    def joined(d):
        y = chip_at(d)
        return copy(join_ref.at[y], land_ref.at[chip], 1, d, 2 * y + side)

    for d in list(range(1, chips)) + [0]:
        y = chip_at(d)
        target = join_ref if d else land_ref
        for pair in range(pairs):
            first, second = gain_rows(y, pair)
            e_first, e_second = both(y, pair, ENTER)
            p_first, p_second = both(y, pair, LEAVE)
            target[y, pair, ENTER, :] = (gain_scale(second) * e_first + e_second).astype(BF16)
            target[y, pair, LEAVE, :] = (p_first + gain_scale(first) * p_second).astype(BF16)
            whole = first * second
            high = whole.astype(BF16).astype(F32)
            upper = iota((EXTRA, LANES), 0) < 8
            target[y, pair, 2 * LANES :, :] = jnp.where(upper, high, whole - high).astype(BF16)
        if d:
            joined(d).start()
    for d in range(1, chips):
        joined(d).wait()

    for pair in range(pairs):
        gains = [gain_scale(gain_row(land_ref, at, pair)) for at in range(chips)]
        state = jnp.zeros((LANES, STATE), F32)
        for at in range(chips):
            part_ref[at, pair, ENTER, :] = state.astype(BF16)
            state = gains[at] * state + land_ref[at, pair, ENTER, :].astype(F32)
        state = jnp.zeros((LANES, STATE), F32)
        for at in reversed(range(chips)):
            part_ref[at, pair, LEAVE, :] = state.astype(BF16)
            state = land_ref[at, pair, LEAVE, :].astype(F32) + gains[at] * state

    def scanned(d):
        y = chip_at(d)
        return copy(part_ref.at[y], got_ref.at[chip], 2, d, 2 * y + side)

    for d in range(1, chips):
        scanned(d).start()
    got_ref[chip] = part_ref[chip]
    for d in range(1, chips):
        scanned(d).wait()

    def given(y):
        return copy(give_ref.at[y], out_ref.at[2 * y + side], 3, y, partner)

    for y in range(chips):
        for pair in range(pairs):
            first, second = gain_rows(y, pair)
            e_first, _ = both(y, pair, ENTER)
            _, p_second = both(y, pair, LEAVE)
            enter = got_ref[y, pair, ENTER, :].astype(F32)
            leave = got_ref[y, pair, LEAVE, :].astype(F32)
            enter_second = gain_scale(first) * enter + e_first
            leave_first = p_second + gain_scale(second) * leave
            for rows, one, two in ((ENTER, enter, enter_second), (LEAVE, leave_first, leave)):
                out_ref[2 * y + side, pair, rows, :] = jnp.where(side == 0, one, two).astype(BF16)
                give_ref[y, pair, rows, :] = jnp.where(side == 0, two, one).astype(BF16)
        given(y).start()
    for y in range(chips):
        given(y).wait()


def exchange_states(parts):
    count, pairs, tall = parts.shape[:3]
    chips = count // 2
    wide = pltpu.VMEM((chips, pairs, tall, STATE), BF16)
    slim = pltpu.VMEM((chips, pairs, 2 * LANES, STATE), BF16)
    return pl.pallas_call(
        functools.partial(state_kernel, chips),
        in_specs=[pl.BlockSpec(memory_space=pltpu.VMEM)],
        out_specs=pl.BlockSpec(memory_space=pltpu.VMEM),
        out_shape=jax.ShapeDtypeStruct((count, pairs, 2 * LANES, STATE), BF16),
        scratch_shapes=[
            wide,
            wide,
            wide,
            slim,
            slim,
            slim,
            pltpu.SemaphoreType.DMA((4, chips)),
            pltpu.SemaphoreType.DMA((4, chips)),
        ],
        compiler_params=pltpu.CompilerParams(collective_id=0, has_side_effects=True),
        name="exchange_states",
    )(parts)


def main_kernel(
    gs_ref,
    skip_ref,
    rows_ref,
    x_ref,
    b_ref,
    c_ref,
    hx_ref,
    hb_ref,
    hc_ref,
    xt_ref,
    xb_ref,
    bt_ref,
    bb_ref,
    ct_ref,
    cb_ref,
    label_ref,
    og_ref,
    xT_ref,
    gT_ref,
    bn_ref,
    cn_ref,
    ent_ref,
    e0_ref,
    t1_ref,
    labr_ref,
    step_ref,
    sig_ref,
    rate_ref,
    y_ref,
    dx_ref,
    db_ref,
    dc_ref,
    ddt_ref,
    tail_ref,
    front_ref,
    sums_ref,
    dcum_ref,
    dstep_ref,
    dskip_ref,
    mask_ref,
    score_ref,
    dscore_ref,
    bT_ref,
    cT_ref,
    dbT_ref,
    dcT_ref,
    pad_ref,
    dpad_ref,
    dxn_ref,
    keep_ref,
    keeps_ref,
):
    i = pl.program_id(0)
    unit = eye(LANES)
    wide_unit = eye(STRETCH)
    spans = [slice(k * STRETCH, (k + 1) * STRETCH) for k in range(2)]

    @pl.when(i == 0)
    def _():
        fill_keep(keep_ref, label_ref)
        fill_keeps(keeps_ref, label_ref)
        dpad_ref[...] = jnp.zeros_like(dpad_ref)
        sums_ref[...] = jnp.zeros_like(sums_ref)
        dcum_ref[...] = jnp.zeros_like(dcum_ref)
        dstep_ref[...] = jnp.zeros_like(dstep_ref)
        dskip_ref[...] = jnp.zeros_like(dskip_ref)
        for k in range(2):
            for t in range(2):
                shape = (STRETCH, LANES)
                left = k * STRETCH + t * LANES
                low = 8 + k * STRETCH
                same = label_ref[low : low + STRETCH, :] == labr_ref[0:1, left : left + LANES]
                lower = iota(shape, 0) >= iota(shape, 1) + t * LANES
                mask_ref[k, :, t * LANES : (t + 1) * LANES] = jnp.where(same & lower, 0.0, NEG)

    @pl.when(i % GROUP_PAIRS == 0)
    def _():
        bT_ref[...] = dot_nt(unit, bn_ref[...]).astype(BF16)
        cT_ref[...] = dot_nt(unit, cn_ref[...]).astype(BF16)
        dbT_ref[...] = jnp.zeros_like(dbT_ref)
        dcT_ref[...] = jnp.zeros_like(dcT_ref)
        dscore_ref[...] = jnp.zeros_like(dscore_ref)
        for k in range(2):
            score_ref[k] = dot_nt(cn_ref[spans[k], :], bn_ref[spans[k], :])

    rows = rows_ref[0]
    columns = jnp.transpose(rows)
    shape = (LANES, STATE)
    gains = [
        (gs_ref[2 * i, k], gs_ref[2 * i + 1, k]) for k in range(2)
    ]
    skip = pair_scale(skip_ref[2 * i], skip_ref[2 * i + 1], (LANES, STRETCH))
    enter0 = ent_ref[0, 0:LANES, :].astype(F32)
    leave1 = ent_ref[0, LANES : 2 * LANES, :].astype(F32)
    enter1 = pair_scale(*gains[0], shape) * enter0 + e0_ref[...]
    leave0 = t1_ref[...] + pair_scale(*gains[1], shape) * leave1
    enters = (enter0, enter1)
    leaves = (leave0, leave1)
    seat = iota((OWN_HEADS, STRETCH), 0)
    for k in range(2):
        span = spans[k]
        x = xT_ref[:, span].astype(F32)
        g_low = gT_ref[:, span]
        g = g_low.astype(F32)
        og = og_ref[span, :]
        step = pair_rows(rows[0:1, span], rows[1:2, span])
        ends = (rows[4:5, span], rows[5:6, span])
        coefs = (rows[0:1, span] * ends[0], rows[1:2, span] * ends[1])
        coef = pair_rows(*coefs)
        gain = pair_rows(rows[6:7, span], rows[7:8, span])
        xs = (step * x).astype(BF16)
        weighted = (coef * x).astype(BF16)
        nothing = jnp.zeros((HEAD_DIM, STRETCH), BF16)
        inner = []
        dxs = []
        for h in range(2):
            part = slice(h * HEAD_DIM, (h + 1) * HEAD_DIM)
            gap = columns[span, 2 + h : 3 + h] - rows[2 + h : 3 + h, span]
            decay = jnp.exp(gap + mask_ref[k])
            mix = (score_ref[k] * decay).astype(BF16)
            own = (xs[part], nothing) if h == 0 else (nothing, xs[part])
            dmix = dot(og, jnp.concatenate(own))
            dscore_ref[k] += dmix * decay
            inner.append(dot_nt(xs[part], mix))
            dxs.append(dot(g_low[part], mix))
        inner = jnp.concatenate(inner)
        dxs = jnp.concatenate(dxs)
        enter = enters[k].astype(BF16)
        leave = leaves[k].astype(BF16)
        carried = gain * dot_nt(enter, cn_ref[span, :])
        y = inner + carried + skip * x
        y_ref[span, :] = dot_nt(wide_unit, y.astype(BF16)).astype(BF16)
        enter_t = dot_nt(unit, enter).astype(BF16)
        leave_t = dot_nt(unit, leave).astype(BF16)
        dcT_ref[:, span] += dot(enter_t, (gain * g).astype(BF16))
        dbT_ref[:, span] += dot(leave_t, weighted)
        dweighted = dot_nt(leave, bn_ref[span, :])
        dx = step * dxs + coef * dweighted + skip * g
        dxn_ref[span, :] = dot_nt(wide_unit, dx.astype(BF16))
        moved = dweighted * x
        direct = dxs * x
        cums = g * (inner + carried) - xs.astype(F32) * dxs
        skipped = g * x
        turned = leaves[k] * enters[k]
        last = iota((1, STRETCH), 1) == STRETCH - 1
        for h in range(2):
            part = slice(h * HEAD_DIM, (h + 1) * HEAD_DIM)
            pulled = jnp.sum(moved[part], axis=0, keepdims=True)
            ended = coefs[h] * pulled
            total = jnp.sum(ended, axis=1, keepdims=True)
            bend = jnp.sum(
                jnp.sum(turned[part], axis=0, keepdims=True), axis=1, keepdims=True
            )
            dcum = jnp.sum(cums[part], axis=0, keepdims=True) - ended
            dcum = dcum + jnp.where(last, total + gains[k][h] * bend, 0.0)
            dstep = jnp.sum(direct[part], axis=0, keepdims=True) + ends[h] * pulled
            dskip = jnp.sum(skipped[part], axis=0, keepdims=True)
            here = seat == 2 * i + h
            dcum_ref[:, span] += jnp.where(here, dcum, 0.0)
            dstep_ref[:, span] += jnp.where(here, dstep, 0.0)
            dskip_ref[:, span] += jnp.where(here, dskip, 0.0)

    moved, sums = conv_back(
        pad_ref, dpad_ref, x_ref, hx_ref, xt_ref[...], xb_ref[...], keep_ref, keeps_ref, dxn_ref[...]
    )
    lanes = pl.ds(pl.multiple_of(i * LANES, LANES), LANES)
    front_ref[:, lanes] = moved[0:8]
    tail_ref[:, lanes] = moved[ROWS:]
    dx_ref[...] = moved[8:].astype(BF16)
    sums_ref[i] = sums

    @pl.when(i % GROUP_PAIRS == GROUP_PAIRS - 1)
    def _():
        for k in range(2):
            span = spans[k]
            dscore = dscore_ref[k].astype(BF16)
            dcT = dcT_ref[:, span] + dot_nt(bT_ref[:, span], dscore)
            dbT = dbT_ref[:, span] + dot(cT_ref[:, span], dscore)
            dcT_ref[:, span] = dcT
            dbT_ref[:, span] = dbT
        sides = (
            (dbT_ref, b_ref, hb_ref, bt_ref, bb_ref[0:1], db_ref, XCOLS),
            (dcT_ref, c_ref, hc_ref, ct_ref, cb_ref[1:2], dc_ref, XCOLS + BCOLS),
        )
        for grad_ref, in_ref, halo_ref, tap_ref, bias, out_ref, left in sides:
            for span in spans:
                dxn_ref[span, :] = dot_nt(wide_unit, grad_ref[:, span].astype(BF16))
            moved, sums = conv_back(
                pad_ref,
                dpad_ref,
                in_ref,
                halo_ref,
                tap_ref[0],
                bias,
                keep_ref,
                keeps_ref,
                dxn_ref[...],
            )
            at = pl.multiple_of(left + (i // GROUP_PAIRS) * LANES, LANES)
            front_ref[:, pl.ds(at, LANES)] = moved[0:8]
            tail_ref[:, pl.ds(at, LANES)] = moved[ROWS:]
            out_ref[...] = moved[8:].astype(BF16)
            sums_ref[left // LANES + i // GROUP_PAIRS] = sums

    @pl.when(i == PAIRS - 1)
    def _():
        shape = (STRETCH, STRETCH)
        tri = jnp.where(iota(shape, 0) >= iota(shape, 1), 1.0, 0.0)
        rate = as_column(rate_ref[...])
        bias_sum = jnp.zeros((OWN_HEADS, 1), F32)
        rate_sum = jnp.zeros((OWN_HEADS, 1), F32)
        for span in spans:
            after = lax.dot_general(
                dcum_ref[:, span],
                tri,
                (((1,), (0,)), ((), ())),
                precision=lax.Precision.HIGHEST,
                preferred_element_type=F32,
            )
            dlogit = (dstep_ref[:, span] - rate * after) * sig_ref[:, span]
            bias_sum += jnp.sum(dlogit, axis=1, keepdims=True)
            rate_sum -= jnp.sum(after * step_ref[:, span], axis=1, keepdims=True)
            tall = jnp.concatenate([dlogit, jnp.zeros((LANES - OWN_HEADS, STRETCH), F32)])
            ddt_ref[span, :] = dot_nt(wide_unit, tall.astype(BF16)).astype(BF16)
        skip_sum = jnp.sum(dskip_ref[...], axis=1, keepdims=True)
        diagonal = iota((OWN_HEADS, LANES), 0) == iota((OWN_HEADS, LANES), 1)
        lines = [
            jnp.sum(jnp.where(diagonal, value, 0.0), axis=0, keepdims=True)
            for value in (bias_sum, rate_sum, skip_sum)
        ]
        sums_ref[CMAIN // LANES] = jnp.concatenate(lines + [jnp.zeros((5, LANES), F32)])


def main_pass(
    gs, skip, rows, conv_args, out_grad, xT, gT, bn, cn, ent, e0, t1, labr, heads
):
    wide = lambda i: (i, 0)
    col = lambda i: (0, i)
    group = lambda i: (0, i // GROUP_PAIRS)
    triple = lambda i: (i, 0, 0)
    fixed = lambda i: (0, 0)
    square = (2, STRETCH, STRETCH)
    return pl.pallas_call(
        main_kernel,
        grid=(PAIRS,),
        in_specs=[
            pl.BlockSpec(memory_space=pltpu.SMEM),
            pl.BlockSpec(memory_space=pltpu.SMEM),
            pl.BlockSpec((1, 8, ROWS), triple),
        ]
        + conv_specs()
        + [
            pl.BlockSpec((ROWS, LANES), col),
            pl.BlockSpec((LANES, ROWS), wide),
            pl.BlockSpec((LANES, ROWS), wide),
            pl.BlockSpec((ROWS, LANES), group),
            pl.BlockSpec((ROWS, LANES), group),
            pl.BlockSpec((1, 2 * LANES, STATE), triple),
            pl.BlockSpec((LANES, STATE), wide),
            pl.BlockSpec((LANES, STATE), wide),
            pl.BlockSpec((8, ROWS), fixed),
            pl.BlockSpec((OWN_HEADS, ROWS), fixed),
            pl.BlockSpec((OWN_HEADS, ROWS), fixed),
            pl.BlockSpec((1, OWN_HEADS), fixed),
        ],
        out_specs=[
            pl.BlockSpec((ROWS, LANES), col),
            pl.BlockSpec((ROWS, LANES), col),
            pl.BlockSpec((ROWS, LANES), group),
            pl.BlockSpec((ROWS, LANES), group),
            pl.BlockSpec((ROWS, LANES), fixed),
            pl.BlockSpec((8, CMAIN), fixed),
            pl.BlockSpec((8, CMAIN), fixed),
            pl.BlockSpec((OWNERS, 8, LANES), lambda i: (0, 0, 0)),
        ],
        out_shape=[
            jax.ShapeDtypeStruct((ROWS, XCOLS), BF16),
            jax.ShapeDtypeStruct((ROWS, XCOLS), BF16),
            jax.ShapeDtypeStruct((ROWS, BCOLS), BF16),
            jax.ShapeDtypeStruct((ROWS, BCOLS), BF16),
            jax.ShapeDtypeStruct((ROWS, LANES), BF16),
            jax.ShapeDtypeStruct((8, CMAIN), F32),
            jax.ShapeDtypeStruct((8, CMAIN), F32),
            jax.ShapeDtypeStruct((OWNERS, 8, LANES), F32),
        ],
        scratch_shapes=[
            pltpu.VMEM((OWN_HEADS, ROWS), F32),
            pltpu.VMEM((OWN_HEADS, ROWS), F32),
            pltpu.VMEM((OWN_HEADS, ROWS), F32),
            pltpu.VMEM(square, F32),
            pltpu.VMEM(square, F32),
            pltpu.VMEM(square, F32),
            pltpu.VMEM((LANES, ROWS), BF16),
            pltpu.VMEM((LANES, ROWS), BF16),
            pltpu.VMEM((LANES, ROWS), F32),
            pltpu.VMEM((LANES, ROWS), F32),
            pltpu.VMEM((ROWS + 16, LANES), F32),
            pltpu.VMEM((ROWS + 16, LANES), F32),
            pltpu.VMEM((ROWS, LANES), F32),
            pltpu.VMEM((KERNEL - 1, ROWS, LANES), F32),
            pltpu.VMEM((KERNEL - 1, ROWS + 8, LANES), F32),
        ],
        name="main_pass",
    )(gs, skip, rows, *conv_args, out_grad, xT, gT, bn, cn, ent, e0, t1, labr, *heads)


def on_device(
    x_rows,
    b_rows,
    c_rows,
    dt_rows,
    length_plan,
    trace_lengths,
    x_taps,
    bc_taps,
    x_bias,
    bc_bias,
    dt_bias,
    decay_rate,
    skip_gain,
    out_grad,
):
    contexts = lax.axis_size("ctx")
    owner = lax.axis_index("dp") * contexts + lax.axis_index("ctx")
    head_at = lax.axis_index("head")
    owned = LBLOCKS * WAYS
    plan = length_plan.reshape(OWNERS, WAYS, LBLOCKS)
    column = lax.dynamic_index_in_dim(plan, head_at, 1, keepdims=False)
    base = (owner * WAYS + head_at) * LBLOCKS
    blocks = jnp.arange(LBLOCKS, dtype=jnp.int32)
    hits = column.reshape(-1)[:, None] == base + blocks[None, :]
    seats = (jnp.arange(OWNERS * LBLOCKS, dtype=jnp.int32) // LBLOCKS)[:, None]
    target = jnp.sum(jnp.where(hits, seats, 0), axis=0)
    earlier = blocks[None, :] < blocks[:, None]
    rank = jnp.sum(((target[None, :] == target[:, None]) & earlier).astype(jnp.int32), axis=1)
    pairs = jnp.arange(BLK, dtype=jnp.int32)
    goes = (((target * DEPTH + rank) * BLK)[:, None] + pairs[None, :]).reshape(-1)
    mine = lax.dynamic_slice_in_dim(length_plan, owner * owned, owned).reshape(WAYS, LBLOCKS)
    source = mine // owned
    same = source[:, :, None] == source[:, None, :]
    lower = mine[:, None, :] < mine[:, :, None]
    place = jnp.sum((same & lower).astype(jnp.int32), axis=2)
    comes = ((source * DEPTH + place) * BLK)[:, :, None] + pairs
    comes = comes.reshape(WAYS, LBLOCKS * BLK)

    heads_dev = dt_bias.shape[0]
    packed, halo, rows, step, sig, gs, label, labr = route_in(
        goes[None, :],
        comes[:, None, :],
        x_rows,
        b_rows,
        c_rows,
        dt_rows,
        dt_bias[None, :],
        decay_rate[None, :],
        trace_lengths,
    )

    conv_args = (
        packed,
        packed,
        packed,
        halo,
        halo,
        halo,
        x_taps,
        x_bias[None, :],
        bc_taps,
        bc_bias,
        bc_taps,
        bc_bias,
        label,
    )
    ep, xT, gT, bn, cn, e0, t1 = first_pass(gs, rows, conv_args, out_grad)

    per = PAIRS // contexts
    tall = 2 * LANES + EXTRA
    ent = exchange_states(ep.reshape(contexts, per, tall, STATE))
    ent = ent.reshape(PAIRS, 2 * LANES, STATE)

    heads = (step, sig, decay_rate[None, :])
    y, dx, db, dc, ddt, tails, fronts, sums = main_pass(
        gs,
        skip_gain,
        rows,
        conv_args,
        out_grad,
        xT,
        gT,
        bn,
        cn,
        ent,
        e0,
        t1,
        labr,
        heads,
    )
    x_grad, b_grad, c_grad, dt_grad, xt_grad, bct_grad, xb_grad, bcb_grad, heads_grad = route_out(
        comes[:, None, :], goes[:, None], dx, db, dc, ddt, tails, fronts, sums
    )
    return (
        y,
        x_grad,
        b_grad,
        c_grad,
        dt_grad,
        xt_grad,
        bct_grad,
        xb_grad.reshape(-1),
        bcb_grad,
        heads_grad[0],
        heads_grad[1],
        heads_grad[2],
    )


def solution(mesh):
    rows = P(("dp", "ctx", "head"), None)
    return jax.shard_map(
        on_device,
        mesh=mesh,
        in_specs=(
            rows,
            rows,
            rows,
            rows,
            P(),
            P("dp", None),
            P(None, "head"),
            P(None, None, "head"),
            P("head"),
            P(None, "head"),
            P("head"),
            P("head"),
            P("head"),
            P(("dp", "ctx"), "head"),
        ),
        out_specs=(
            P(("dp", "ctx"), "head"),
            rows,
            rows,
            rows,
            rows,
            P(None, "head"),
            P(None, None, "head"),
            P("head"),
            P(None, "head"),
            P("head"),
            P("head"),
            P("head"),
        ),
        check_vma=False,
    )
```
